32 devices in a mesh: dp: 8 (over y, x, core), expert: 4 (over z).
Axes of the slice: x: 2, y: 2, z: 4, core: 2. Of those that a mesh axis runs over, the one named last changes fastest.
Arguments:
- tokens: bfloat16 [4, 32, 256, 768], P(None, ('dp', 'expert')), may hold values from -6 to 6
- cotangent: bfloat16 [4, 32, 256, 768], P(None, ('dp', 'expert')), may hold values from -6 to 6
- segments: int32 [4, 32, 256], P(None, ('dp', 'expert')), may hold values from 0 to 2, never falling along the last dimension, each value on 1 to 128 neighbouring positions
- routes: int32 [4, 32, 256, 2], P(None, ('dp', 'expert')), may hold values from 0 to 15, as said below
- slots: int32 [4, 32, 256, 2], P(None, ('dp', 'expert')), may hold values from 0 to 39, as said below
- norm1_gain: bfloat16 [768], P('dp'), may hold values from 0.5 to 1.5
- w_query: bfloat16 [768, 768], P('dp'), may hold values from -0.21875 to 0.21875
- w_key: bfloat16 [768, 768], P('dp'), may hold values from -0.21875 to 0.21875
- w_value: bfloat16 [768, 768], P('dp'), may hold values from -0.21875 to 0.21875
- w_out: bfloat16 [768, 768], P('dp'), may hold values from -0.625 to 0.625
- norm2_gain: bfloat16 [768], P('dp'), may hold values from 0.5 to 1.5
- w_router: bfloat16 [768, 16], P('dp'), may hold values from -0.15625 to 0.15625
- shared_gate: bfloat16 [768, 2048], P('dp'), may hold values from -0.21875 to 0.21875
- shared_up: bfloat16 [768, 2048], P('dp'), may hold values from -0.21875 to 0.21875
- shared_down: bfloat16 [2048, 768], P('dp'), may hold values from -0.25 to 0.25
- expert_gate: bfloat16 [16, 768, 2048], P('expert', 'dp'), may hold values from -0.21875 to 0.21875
- expert_up: bfloat16 [16, 768, 2048], P('expert', 'dp'), may hold values from -0.21875 to 0.21875
- expert_down: bfloat16 [16, 2048, 768], P('expert', 'dp'), may hold values from -2 to 2
Outputs:
- layer_out: bfloat16 [4, 32, 256, 768], P(None, ('dp', 'expert'))
- grad_tokens: float32 [4, 32, 256, 768], P(None, ('dp', 'expert'))
- grad_norm1_gain: float32 [768], P('dp')
- grad_w_query: float32 [768, 768], P('dp')
- grad_w_key: float32 [768, 768], P('dp')
- grad_w_value: float32 [768, 768], P('dp')
- grad_w_out: float32 [768, 768], P('dp')
- grad_norm2_gain: float32 [768], P('dp')
- grad_w_router: float32 [768, 16], P('dp')
- grad_shared_gate: float32 [768, 2048], P('dp')
- grad_shared_up: float32 [768, 2048], P('dp')
- grad_shared_down: float32 [2048, 768], P('dp')
- grad_expert_gate: float32 [16, 768, 2048], P('expert', 'dp')
- grad_expert_up: float32 [16, 768, 2048], P('expert', 'dp')
- grad_expert_down: float32 [16, 2048, 768], P('expert', 'dp')
The draws below stay inside these ranges and needn't reach their ends.
Inputs may be any that keep to these rules, and one draw needn't show every extreme that they name: `routes`: each token names 2 different experts. Within one sequence of one micro-batch every expert is named by at most 40 of the token choices, and some expert by exactly 40; every expert is named somewhere. Within one sequence of one micro-batch the choices that name one expert hold different slots, numbered 0 upward without gaps.
All inputs are finite; a program needn't handle non-finite values.
Results may differ from the reference program's by a relative error of at most 0.023.
Values may be sent and summed in bfloat16 or wider, within the bound.
No kernel may reach another device: no remote copies, remote signals or barrier semaphores. Data moves between devices by JAX's collectives and lax.ppermute only.
A program may use at most 384 MiB of HBM per device.

```python
import math
import jax
import jax.numpy as jnp
import numpy as np
from jax import lax

D = 768
HEADS = 12
HEAD_DIM = 64
FF = 2048
EFF = 2048
EXPERTS = 16
TOP = 2
MICRO = 4
SEQ = 256
SEQS = 32
CAP = 40


def route_table(key):
    block_count = MICRO * SEQS
    block_unit = SEQ // 32
    pattern = jnp.array([5, 5, 5, 5, 4, 4, 4, 4, 4, 4, 4, 4, 3, 3, 3, 3], jnp.int32) * block_unit

    def single_block(block_index):
        block_key = jax.random.fold_in(key, block_index)
        key_shift, key_label, key_order = jax.random.split(block_key, 3)
        moved = jax.random.randint(key_shift, (4,), 0, block_unit).astype(jnp.int32)
        delta = jnp.zeros((16,), jnp.int32).at[jnp.array([4, 6, 8, 10])].add(moved)
        delta = delta.at[jnp.array([5, 7, 9, 11])].add(-moved)
        counts = pattern + delta
        labels = jax.random.permutation(key_label, 16).astype(jnp.int32)
        bounds = jnp.cumsum(counts)
        starts = bounds - counts
        places = jnp.arange(2 * SEQ, dtype=jnp.int32)
        ranking = jnp.sum((places[:, None] >= bounds[None, :]).astype(jnp.int32), axis=1)
        slot_flat = places - starts[ranking]
        expert_flat = labels[ranking]
        ordering = jax.random.permutation(key_order, SEQ).astype(jnp.int32)
        expert_pairs = expert_flat.reshape(2, SEQ).T
        slot_pairs = slot_flat.reshape(2, SEQ).T
        route_out = jnp.zeros((SEQ, 2), jnp.int32).at[ordering].set(expert_pairs)
        slot_out = jnp.zeros((SEQ, 2), jnp.int32).at[ordering].set(slot_pairs)
        return (route_out, slot_out)
    route_all, slot_all = jax.vmap(single_block)(jnp.arange(block_count, dtype=jnp.int32))
    return (route_all.reshape(MICRO, SEQS, SEQ, 2), slot_all.reshape(MICRO, SEQS, SEQ, 2))


def draw_routes(key, part):
    return route_table(jax.random.fold_in(key, 11))[0]


def draw_slots(key, part):
    return route_table(jax.random.fold_in(key, 11))[1]


def shard_levels(rng, extent, cuts, least, top_value):
    factor_of, own = 1.0, jax.random.fold_in(rng, 6)
    for axis_at, blocks in cuts:
        steps = jnp.exp(jax.random.uniform(jax.random.fold_in(own, axis_at), (blocks,), jnp.float32, least / len(cuts), top_value / len(cuts)))
        factor_of = factor_of * jnp.repeat(steps, extent[axis_at] // blocks).reshape([-1 if axis == axis_at else 1 for axis in range(len(extent))])
    return factor_of


def profile(number_of, total, bound, skew):
    portions = [(1 << 20) // math.isqrt(rank ** skew) + 1 for rank in range(2, number_of + 1)]
    rest, holding = total - bound - (number_of - 1), [1] * (number_of - 1)
    while rest > 0:
        candidates = [i for i in range(number_of - 1) if holding[i] < bound]
        whole, remaining = sum([portions[i] for i in candidates]), rest
        for i in candidates:
            extra = min(bound - holding[i], max(1, remaining * portions[i] // whole), rest)
            holding[i] = holding[i] + extra
            rest = rest - extra
    return np.array([bound] + holding)


def ragged_sizes(key, count, total, most, lean):
    if count == 2:
        one = jax.random.randint(key, (), max(1, total - most), min(most, total - 1) + 1)
        return jnp.stack([one, total - one])
    sizes = jnp.asarray(profile(count, total, most, lean), jnp.int32)
    couples = (count - 1) // 2
    giver, receiver = sizes[1:1 + 2 * couples:2], sizes[2:2 + 2 * couples:2]
    room = jnp.minimum(giver - 1, most - receiver)
    passed = jax.random.randint(jax.random.fold_in(key, 1), (couples,), 0, 1 << 20) % (room + 1)
    sizes = sizes.at[1:1 + 2 * couples:2].set(giver - passed).at[2:2 + 2 * couples:2].set(receiver + passed)
    return sizes[jax.random.permutation(jax.random.fold_in(key, 2), count)]


def scatter_about(stream_key, extent, scale, limit, cuts=(), held_as=jnp.bfloat16):
    factor_of = shard_levels(stream_key, extent, cuts, -0.22, 0.18) if cuts else 1.0
    entries = jax.random.normal(stream_key, extent, jnp.float32) * scale * factor_of
    return jnp.minimum(jnp.maximum(entries, -limit), limit).astype(held_as)


def setup_inputs(seed: int = 0) -> dict:
    key_list = jax.random.split(jax.random.key(seed), 19)
    tokens = scatter_about(key_list[0], (MICRO, SEQS, SEQ, D), 1.0, 6.0, ((1, 32),))
    cotangent = scatter_about(key_list[1], (MICRO, SEQS, SEQ, D), 1.0, 6.0, ((1, 32),))
    segments = jax.vmap(lambda own: jnp.searchsorted(jnp.cumsum(ragged_sizes(own, max(3, SEQ // 128), SEQ, SEQ // 2, 2)), jnp.arange(SEQ), side="right"))(jax.random.split(key_list[2], MICRO * SEQS)).reshape((MICRO, SEQS, SEQ)).astype(jnp.int32)
    routes = draw_routes(jax.random.fold_in(key_list[18], 71), 0)
    slots = draw_slots(jax.random.fold_in(key_list[18], 71), 0)
    norm1_gain = jnp.clip(1.0 + 0.1 * jax.random.normal(key_list[5], (D,), jnp.float32), 0.5, 1.5).astype(jnp.bfloat16)
    w_query = scatter_about(key_list[6], (D, D), D ** -0.5, 0.21875, ((0, 8),))
    w_key = scatter_about(key_list[7], (D, D), D ** -0.5, 0.21875, ((0, 8),))
    w_value = scatter_about(key_list[8], (D, D), D ** -0.5, 0.21875, ((0, 8),))
    w_out = scatter_about(key_list[9], (D, D), (D // 8) ** -0.5, 0.625, ((0, 8),))
    norm2_gain = jnp.clip(1.0 + 0.1 * jax.random.normal(key_list[10], (D,), jnp.float32), 0.5, 1.5).astype(jnp.bfloat16)
    w_router = scatter_about(key_list[11], (D, EXPERTS), (2 * D) ** -0.5, 0.15625, ((0, 8),))
    shared_gate = scatter_about(key_list[12], (D, FF), D ** -0.5, 0.21875, ((0, 8),))
    shared_up = scatter_about(key_list[13], (D, FF), D ** -0.5, 0.21875, ((0, 8),))
    shared_down = scatter_about(key_list[14], (FF, D), (FF // 4) ** -0.5, 0.25, ((0, 8),))
    expert_gate = scatter_about(key_list[15], (EXPERTS, D, EFF), D ** -0.5, 0.21875, ((0, 4), (1, 8)))
    expert_up = scatter_about(key_list[16], (EXPERTS, D, EFF), D ** -0.5, 0.21875, ((0, 4), (1, 8)))
    expert_down = scatter_about(key_list[17], (EXPERTS, EFF, D), (max(EFF // 256, 1)) ** -0.5, 2.0, ((0, 4), (1, 8)))
    return dict(tokens=tokens, cotangent=cotangent, segments=segments, routes=routes, slots=slots, norm1_gain=norm1_gain, w_query=w_query, w_key=w_key, w_value=w_value, w_out=w_out, norm2_gain=norm2_gain, w_router=w_router, shared_gate=shared_gate, shared_up=shared_up, shared_down=shared_down, expert_gate=expert_gate, expert_up=expert_up, expert_down=expert_down)


@jax.custom_vjp
def low(v):
    return lax.optimization_barrier(v.astype(jnp.bfloat16)).astype(jnp.float32)

@jax.custom_vjp
def low_back(v):
    return v

def low_keep(v):
    return (low(v), None)

def low_pass(kept, grad):
    return (grad,)

def back_keep(v):
    return (v, None)

def back_low(kept, grad):
    return (low(grad),)
low.defvjp(low_keep, low_pass)
low_back.defvjp(back_keep, back_low)
epsilon = 1e-06
highest = lax.Precision.HIGHEST

def product(left, right):
    return jnp.dot(left, right, precision=highest, preferred_element_type=jnp.float32)

def rotate(field, head_count, head_width):
    length = field.shape[0]
    half_width = head_width // 2
    frequency = jnp.exp(-jnp.log(10000.0) * jnp.arange(half_width, dtype=jnp.float32) / half_width)
    angles = jnp.arange(length, dtype=jnp.float32)[:, None] * frequency[None, :]
    cosine = jnp.cos(angles)[:, None, :]
    sine_part = jnp.sin(angles)[:, None, :]
    shaped = field.reshape(length, head_count, head_width)
    first = shaped[..., :half_width]
    second = shaped[..., half_width:]
    turned = jnp.concatenate([first * cosine - second * sine_part, second * cosine + first * sine_part], axis=-1)
    return turned.reshape(length, head_count * head_width)

def rms_scale(field):
    return lax.rsqrt(lax.optimization_barrier(jnp.mean(field * field, axis=-1, keepdims=True)) + epsilon)

def sequence_layer(weight_set, pieces):
    gain_first, query_weight, key_weight, value_weight, output_weight, gain_second, router_weight, common_gate, common_up, common_down, pool_gate, pool_up, pool_down = weight_set
    token_rows, segment_ids, route_ids, slot_ids = pieces
    length = token_rows.shape[0]
    model_width = token_rows.shape[1]
    normed = low(token_rows * rms_scale(token_rows) * gain_first)
    query_pre = low_back(product(normed, query_weight))
    key_pre = low_back(product(normed, key_weight))
    value_pre = low_back(product(normed, value_weight))
    queries = low(rotate(query_pre, HEADS, HEAD_DIM)).reshape(length, HEADS, HEAD_DIM)
    key_rows = low(rotate(key_pre, HEADS, HEAD_DIM)).reshape(length, HEADS, HEAD_DIM)
    values = low(value_pre).reshape(length, HEADS, HEAD_DIM)
    positions = jnp.arange(length, dtype=jnp.int32)
    allowed = (positions[:, None] >= positions[None, :]) & (segment_ids[:, None] == segment_ids[None, :])
    score_scale = 1.0 / math.sqrt(HEAD_DIM)
    scores = jnp.einsum('qhd,khd->hqk', queries, key_rows, precision=highest) * score_scale
    scores = low_back(jnp.where(allowed[None], scores, -1e+30))
    attn_weights = low(jax.nn.softmax(scores, axis=-1))
    attended = jnp.einsum('hqk,khd->qhd', attn_weights, values, precision=highest).reshape(length, model_width)
    attended = low_back(low(attended))
    hidden = token_rows + low_back(product(attended, output_weight))
    mixed_in = low(hidden * rms_scale(hidden) * gain_second)
    router = jax.nn.softmax(low_back(product(mixed_in, router_weight)), axis=-1)
    gate_values = jnp.take_along_axis(router, route_ids, axis=1)
    common_g = low_back(product(mixed_in, common_gate))
    common_u = low_back(product(mixed_in, common_up))
    shared_inner = low(jax.nn.silu(common_g) * common_u)
    shared_out = low_back(product(shared_inner, common_down))
    flat_slots = (route_ids * CAP + slot_ids).reshape(-1).astype(jnp.int32)
    token_ids = jnp.repeat(positions, route_ids.shape[1]).astype(jnp.int32)
    holder = jnp.zeros((EXPERTS * CAP,), jnp.int32).at[flat_slots].set(token_ids)
    filled = jnp.zeros((EXPERTS * CAP,), jnp.float32).at[flat_slots].set(1.0)
    send_rows = low_back(jnp.take(mixed_in, holder, axis=0) * filled[:, None]).reshape(EXPERTS, CAP, model_width)
    pool_g = low_back(jnp.einsum('ecd,edf->ecf', send_rows, pool_gate, precision=highest))
    pool_u = low_back(jnp.einsum('ecd,edf->ecf', send_rows, pool_up, precision=highest))
    pool_inner = low(jax.nn.silu(pool_g) * pool_u)
    pool_result = low_back(low(jnp.einsum('ecf,efd->ecd', pool_inner, pool_down, precision=highest)))
    picked = jnp.take(pool_result.reshape(EXPERTS * CAP, model_width), flat_slots, axis=0)
    picked = picked.reshape(length, route_ids.shape[1], model_width)
    mixture = lax.optimization_barrier(jnp.sum(gate_values[:, :, None] * picked, axis=1))
    return hidden + shared_out + mixture

def reference(tokens, cotangent, segments, routes, slots, norm1_gain, w_query, w_key, w_value, w_out, norm2_gain, w_router, shared_gate, shared_up, shared_down, expert_gate, expert_up, expert_down):
    weight_set = tuple((array.astype(jnp.float32) for array in (norm1_gain, w_query, w_key, w_value, w_out, norm2_gain, w_router, shared_gate, shared_up, shared_down, expert_gate, expert_up, expert_down)))
    model_width = tokens.shape[-1]
    token_rows = tokens.astype(jnp.float32).reshape(-1, SEQ, model_width)
    segment_rows = segments.reshape(-1, SEQ)
    route_rows = routes.reshape(-1, SEQ, TOP)
    slot_rows = slots.reshape(-1, SEQ, TOP)

    def forward(weights_in, inputs):
        layer = jax.checkpoint(lambda piece: sequence_layer(weights_in, piece))
        return lax.map(layer, (inputs, segment_rows, route_rows, slot_rows))
    outputs, pullback = jax.vjp(forward, weight_set, token_rows)
    weight_grads, row_grads = pullback(cotangent.astype(jnp.float32).reshape(token_rows.shape))
    return (outputs.astype(jnp.bfloat16).reshape(tokens.shape), row_grads.reshape(tokens.shape), weight_grads[0], weight_grads[1], weight_grads[2], weight_grads[3], weight_grads[4], weight_grads[5], weight_grads[6], weight_grads[7], weight_grads[8], weight_grads[9], weight_grads[10], weight_grads[11], weight_grads[12])
```

```python
import functools
import math

import jax
import jax.numpy as jnp
from jax import lax
from jax.experimental import pallas as pl
from jax.experimental.pallas import tpu as pltpu
from jax.sharding import PartitionSpec as P

HEAD_DIM = 64
PAIR = 2 * HEAD_DIM
CAP = 40
LANES = 128
EPSILON = 1e-06
F32 = jnp.float32
BF16 = jnp.bfloat16
NN = (((1,), (0,)), ((), ()))
NT = (((1,), (1,)), ((), ()))
TN = (((0,), (0,)), ((), ()))
VMEM_BYTES = 60 * 1024 * 1024
ANY = pl.BlockSpec(memory_space=pl.ANY)


def mm(left, right, dims):
    return lax.dot_general(left, right, dims, preferred_element_type=F32)


def iota(shape, axis):
    return lax.broadcasted_iota(jnp.int32, shape, axis)


def first_step(i):
    return i ^ (2 if i % 2 == 0 else 4)


def second_step(i):
    return i ^ (4 if i % 2 == 0 else 2)


def core_step(i):
    return i ^ 1


def send(field, step):
    return lax.ppermute(field, "dp", [(i, step(i)) for i in range(8)])


def place_kernel(where, *refs):
    pieces, (out, held, came, left) = refs[:8], refs[8:]
    loads = [pltpu.make_async_copy(pieces[k], held.at[k], came.at[k]) for k in range(8)]
    stores = [pltpu.make_async_copy(held.at[k], out.at[where[k]], left.at[k]) for k in range(8)]
    for load in loads:
        load.start()
    for load, store in zip(loads, stores):
        load.wait()
        store.start()
    for store in stores:
        store.wait()


def gather_rows(part):
    count = lax.axis_size("dp")
    if count != 8:
        return lax.all_gather(part, "dp", axis=0)
    near = send(part, first_step)
    side = send(part, second_step)
    far = send(near, second_step)
    mine = [part, near, side, far]
    pieces = mine + [send(piece, core_step) for piece in mine]
    index = lax.axis_index("dp")
    even = jnp.array([0, 2, 4, 6], jnp.int32)
    odd = jnp.array([0, 4, 2, 6], jnp.int32)
    own = jnp.where(index % 2 == 0, even, odd)
    other = jnp.where(index % 2 == 0, odd, even)
    where = jnp.concatenate([index ^ own, (index ^ 1) ^ other]).astype(jnp.int32)
    size = part.size * part.dtype.itemsize * 8
    return pl.pallas_call(
        place_kernel,
        out_shape=jax.ShapeDtypeStruct((8,) + part.shape, part.dtype),
        in_specs=[pl.BlockSpec(memory_space=pltpu.SMEM)] + [ANY] * 8,
        out_specs=ANY,
        scratch_shapes=[
            pltpu.VMEM((8,) + part.shape, part.dtype),
            pltpu.SemaphoreType.DMA((8,)),
            pltpu.SemaphoreType.DMA((8,)),
        ],
        cost_estimate=pl.CostEstimate(flops=0, bytes_accessed=2 * size, transcendentals=0),
        name="place",
    )(where, *pieces)


def scatter_rows(field):
    count = lax.axis_size("dp")
    if count != 8:
        return lax.psum_scatter(field, "dp", scatter_dimension=0, tiled=False)
    index = lax.axis_index("dp")
    core, x, y = index % 2, (index // 2) % 2, index // 4
    take = functools.partial(lax.dynamic_index_in_dim, keepdims=False)
    blocks = field.reshape((4, 2) + field.shape[1:])
    came = send(take(blocks, 1 - core, 1), core_step)
    total = (take(blocks, core, 1).astype(F32) + came.astype(F32)).astype(BF16)
    one, two = jnp.where(core == 0, x, y), jnp.where(core == 0, y, x)

    def at(first, second):
        return take(total, jnp.where(core == 0, second * 2 + first, first * 2 + second), 0)

    came = send(jnp.stack([at(1 - one, two), at(1 - one, 1 - two)]), first_step).astype(F32)
    keep = (at(one, two).astype(F32) + came[0]).astype(BF16)
    pass_on = (at(one, 1 - two).astype(F32) + came[1]).astype(BF16)
    return (keep.astype(F32) + send(pass_on, second_step).astype(F32)).astype(BF16)


def place_of(flat, rows):
    at = iota((rows, flat.shape[1]), 0)
    held = jnp.logical_or(flat[0:1, :] == at, flat[1:2, :] == at)
    return jnp.where(held, 1.0, 0.0).astype(BF16)


def put_rows(sent, outs):
    at = 0
    for out in outs:
        for expert in range(out.shape[0]):
            out[expert, 0] = sent[at : at + CAP].astype(BF16)
            at += CAP


def dispatch_kernel(flat_ref, field_ref, *outs):
    rows = len(outs) * outs[0].shape[0] * CAP
    put_rows(mm(place_of(flat_ref[0], rows), field_ref[0], NN), outs)


def swap_halves(field):
    low = iota(field.shape, 1) % HEAD_DIM < HEAD_DIM // 2
    ahead = pltpu.roll(field, PAIR - HEAD_DIM // 2, 1)
    behind = pltpu.roll(field, HEAD_DIM // 2, 1)
    return jnp.where(low, ahead, behind)


def turn(field, cosine, sine):
    return field * cosine + swap_halves(field) * sine


def allowed_of(column_ref, row_ref):
    length = row_ref.shape[2]
    square = (length, length)
    return jnp.logical_and(iota(square, 0) >= iota(square, 1), column_ref[0] == row_ref[0])


def inverse_rms(field):
    return lax.rsqrt(jnp.mean(field * field, axis=-1, keepdims=True) + EPSILON)


def forward_kernel(
    experts, tokens_ref, column_ref, row_ref, flat_ref, weight_ref, gain_one_ref, gain_two_ref, cosine_ref, sine_ref,
    hidden_ref, mixed_ref, attended_ref, qkv_ref, logsum_ref, router_ref, *outs,
):
    width = tokens_ref.shape[2]
    x = tokens_ref[0].astype(F32)
    normed = (x * inverse_rms(x) * gain_one_ref[...]).astype(BF16)
    allowed = allowed_of(column_ref, row_ref)
    cosine, sine = cosine_ref[...], sine_ref[...]
    low = iota((x.shape[0], PAIR), 1) < HEAD_DIM
    lane = iota((x.shape[0], LANES), 1)
    logsum = jnp.zeros((x.shape[0], LANES), F32)
    for pair in range(width // PAIR):
        at = slice(pair * PAIR, (pair + 1) * PAIR)
        query = turn(mm(normed, weight_ref[:, at], NN), cosine, sine).astype(BF16) * BF16(0.125)
        key = turn(mm(normed, weight_ref[:, width + at.start : width + at.stop], NN), cosine, sine).astype(BF16)
        value = mm(normed, weight_ref[:, 2 * width + at.start : 2 * width + at.stop], NN).astype(BF16)
        qkv_ref[0, :, at] = query
        qkv_ref[0, :, width + at.start : width + at.stop] = key
        qkv_ref[0, :, 2 * width + at.start : 2 * width + at.stop] = value
        both = []
        for half in range(2):
            mine = low if half == 0 else jnp.logical_not(low)
            scores = jnp.where(allowed, mm(jnp.where(mine, query, BF16(0.0)), key, NT), -1e30)
            peak = jnp.max(scores, axis=-1, keepdims=True)
            expo = jnp.exp(scores - peak)
            total = jnp.sum(expo, axis=-1, keepdims=True)
            logsum = jnp.where(lane == 2 * pair + half, peak + jnp.log(total), logsum)
            both.append(mm((expo * (1.0 / total)).astype(BF16), value, NN))
        attended_ref[0, :, at] = jnp.where(low, both[0], both[1]).astype(BF16)
    logsum_ref[0] = logsum
    hidden = x + mm(attended_ref[0], weight_ref[:, 3 * width : 4 * width], NN)
    hidden_ref[0] = hidden
    mixed = (hidden * inverse_rms(hidden) * gain_two_ref[...]).astype(BF16)
    mixed_ref[0] = mixed
    logits = jnp.where(lane < experts, mm(mixed, weight_ref[:, 4 * width :], NN), -1e30)
    expo = jnp.exp(logits - jnp.max(logits, axis=-1, keepdims=True))
    router_ref[0] = expo / jnp.sum(expo, axis=-1, keepdims=True)
    put_rows(mm(place_of(flat_ref[0], experts * CAP), mixed, NN), outs)


def get_rows(pieces, held_ref):
    at = 0
    for piece in pieces:
        for expert in range(piece.shape[0]):
            held_ref[at : at + CAP, :] = piece[expert, 0].astype(F32)
            at += CAP
    return held_ref[...].astype(BF16)


def backward_kernel(
    experts, count, tokens_ref, grad_ref, column_ref, row_ref, flat_ref, routes_ref, weight_ref, gain_one_ref, gain_two_ref,
    cosine_ref, sine_ref, hidden_ref, mixed_ref, attended_ref, qkv_ref, logsum_ref, router_ref, shared_ref, d_mixed_ref, *refs,
):
    returned, d_back = refs[:count], refs[count : 2 * count]
    out_ref, grad_tokens_ref, grad_weight_ref, held_ref, sum_ref, gains_ref, d_qkv_ref = refs[2 * count :]
    width = tokens_ref.shape[2]
    step = pl.program_id(0)

    @pl.when(step == 0)
    def _():
        sum_ref[...] = jnp.zeros_like(sum_ref)
        gains_ref[...] = jnp.zeros_like(gains_ref)

    length = tokens_ref.shape[1]
    lane = iota((length, LANES), 1)
    grad = grad_ref[0].astype(F32)
    hidden = hidden_ref[0]
    mixed = mixed_ref[0]
    router = router_ref[0]
    flat = flat_ref[0]
    rows = experts * CAP
    at_row = iota((rows, length), 0)
    came = get_rows(returned, held_ref)
    layer = hidden + shared_ref[0]
    d_router = jnp.zeros((length, LANES), F32)
    for choice in range(2):
        place = jnp.where(flat[choice : choice + 1, :] == at_row, 1.0, 0.0).astype(BF16)
        picked = mm(place, came, TN)
        chosen = lane == routes_ref[0, :, choice : choice + 1]
        gate = jnp.sum(jnp.where(chosen, router, 0.0), axis=-1, keepdims=True)
        layer = layer + gate * picked
        d_gate = jnp.sum(grad * picked, axis=-1, keepdims=True)
        d_router = d_router + jnp.where(chosen, d_gate, 0.0)
    out_ref[0] = layer.astype(BF16)
    d_logits = (router * (d_router - jnp.sum(router * d_router, axis=-1, keepdims=True))).astype(BF16)
    sum_ref[:, 4 * width :] += mm(mixed, d_logits, TN)
    came = get_rows(d_back, held_ref)
    d_mixed = d_mixed_ref[0] + mm(place_of(flat, rows), came, TN) + mm(d_logits, weight_ref[:, 4 * width :], NT)

    inverse_two = inverse_rms(hidden)
    unit_two = hidden * inverse_two
    gains_ref[1:2, :] += jnp.sum(d_mixed * unit_two, axis=0, keepdims=True)
    scaled = d_mixed * gain_two_ref[...]
    d_hidden = grad + inverse_two * (scaled - unit_two * jnp.mean(scaled * unit_two, axis=-1, keepdims=True))
    d_branch = d_hidden.astype(BF16)
    sum_ref[:, 3 * width : 4 * width] += mm(attended_ref[0], d_branch, TN)
    d_attended = mm(d_branch, weight_ref[:, 3 * width : 4 * width], NT).astype(BF16)

    allowed = allowed_of(column_ref, row_ref)
    cosine, sine = cosine_ref[...], -sine_ref[...]
    low = iota((length, PAIR), 1) < HEAD_DIM
    logsum = logsum_ref[0]
    for pair in range(width // PAIR):
        at = slice(pair * PAIR, (pair + 1) * PAIR)
        query = qkv_ref[0, :, at]
        key = qkv_ref[0, :, width + at.start : width + at.stop]
        value = qkv_ref[0, :, 2 * width + at.start : 2 * width + at.stop]
        d_out = d_attended[:, at]
        parts = []
        for half in range(2):
            mine = low if half == 0 else jnp.logical_not(low)
            scores = jnp.where(allowed, mm(jnp.where(mine, query, BF16(0.0)), key, NT), -1e30)
            head = 2 * pair + half
            probs = jnp.exp(scores - logsum[:, head : head + 1])
            d_probs = mm(jnp.where(mine, d_out, BF16(0.0)), value, NT)
            d_scores = (probs * (d_probs - jnp.sum(probs * d_probs, axis=-1, keepdims=True))).astype(BF16)
            parts.append((mm(d_scores, key, NN), mm(d_scores, query, TN), mm(probs.astype(BF16), d_out, TN)))
        d_query, d_key, d_value = (jnp.where(low, a, b) for a, b in zip(*parts))
        d_qkv_ref[:, at] = turn(d_query * 0.125, cosine, sine).astype(BF16)
        d_qkv_ref[:, width + at.start : width + at.stop] = turn(d_key, cosine, sine).astype(BF16)
        d_qkv_ref[:, 2 * width + at.start : 2 * width + at.stop] = d_value.astype(BF16)

    x = tokens_ref[0].astype(F32)
    inverse_one = inverse_rms(x)
    unit_one = x * inverse_one
    normed = (unit_one * gain_one_ref[...]).astype(BF16)
    d_qkv = d_qkv_ref[...]
    sum_ref[:, : 3 * width] += mm(normed, d_qkv, TN)
    d_normed = mm(d_qkv, weight_ref[:, : 3 * width], NT)
    gains_ref[0:1, :] += jnp.sum(d_normed * unit_one, axis=0, keepdims=True)
    scaled = d_normed * gain_one_ref[...]
    grad_tokens_ref[0] = d_hidden + inverse_one * (
        scaled - unit_one * jnp.mean(scaled * unit_one, axis=-1, keepdims=True))

    @pl.when(step == pl.num_programs(0) - 1)
    def _():
        grad_weight_ref[:, : 4 * width] = sum_ref[:, : 4 * width].astype(BF16)
        gains = jnp.concatenate(
            [jnp.zeros((experts, width), F32), gains_ref[...], jnp.zeros((LANES - experts - 8, width), F32)], axis=0)
        grad_weight_ref[:, 4 * width :] = (sum_ref[:, 4 * width :] + gains.T).astype(BF16)


def feed_kernel(count, gated, *refs):
    rows_in, grads_in = refs[:count], refs[count : 2 * count]
    refs = refs[2 * count :]
    gates_in = refs[: count if gated else 0]
    refs = refs[len(gates_in) :]
    gate_ref, up_ref, down_ref = refs[:3]
    rows_out, grads_out = refs[3 : 3 + count], refs[3 + count : 3 + 2 * count]
    grad_in_ref, grad_down_ref, x_ref, d_ref, out_ref, dx_ref = refs[3 + 2 * count :]
    part = rows_in[0].shape[0]
    step = pl.program_id(1)

    @pl.when(step == 0)
    def _():
        out_ref[...] = jnp.zeros_like(out_ref)
        dx_ref[...] = jnp.zeros_like(dx_ref)
        for k in range(count):
            at = slice(k * part, (k + 1) * part)
            x_ref[at, :] = rows_in[k][...]
            grads = grads_in[k][...]
            if gated:
                square = (part, part)
                line = jnp.broadcast_to(gates_in[k][...], square)
                column = jnp.sum(jnp.where(iota(square, 0) == iota(square, 1), line, 0.0), axis=1, keepdims=True)
                grads = (grads.astype(F32) * column).astype(BF16)
            d_ref[at, :] = grads

    x, d = x_ref[...], d_ref[...]
    gate_weight, up_weight, down_weight = gate_ref[...], up_ref[...], down_ref[...]
    g = mm(x, gate_weight, NN)
    u = mm(x, up_weight, NN)
    sigma = 1.0 / (1.0 + jnp.exp(-g))
    active = g * sigma
    inner = (active * u).astype(BF16)
    out_ref[...] += mm(inner, down_weight, NN)
    d_inner = mm(d, down_weight, NT)
    d_g = (d_inner * u * (sigma * (1.0 + g * (1.0 - sigma)))).astype(BF16)
    d_u = (d_inner * active).astype(BF16)
    dx_ref[...] += mm(d_g, gate_weight, NT) + mm(d_u, up_weight, NT)
    grad_in_ref[0] = mm(x, d_g, TN).astype(BF16)
    grad_in_ref[1] = mm(x, d_u, TN).astype(BF16)
    grad_down_ref[...] = mm(inner, d, TN).astype(BF16)

    @pl.when(step == pl.num_programs(1) - 1)
    def _():
        for k in range(count):
            at = slice(k * part, (k + 1) * part)
            rows_out[k][...] = out_ref[at, :].astype(rows_out[k].dtype)
            grads_out[k][...] = dx_ref[at, :].astype(grads_out[k].dtype)


def feed(rows, grads, gates, both, down, block, out_dtype, name):
    count = len(rows)
    experts, part, width = rows[0].shape
    units = down.shape[1]
    squeezed = pl.Squeezed()
    piece = pl.BlockSpec((squeezed, part, width), lambda l, f: (l, 0, 0))
    gate = pl.BlockSpec((squeezed, 1, part), lambda l, f: (l, 0, 0))
    total = count * part
    outs = pl.pallas_call(
        functools.partial(feed_kernel, count, bool(gates)),
        grid=(experts, units // block),
        in_specs=[piece] * (2 * count)
        + [gate] * len(gates)
        + [
            pl.BlockSpec((squeezed, squeezed, width, block), lambda l, f: (l, 0, 0, f)),
            pl.BlockSpec((squeezed, squeezed, width, block), lambda l, f: (l, 1, 0, f)),
            pl.BlockSpec((squeezed, block, width), lambda l, f: (l, f, 0)),
        ],
        out_specs=[piece] * (2 * count)
        + [
            pl.BlockSpec((squeezed, 2, width, block), lambda l, f: (l, 0, 0, f)),
            pl.BlockSpec((squeezed, block, width), lambda l, f: (l, f, 0)),
        ],
        out_shape=[jax.ShapeDtypeStruct((experts, part, width), out_dtype)] * (2 * count)
        + [
            jax.ShapeDtypeStruct((experts, 2, width, units), BF16),
            jax.ShapeDtypeStruct((experts, units, width), BF16),
        ],
        scratch_shapes=[
            pltpu.VMEM((total, width), BF16),
            pltpu.VMEM((total, width), BF16),
            pltpu.VMEM((total, width), F32),
            pltpu.VMEM((total, width), F32),
        ],
        compiler_params=pltpu.CompilerParams(vmem_limit_bytes=VMEM_BYTES),
        cost_estimate=pl.CostEstimate(
            flops=18 * experts * total * width * units,
            bytes_accessed=experts * (12 * width * units + 8 * total * width),
            transcendentals=experts * total * units,
        ),
        name=name,
    )(*rows, *grads, *gates, both, both, down)
    return outs[:count], outs[count : 2 * count], outs[-2], outs[-1]


def on_device(
    tokens, cotangent, segments, routes, slots,
    norm1_gain, w_query, w_key, w_value, w_out, norm2_gain, w_router,
    shared_gate, shared_up, shared_down, expert_gate, expert_up, expert_down,
):
    length, width = tokens.shape[2], tokens.shape[3]
    batch = tokens.shape[0] * tokens.shape[1]
    devices = lax.axis_size("dp")
    owners = lax.axis_size("expert")
    local_experts = expert_gate.shape[0]
    experts = owners * local_experts
    hidden_units = shared_gate.shape[1]
    groups = 2
    group_size = local_experts // groups
    count = groups * owners
    own_owner = lax.axis_index("expert")

    pad = LANES - experts - 2
    first_part = jnp.concatenate(
        [w_query, w_key, w_value, w_out, w_router, norm1_gain[:, None], norm2_gain[:, None],
         jnp.zeros((w_query.shape[0], pad), BF16)], axis=1)
    first_all = gather_rows(first_part).reshape(width, -1)
    shared_both = jnp.stack(
        [gather_rows(shared_gate).reshape(width, -1), gather_rows(shared_up).reshape(width, -1)])[None]
    shared_dn = gather_rows(shared_down).reshape(1, hidden_units, width)
    pool_in, pool_dn = [], []
    for h in range(groups):
        part = slice(h * group_size, (h + 1) * group_size)
        both = jnp.stack([expert_gate[part], expert_up[part]], axis=1)
        pool_in.append(lax.all_gather(both, "dp", axis=2, tiled=True))
        pool_dn.append(lax.all_gather(expert_down[part], "dp", axis=1, tiled=True))
    gains = first_all[:, 4 * width + experts : 4 * width + experts + 2].astype(F32).T
    gain_one, gain_two = gains[0:1], gains[1:2]

    route_ids = routes.reshape(batch, length, 2)
    owner_of = (route_ids // local_experts) ^ own_owner
    local = route_ids % local_experts
    flat = ((local // group_size * owners + owner_of) * group_size + local % group_size) * CAP
    flat = (flat + slots.reshape(batch, length, 2)).transpose(0, 2, 1)

    def trade(field, k):
        if k == 0:
            return field
        return lax.ppermute(field, "expert", [(i, i ^ k) for i in range(owners)])

    def trade_all(pieces):
        return [trade(piece, n % owners) for n, piece in enumerate(pieces)]

    def lined(pieces):
        return [piece.reshape(group_size, batch * CAP, width) for piece in pieces]

    whole = lambda shape: pl.BlockSpec(shape, lambda b: (0,) * len(shape))
    each = lambda *shape: pl.BlockSpec((1,) + shape, lambda b: (b, 0, 0))
    piece_spec = pl.BlockSpec((group_size, 1, CAP, width), lambda b: (0, b, 0, 0))
    piece_shape = jax.ShapeDtypeStruct((group_size, batch, CAP, width), BF16)
    rows = experts * CAP
    params = pltpu.CompilerParams(vmem_limit_bytes=VMEM_BYTES)

    grad_low = cotangent.reshape(batch, length, width)
    grad_sent = pl.pallas_call(
        dispatch_kernel,
        grid=(batch,),
        in_specs=[each(2, length), each(length, width)],
        out_specs=[piece_spec] * count,
        out_shape=[piece_shape] * count,
        compiler_params=params,
        cost_estimate=pl.CostEstimate(
            flops=2 * batch * rows * length * width, bytes_accessed=4 * batch * rows * width, transcendentals=0),
        name="dispatch",
    )(flat, grad_low)
    grad_arrived = trade_all(grad_sent)

    token_rows = tokens.reshape(batch, length, width)
    segment_ids = segments.reshape(batch, length)
    half = HEAD_DIM // 2
    frequency = jnp.exp(-jnp.log(10000.0) * jnp.arange(half, dtype=F32) / half)
    angles = jnp.arange(length, dtype=F32)[:, None] * frequency[None, :]
    cosine = jnp.tile(jnp.cos(angles), (1, 4))
    sine = jnp.tile(jnp.concatenate([-jnp.sin(angles), jnp.sin(angles)], axis=1), (1, 2))
    columns = first_all.shape[1]
    position_args = (segment_ids[:, :, None], segment_ids[:, None, :], flat)
    position_specs = [each(length, 1), each(1, length), each(2, length)]
    weight_args = (first_all, gain_one, gain_two, cosine, sine)
    weight_specs = [
        whole((width, columns)), whole((1, width)), whole((1, width)), whole((length, LANES)), whole((length, LANES))]
    kept_shapes = [
        jax.ShapeDtypeStruct((batch, length, width), F32),
        jax.ShapeDtypeStruct((batch, length, width), BF16),
        jax.ShapeDtypeStruct((batch, length, width), BF16),
        jax.ShapeDtypeStruct((batch, length, 3 * width), BF16),
        jax.ShapeDtypeStruct((batch, length, LANES), F32),
        jax.ShapeDtypeStruct((batch, length, LANES), F32),
    ]
    kept_specs = [each(*shape.shape[1:]) for shape in kept_shapes]
    tokens_all = batch * length
    outs = pl.pallas_call(
        functools.partial(forward_kernel, experts),
        grid=(batch,),
        in_specs=[each(length, width)] + position_specs + weight_specs,
        out_specs=kept_specs + [piece_spec] * count,
        out_shape=kept_shapes + [piece_shape] * count,
        compiler_params=params,
        cost_estimate=pl.CostEstimate(
            flops=2 * tokens_all * width * (columns + 4 * length + rows),
            bytes_accessed=2 * width * columns + tokens_all * width * 20,
            transcendentals=tokens_all * length * width // HEAD_DIM,
        ),
        name="attention",
    )(token_rows, *position_args, *weight_args)
    kept, sent = outs[:6], outs[6:]
    mixed_in, router = kept[1], kept[5]
    arrived = trade_all(sent)
    chosen = route_ids[..., None] == jnp.arange(experts, dtype=jnp.int32)
    gates = jnp.sum(jnp.where(chosen, router[:, :, None, :experts], 0.0), axis=-1).transpose(0, 2, 1)
    held = flat[:, :, None, :] == jnp.arange(rows, dtype=jnp.int32)[:, None]
    slot_gates = jnp.sum(jnp.where(held, gates[:, :, None, :], 0.0), axis=(1, 3))
    slot_gates = slot_gates.reshape(batch, groups, owners, group_size, CAP).transpose(2, 1, 3, 0, 4)
    slot_gates = slot_gates.reshape(owners, groups, group_size, 1, batch * CAP)
    slot_gates = [trade(slot_gates[k], k) for k in range(owners)]

    shared_out, d_mixed, grad_shared_both, grad_shared_dn = feed(
        [mixed_in.reshape(1, tokens_all, width)], [grad_low.reshape(1, tokens_all, width)], [],
        shared_both, shared_dn, 512, F32, "shared")

    returned, d_back, pool_in_mine, pool_dn_mine = [], [], [], []
    for h in range(groups):
        part = slice(h * owners, (h + 1) * owners)
        results, d_send, grad_both, grad_dn = feed(
            lined(arrived[part]), lined(grad_arrived[part]), [gate[h] for gate in slot_gates],
            pool_in[h], pool_dn[h], 512, BF16, "experts")
        returned += trade_all(results)
        d_back += trade_all(d_send)
        pool_dn_mine.append(lax.psum_scatter(grad_dn, "dp", scatter_dimension=1, tiled=True))
        pool_in_mine.append(lax.psum_scatter(grad_both, "dp", scatter_dimension=2, tiled=True))
    unlined = lambda pieces: [piece.reshape(piece_shape.shape) for piece in pieces]
    pool_dn_mine = jnp.concatenate(pool_dn_mine, axis=0).astype(F32)
    pool_in_mine = jnp.concatenate(pool_in_mine, axis=0).astype(F32)

    layer_out, grad_tokens, first_grad = pl.pallas_call(
        functools.partial(backward_kernel, experts, count),
        grid=(batch,),
        in_specs=[each(length, width)] * 2 + position_specs + [each(length, 2)] + weight_specs + kept_specs
        + [each(length, width)] * 2 + [piece_spec] * (2 * count),
        out_specs=[each(length, width)] * 2 + [whole((width, columns))],
        out_shape=[
            jax.ShapeDtypeStruct((batch, length, width), BF16),
            jax.ShapeDtypeStruct((batch, length, width), F32),
            jax.ShapeDtypeStruct((width, columns), BF16),
        ],
        scratch_shapes=[
            pltpu.VMEM((rows, width), F32),
            pltpu.VMEM((width, columns), F32),
            pltpu.VMEM((8, width), F32),
            pltpu.VMEM((length, 3 * width), BF16),
        ],
        compiler_params=params,
        cost_estimate=pl.CostEstimate(
            flops=4 * tokens_all * width * (columns + 4 * length + rows),
            bytes_accessed=4 * width * columns + tokens_all * width * 32,
            transcendentals=tokens_all * length * width // HEAD_DIM,
        ),
        name="attention_back",
    )(
        token_rows, grad_low, *position_args, route_ids, *weight_args, *kept,
        shared_out[0].reshape(batch, length, width), d_mixed[0].reshape(batch, length, width),
        *unlined(returned), *unlined(d_back),
    )

    def finish(field):
        mine = scatter_rows(field.reshape((devices, field.shape[0] // devices) + field.shape[1:]))
        total = mine.astype(F32)
        for k in range(1, owners):
            total = total + trade(mine, k).astype(F32)
        return total

    shared_dn_mine = finish(grad_shared_dn[0])
    shared_gate_mine = finish(grad_shared_both[0, 0])
    shared_up_mine = finish(grad_shared_both[0, 1])
    first_mine = finish(first_grad)
    return (
        layer_out.reshape(tokens.shape),
        grad_tokens.reshape(tokens.shape),
        first_mine[:, 4 * width + experts],
        first_mine[:, :width],
        first_mine[:, width : 2 * width],
        first_mine[:, 2 * width : 3 * width],
        first_mine[:, 3 * width : 4 * width],
        first_mine[:, 4 * width + experts + 1],
        first_mine[:, 4 * width : 4 * width + experts],
        shared_gate_mine,
        shared_up_mine,
        shared_dn_mine,
        pool_in_mine[:, 0],
        pool_in_mine[:, 1],
        pool_dn_mine,
    )


def solution(mesh):
    token_spec = P(None, ("dp", "expert"), None, None)
    vector, matrix, pool = P("dp"), P("dp", None), P("expert", "dp", None)
    weights = (vector, matrix, matrix, matrix, matrix, vector, matrix, matrix, matrix, matrix, pool, pool, pool)
    return jax.shard_map(
        on_device,
        mesh=mesh,
        in_specs=(token_spec, token_spec, P(None, ("dp", "expert"), None), token_spec, token_spec) + weights,
        out_specs=(token_spec, token_spec) + weights,
        check_vma=False,
    )
```

```python
import functools

import jax
import jax.numpy as jnp
from jax import lax
from jax.experimental import pallas as pl
from jax.experimental.pallas import tpu as pltpu
from jax.sharding import PartitionSpec as P

HEAD_DIM = 64
PAIR = 2 * HEAD_DIM
CAP = 40
LANES = 128
EPSILON = 1e-06
F32 = jnp.float32
BF16 = jnp.bfloat16
NN = (((1,), (0,)), ((), ()))
NT = (((1,), (1,)), ((), ()))
TN = (((0,), (0,)), ((), ()))
VMEM_BYTES = 60 * 1024 * 1024
ANY = pl.BlockSpec(memory_space=pl.ANY)


def mm(left, right, dims):
    return lax.dot_general(left, right, dims, preferred_element_type=F32)


def iota(shape, axis):
    return lax.broadcasted_iota(jnp.int32, shape, axis)


def skipping(body, inputs, unread):
    return lambda *refs: body(*refs[:inputs], *refs[inputs + unread :])


def tie(field, *after):
    return pl.pallas_call(
        lambda *refs: None,
        out_shape=jax.ShapeDtypeStruct(field.shape, field.dtype),
        in_specs=[ANY] * (1 + len(after)),
        out_specs=ANY,
        input_output_aliases={0: 0},
        name="tie",
    )(field, *after)


def place_of(flat, rows):
    at = iota((rows, flat.shape[1]), 0)
    held = jnp.logical_or(flat[0:1, :] == at, flat[1:2, :] == at)
    return jnp.where(held, 1.0, 0.0).astype(BF16)


def put_rows(sent, out):
    for expert in range(out.shape[0]):
        out[expert, 0] = sent[expert * CAP : (expert + 1) * CAP].astype(BF16)


def dispatch_kernel(flat_ref, field_ref, out_ref):
    put_rows(mm(place_of(flat_ref[0], out_ref.shape[0] * CAP), field_ref[0], NN), out_ref)


def swap_halves(field):
    low = iota(field.shape, 1) % HEAD_DIM < HEAD_DIM // 2
    ahead = pltpu.roll(field, PAIR - HEAD_DIM // 2, 1)
    behind = pltpu.roll(field, HEAD_DIM // 2, 1)
    return jnp.where(low, ahead, behind)


def turn(field, cosine, sine):
    return field * cosine + swap_halves(field) * sine


def allowed_of(column_ref, row_ref):
    length = row_ref.shape[2]
    square = (length, length)
    return jnp.logical_and(iota(square, 0) >= iota(square, 1), column_ref[0] == row_ref[0])


def inverse_rms(field):
    return lax.rsqrt(jnp.mean(field * field, axis=-1, keepdims=True) + EPSILON)


def forward_kernel(
    experts, tokens_ref, column_ref, row_ref, flat_ref, weight_ref, gain_one_ref, gain_two_ref, cosine_ref, sine_ref,
    hidden_ref, mixed_ref, attended_ref, qkv_ref, logsum_ref, router_ref, sent_ref,
):
    width = tokens_ref.shape[2]
    x = tokens_ref[0].astype(F32)
    normed = (x * inverse_rms(x) * gain_one_ref[...]).astype(BF16)
    allowed = allowed_of(column_ref, row_ref)
    cosine, sine = cosine_ref[...], sine_ref[...]
    low = iota((x.shape[0], PAIR), 1) < HEAD_DIM
    lane = iota((x.shape[0], LANES), 1)
    logsum = jnp.zeros((x.shape[0], LANES), F32)
    for pair in range(width // PAIR):
        at = slice(pair * PAIR, (pair + 1) * PAIR)
        query = turn(mm(normed, weight_ref[:, at], NN), cosine, sine).astype(BF16) * BF16(0.125)
        key = turn(mm(normed, weight_ref[:, width + at.start : width + at.stop], NN), cosine, sine).astype(BF16)
        value = mm(normed, weight_ref[:, 2 * width + at.start : 2 * width + at.stop], NN).astype(BF16)
        qkv_ref[0, :, at] = query
        qkv_ref[0, :, width + at.start : width + at.stop] = key
        qkv_ref[0, :, 2 * width + at.start : 2 * width + at.stop] = value
        both = []
        for half in range(2):
            mine = low if half == 0 else jnp.logical_not(low)
            scores = jnp.where(allowed, mm(jnp.where(mine, query, BF16(0.0)), key, NT), -1e30)
            peak = jnp.max(scores, axis=-1, keepdims=True)
            expo = jnp.exp(scores - peak)
            total = jnp.sum(expo, axis=-1, keepdims=True)
            logsum = jnp.where(lane == 2 * pair + half, peak + jnp.log(total), logsum)
            both.append(mm((expo * (1.0 / total)).astype(BF16), value, NN))
        attended_ref[0, :, at] = jnp.where(low, both[0], both[1]).astype(BF16)
    logsum_ref[0] = logsum
    hidden = x + mm(attended_ref[0], weight_ref[:, 3 * width : 4 * width], NN)
    hidden_ref[0] = hidden
    mixed = (hidden * inverse_rms(hidden) * gain_two_ref[...]).astype(BF16)
    mixed_ref[0] = mixed
    logits = jnp.where(lane < experts, mm(mixed, weight_ref[:, 4 * width :], NN), -1e30)
    expo = jnp.exp(logits - jnp.max(logits, axis=-1, keepdims=True))
    router_ref[0] = expo / jnp.sum(expo, axis=-1, keepdims=True)
    put_rows(mm(place_of(flat_ref[0], experts * CAP), mixed, NN), sent_ref)


def get_rows(backs, which, experts, held_ref):
    owners, _, size = backs[0].shape[:3]
    for expert in range(experts):
        owner, local = expert // (len(backs) * size), expert % (len(backs) * size)
        held_ref[expert * CAP : (expert + 1) * CAP, :] = backs[local // size][owner, which, local % size, 0].astype(F32)
    return held_ref[...].astype(BF16)


def backward_kernel(
    experts, groups, tokens_ref, grad_ref, column_ref, row_ref, flat_ref, routes_ref, weight_ref, gain_one_ref, gain_two_ref,
    cosine_ref, sine_ref, hidden_ref, mixed_ref, attended_ref, qkv_ref, logsum_ref, router_ref, shared_ref, d_mixed_ref, *refs,
):
    backs = refs[:groups]
    out_ref, grad_tokens_ref, grad_weight_ref, held_ref, sum_ref, gains_ref, d_qkv_ref = refs[groups:]
    width = tokens_ref.shape[2]
    step = pl.program_id(0)

    @pl.when(step == 0)
    def _():
        sum_ref[...] = jnp.zeros_like(sum_ref)
        gains_ref[...] = jnp.zeros_like(gains_ref)

    length = tokens_ref.shape[1]
    lane = iota((length, LANES), 1)
    grad = grad_ref[0].astype(F32)
    hidden = hidden_ref[0]
    mixed = mixed_ref[0]
    router = router_ref[0]
    flat = flat_ref[0]
    rows = experts * CAP
    at_row = iota((rows, length), 0)
    came = get_rows(backs, 0, experts, held_ref)
    layer = hidden + shared_ref[0]
    d_router = jnp.zeros((length, LANES), F32)
    for choice in range(2):
        place = jnp.where(flat[choice : choice + 1, :] == at_row, 1.0, 0.0).astype(BF16)
        picked = mm(place, came, TN)
        chosen = lane == routes_ref[0, :, choice : choice + 1]
        gate = jnp.sum(jnp.where(chosen, router, 0.0), axis=-1, keepdims=True)
        layer = layer + gate * picked
        d_gate = jnp.sum(grad * picked, axis=-1, keepdims=True)
        d_router = d_router + jnp.where(chosen, d_gate, 0.0)
    out_ref[0] = layer.astype(BF16)
    d_logits = (router * (d_router - jnp.sum(router * d_router, axis=-1, keepdims=True))).astype(BF16)
    sum_ref[:, 4 * width :] += mm(mixed, d_logits, TN)
    came = get_rows(backs, 1, experts, held_ref)
    d_mixed = d_mixed_ref[0] + mm(place_of(flat, rows), came, TN) + mm(d_logits, weight_ref[:, 4 * width :], NT)

    inverse_two = inverse_rms(hidden)
    unit_two = hidden * inverse_two
    gains_ref[1:2, :] += jnp.sum(d_mixed * unit_two, axis=0, keepdims=True)
    scaled = d_mixed * gain_two_ref[...]
    d_hidden = grad + inverse_two * (scaled - unit_two * jnp.mean(scaled * unit_two, axis=-1, keepdims=True))
    d_branch = d_hidden.astype(BF16)
    sum_ref[:, 3 * width : 4 * width] += mm(attended_ref[0], d_branch, TN)
    d_attended = mm(d_branch, weight_ref[:, 3 * width : 4 * width], NT).astype(BF16)

    allowed = allowed_of(column_ref, row_ref)
    cosine, sine = cosine_ref[...], -sine_ref[...]
    low = iota((length, PAIR), 1) < HEAD_DIM
    logsum = logsum_ref[0]
    for pair in range(width // PAIR):
        at = slice(pair * PAIR, (pair + 1) * PAIR)
        query = qkv_ref[0, :, at]
        key = qkv_ref[0, :, width + at.start : width + at.stop]
        value = qkv_ref[0, :, 2 * width + at.start : 2 * width + at.stop]
        d_out = d_attended[:, at]
        parts = []
        for half in range(2):
            mine = low if half == 0 else jnp.logical_not(low)
            scores = jnp.where(allowed, mm(jnp.where(mine, query, BF16(0.0)), key, NT), -1e30)
            head = 2 * pair + half
            probs = jnp.exp(scores - logsum[:, head : head + 1])
            d_probs = mm(jnp.where(mine, d_out, BF16(0.0)), value, NT)
            d_scores = (probs * (d_probs - jnp.sum(probs * d_probs, axis=-1, keepdims=True))).astype(BF16)
            parts.append((mm(d_scores, key, NN), mm(d_scores, query, TN), mm(probs.astype(BF16), d_out, TN)))
        d_query, d_key, d_value = (jnp.where(low, a, b) for a, b in zip(*parts))
        d_qkv_ref[:, at] = turn(d_query * 0.125, cosine, sine).astype(BF16)
        d_qkv_ref[:, width + at.start : width + at.stop] = turn(d_key, cosine, sine).astype(BF16)
        d_qkv_ref[:, 2 * width + at.start : 2 * width + at.stop] = d_value.astype(BF16)

    x = tokens_ref[0].astype(F32)
    inverse_one = inverse_rms(x)
    unit_one = x * inverse_one
    normed = (unit_one * gain_one_ref[...]).astype(BF16)
    d_qkv = d_qkv_ref[...]
    sum_ref[:, : 3 * width] += mm(normed, d_qkv, TN)
    d_normed = mm(d_qkv, weight_ref[:, : 3 * width], NT)
    gains_ref[0:1, :] += jnp.sum(d_normed * unit_one, axis=0, keepdims=True)
    scaled = d_normed * gain_one_ref[...]
    grad_tokens_ref[0] = d_hidden + inverse_one * (
        scaled - unit_one * jnp.mean(scaled * unit_one, axis=-1, keepdims=True))

    @pl.when(step == pl.num_programs(0) - 1)
    def _():
        grad_weight_ref[:, : 4 * width] = sum_ref[:, : 4 * width].astype(BF16)
        gains = jnp.concatenate(
            [jnp.zeros((experts, width), F32), gains_ref[...], jnp.zeros((LANES - experts - 8, width), F32)], axis=0)
        grad_weight_ref[:, 4 * width :] = (sum_ref[:, 4 * width :] + gains.T).astype(BF16)


def pack_pieces(packed, gate, up, down):
    steps, width = packed.shape[1], packed.shape[2]
    rows = gate.shape[0]
    for f in range(steps):
        for j in range(width // rows):
            at = slice((j * steps + f) * LANES, (j * steps + f + 1) * LANES)
            yield packed.at[0, f, j * rows : (j + 1) * rows], gate.at[:, at]
            yield packed.at[1, f, j * rows : (j + 1) * rows], up.at[:, at]
        for c in range(width // LANES):
            at = slice(c * LANES, (c + 1) * LANES)
            yield packed.at[2, f, at], down.at[f * LANES : (f + 1) * LANES, at]


def pack_kernel(count, *refs):
    out = refs[-1]
    step = pl.program_id(0)
    for n in range((len(refs) - 1) // 3):
        @pl.when((step < count) if n == 0 else (step >= count))
        def _():
            for to, source in pack_pieces(out, *refs[3 * n : 3 * n + 3]):
                to[...] = source[...]


def pack(first, count, pool, shared, devices):
    rows, units = pool[0].shape[1:]
    width = rows * devices
    steps = units // (devices * LANES)
    squeezed = pl.Squeezed()
    take = lambda l: (first + jnp.minimum(l, count - 1), 0, 0)
    total = count + (1 if shared else 0)
    return pl.pallas_call(
        functools.partial(pack_kernel, count),
        grid=(total,),
        in_specs=[pl.BlockSpec((squeezed,) + field.shape[1:], take) for field in pool]
        + [pl.BlockSpec(field.shape, lambda l: (0, 0)) for field in shared],
        out_specs=pl.BlockSpec((squeezed, 3, steps, width, LANES), lambda l: (l, 0, 0, 0, 0)),
        out_shape=jax.ShapeDtypeStruct((total, 3, steps, width, LANES), BF16),
        name="pack",
    )(*pool, *shared)


def unpack_kernel(sizes, *refs):
    packs, outs = refs[: len(sizes)], refs[len(sizes) :]
    step = pl.program_id(0)
    start = 0
    for n, size in enumerate(sizes):
        @pl.when(jnp.logical_and(step >= start, step < start + size))
        def _(source=packs[n]):
            for piece, to in pack_pieces(source, *outs):
                to[...] = piece[...].astype(F32)
        start += size


def unpack(packs, sizes, rows, units, name):
    squeezed = pl.Squeezed()
    specs, start = [], 0
    for field, size in zip(packs, sizes):
        specs.append(pl.BlockSpec(
            (squeezed,) + field.shape[1:],
            lambda l, start=start, size=size: (jnp.clip(l - start, 0, size - 1), 0, 0, 0, 0)))
        start += size
    width = packs[0].shape[3]
    shapes = [(rows, units), (rows, units), (rows * units // width, width)]
    return pl.pallas_call(
        functools.partial(unpack_kernel, tuple(sizes)),
        grid=(start,),
        in_specs=specs,
        out_specs=[pl.BlockSpec((squeezed,) + shape, lambda l: (l, 0, 0)) for shape in shapes],
        out_shape=[jax.ShapeDtypeStruct((start,) + shape, F32) for shape in shapes],
        name=name,
    )(*packs)


def feed_step(x, d, gate_weight, up_weight, down_weight, out, dx):
    g = mm(x, gate_weight, NN)
    u = mm(x, up_weight, NN)
    sigma = 1.0 / (1.0 + jnp.exp(-g))
    active = g * sigma
    inner = (active * u).astype(BF16)
    out[...] += mm(inner, down_weight, NN)
    d_inner = mm(d, down_weight, NT)
    d_g = (d_inner * u * (sigma * (1.0 + g * (1.0 - sigma)))).astype(BF16)
    d_u = (d_inner * active).astype(BF16)
    dx[...] += mm(d_g, gate_weight, NT) + mm(d_u, up_weight, NT)
    return mm(x, d_g, TN).astype(BF16), mm(x, d_u, TN).astype(BF16), mm(inner, d, TN).astype(BF16)


def feed_kernel(gated, packed, rows_ref, grads_ref, *refs):
    if gated:
        gates_ref, refs = refs[0], refs[1:]
    count, part, width = rows_ref.shape
    weights = refs[: 1 if packed else 3]
    refs = refs[len(weights) :]
    if gated:
        back_ref, refs = refs[0], refs[1:]
        sums, (x_ref, d_ref, out_ref, dx_ref) = refs[:-4], refs[-4:]
    else:
        out_ref, dx_ref, sums = refs[0].at[0], refs[1].at[0], refs[2:]
    step = pl.program_id(1)

    @pl.when(step == 0)
    def _():
        out_ref[...] = jnp.zeros_like(out_ref)
        dx_ref[...] = jnp.zeros_like(dx_ref)
        if gated:
            square = (part, part)
            for k in range(count):
                at = slice(k * part, (k + 1) * part)
                x_ref[at, :] = rows_ref[k]
                line = jnp.broadcast_to(gates_ref[k], square)
                column = jnp.sum(jnp.where(iota(square, 0) == iota(square, 1), line, 0.0), axis=1, keepdims=True)
                d_ref[at, :] = (grads_ref[k].astype(F32) * column).astype(BF16)

    x, d = (x_ref[...], d_ref[...]) if gated else (rows_ref[0], grads_ref[0])
    if packed:
        field, total = weights[0], sums[0]
        devices = field.shape[0]
        rows = width // devices
        size = min(devices, 4)
        for start in range(0, devices, size):
            columns = range(start, start + size)
            side = lambda n: jnp.concatenate(
                [field[:, n, j * rows : (j + 1) * rows, :].reshape(width, LANES) for j in columns], axis=1)
            down = jnp.concatenate(
                [field[start : start + size, 2, c * LANES : (c + 1) * LANES, :].reshape(size * LANES, LANES)
                 for c in range(width // LANES)], axis=1)
            gate_sum, up_sum, down_sum = feed_step(x, d, side(0), side(1), down, out_ref, dx_ref)
            for n, value in enumerate((gate_sum, up_sum)):
                for j in columns:
                    total[:, n, j * rows : (j + 1) * rows, :] = value[
                        :, (j - start) * LANES : (j - start + 1) * LANES].reshape(devices, rows, LANES)
            for c in range(width // LANES):
                at = slice(c * LANES, (c + 1) * LANES)
                total[start : start + size, 2, at, :] = down_sum[:, at].reshape(size, LANES, LANES)
    else:
        sums[0][0], sums[0][1], sums[1][...] = feed_step(x, d, *(ref[...] for ref in weights), out_ref, dx_ref)

    if gated:
        @pl.when(step == pl.num_programs(1) - 1)
        def _():
            for k in range(count):
                at = slice(k * part, (k + 1) * part)
                back_ref[k, 0] = out_ref[at, :].astype(BF16)
                back_ref[k, 1] = dx_ref[at, :].astype(BF16)


def feed(rows, grads, gates, weights, first_row, first_weight, experts, name, carried=None, after=()):
    count, _, part, width = rows.shape
    squeezed = pl.Squeezed()
    gated, packed = gates is not None, len(weights) == 1
    total = count * part
    row = lambda l, f: (0, first_row + l, 0, 0)
    operands = [rows, grads] + ([gates] if gated else [])
    in_specs = [pl.BlockSpec((count, squeezed, part, width), row)] * 2
    in_specs += [pl.BlockSpec((count, squeezed, 1, part), row)] * gated
    if packed:
        devices, _, _, steps = weights[0].shape[:4]
        units = steps * devices * LANES
        pack_spec = pl.BlockSpec(
            (devices, squeezed, 3, squeezed, width, LANES), lambda l, f: (0, first_weight + l, 0, f, 0, 0))
        operands += weights
        in_specs += [pack_spec]
        sum_specs, sum_shapes = [pack_spec], [jax.ShapeDtypeStruct(weights[0].shape, BF16)]
    else:
        units, block = weights[1].shape[1], 512
        steps = units // block
        side = lambda n: pl.BlockSpec((squeezed, squeezed, width, block), lambda l, f: (l, n, 0, f))
        down_spec = pl.BlockSpec((squeezed, block, width), lambda l, f: (l, f, 0))
        operands += [weights[0], weights[0], weights[1]]
        in_specs += [side(0), side(1), down_spec]
        sum_specs = [pl.BlockSpec((squeezed, 2, width, block), lambda l, f: (l, 0, 0, f)), down_spec]
        sum_shapes = [jax.ShapeDtypeStruct(field.shape, BF16) for field in weights]
    if gated:
        out_specs = [pl.BlockSpec((count, 2, squeezed, part, width), lambda l, f: (0, 0, l, 0, 0))]
        out_shapes = [jax.ShapeDtypeStruct((count, 2, experts, part, width), BF16)]
        scratch = [pltpu.VMEM((total, width), BF16)] * 2 + [pltpu.VMEM((total, width), F32)] * 2
    else:
        out_specs = [pl.BlockSpec((count, squeezed, part, width), lambda l, f: (0, l, 0, 0))] * 2
        out_shapes = [jax.ShapeDtypeStruct((count, experts, part, width), F32)] * 2
        scratch = []
    inputs = len(operands)
    unread = ([carried] if carried is not None else []) + list(after)
    return pl.pallas_call(
        skipping(functools.partial(feed_kernel, gated, packed), inputs, len(unread)),
        grid=(experts, steps),
        in_specs=in_specs + [ANY] * len(unread),
        out_specs=out_specs + sum_specs,
        out_shape=out_shapes + sum_shapes,
        scratch_shapes=scratch,
        input_output_aliases={inputs: len(out_shapes)} if carried is not None else {},
        compiler_params=pltpu.CompilerParams(vmem_limit_bytes=VMEM_BYTES),
        cost_estimate=pl.CostEstimate(
            flops=18 * experts * total * width * units,
            bytes_accessed=experts * (12 * width * units + 8 * total * width),
            transcendentals=experts * total * units,
        ),
        name=name,
    )(*operands, *unread)


def on_device(
    tokens, cotangent, segments, routes, slots,
    norm1_gain, w_query, w_key, w_value, w_out, norm2_gain, w_router,
    shared_gate, shared_up, shared_down, expert_gate, expert_up, expert_down,
):
    length, width = tokens.shape[2], tokens.shape[3]
    batch = tokens.shape[0] * tokens.shape[1]
    devices = lax.axis_size("dp")
    owners = lax.axis_size("expert")
    local_experts = expert_gate.shape[0]
    experts = owners * local_experts
    hidden_units = shared_gate.shape[1]
    groups = 2
    size = local_experts // groups
    packed = (hidden_units == expert_gate.shape[2] and hidden_units % (devices * LANES) == 0
              and width % LANES == 0 and expert_gate.shape[1] % 16 == 0)
    pool = (expert_gate, expert_up, expert_down)

    pad = LANES - experts - 2
    first_part = jnp.concatenate(
        [w_query, w_key, w_value, w_out, w_router, norm1_gain[:, None], norm2_gain[:, None],
         jnp.zeros((w_query.shape[0], pad), BF16)], axis=1)
    first_all = lax.all_gather(first_part, "dp", axis=0, tiled=True)
    if packed:
        weights = [
            [lax.all_gather(
                pack(h * size, size, pool, (shared_gate, shared_up, shared_down) if h == 0 else (), devices), "dp", axis=0)]
            for h in range(groups)]
        shared_weights = weights[0]
    else:
        gather = lambda both, down: [
            lax.all_gather(both, "dp", axis=2, tiled=True), lax.all_gather(down, "dp", axis=1, tiled=True)]
        shared_weights = gather(jnp.stack([shared_gate, shared_up])[None], shared_down[None])
        weights = []
        for h in range(groups):
            part = slice(h * size, (h + 1) * size)
            weights.append(gather(jnp.stack([expert_gate[part], expert_up[part]], axis=1), expert_down[part]))
    gains = first_all[:, 4 * width + experts : 4 * width + experts + 2].astype(F32).T
    gain_one, gain_two = gains[0:1], gains[1:2]

    route_ids = routes.reshape(batch, length, 2)
    flat = (route_ids * CAP + slots.reshape(batch, length, 2)).transpose(0, 2, 1)

    def trade(field):
        return lax.all_to_all(field.reshape(owners, local_experts, batch * CAP, width), "expert", 0, 0)

    whole = lambda shape: pl.BlockSpec(shape, lambda b: (0,) * len(shape))
    each = lambda *shape: pl.BlockSpec((1,) + shape, lambda b: (b, 0, 0))
    piece_spec = pl.BlockSpec((experts, 1, CAP, width), lambda b: (0, b, 0, 0))
    piece_shape = jax.ShapeDtypeStruct((experts, batch, CAP, width), BF16)
    rows = experts * CAP
    params = pltpu.CompilerParams(vmem_limit_bytes=VMEM_BYTES)

    grad_low = cotangent.reshape(batch, length, width)
    grad_sent = pl.pallas_call(
        dispatch_kernel,
        grid=(batch,),
        in_specs=[each(2, length), each(length, width)],
        out_specs=piece_spec,
        out_shape=piece_shape,
        compiler_params=params,
        cost_estimate=pl.CostEstimate(
            flops=2 * batch * rows * length * width, bytes_accessed=4 * batch * rows * width, transcendentals=0),
        name="dispatch",
    )(flat, grad_low)
    grad_arrived = trade(grad_sent)

    token_rows = tokens.reshape(batch, length, width)
    segment_ids = segments.reshape(batch, length)
    half = HEAD_DIM // 2
    frequency = jnp.exp(-jnp.log(10000.0) * jnp.arange(half, dtype=F32) / half)
    angles = jnp.arange(length, dtype=F32)[:, None] * frequency[None, :]
    cosine = jnp.tile(jnp.cos(angles), (1, 4))
    sine = jnp.tile(jnp.concatenate([-jnp.sin(angles), jnp.sin(angles)], axis=1), (1, 2))
    columns = first_all.shape[1]
    position_args = (segment_ids[:, :, None], segment_ids[:, None, :], flat)
    position_specs = [each(length, 1), each(1, length), each(2, length)]
    weight_args = (first_all, gain_one, gain_two, cosine, sine)
    weight_specs = [
        whole((width, columns)), whole((1, width)), whole((1, width)), whole((length, LANES)), whole((length, LANES))]
    kept_shapes = [
        jax.ShapeDtypeStruct((batch, length, width), F32),
        jax.ShapeDtypeStruct((batch, length, width), BF16),
        jax.ShapeDtypeStruct((batch, length, width), BF16),
        jax.ShapeDtypeStruct((batch, length, 3 * width), BF16),
        jax.ShapeDtypeStruct((batch, length, LANES), F32),
        jax.ShapeDtypeStruct((batch, length, LANES), F32),
    ]
    kept_specs = [each(*shape.shape[1:]) for shape in kept_shapes]
    tokens_all = batch * length
    outs = pl.pallas_call(
        functools.partial(forward_kernel, experts),
        grid=(batch,),
        in_specs=[each(length, width)] + position_specs + weight_specs,
        out_specs=kept_specs + [piece_spec],
        out_shape=kept_shapes + [piece_shape],
        compiler_params=params,
        cost_estimate=pl.CostEstimate(
            flops=2 * tokens_all * width * (columns + 4 * length + rows),
            bytes_accessed=2 * width * columns + tokens_all * width * 20,
            transcendentals=tokens_all * length * width // HEAD_DIM,
        ),
        name="attention",
    )(token_rows, *position_args, *weight_args)
    kept, sent = outs[:6], outs[6]
    mixed_in, router = kept[1], kept[5]
    arrived = trade(sent)
    chosen = route_ids[..., None] == jnp.arange(experts, dtype=jnp.int32)
    gates = jnp.sum(jnp.where(chosen, router[:, :, None, :experts], 0.0), axis=-1).transpose(0, 2, 1)
    held = flat[:, :, None, :] == jnp.arange(rows, dtype=jnp.int32)[:, None]
    slot_gates = jnp.sum(jnp.where(held, gates[:, :, None, :], 0.0), axis=(1, 3))
    slot_gates = slot_gates.reshape(batch, owners, local_experts, CAP).transpose(1, 2, 0, 3)
    slot_gates = lax.all_to_all(slot_gates.reshape(owners, local_experts, 1, batch * CAP), "expert", 0, 0)

    shared_out, d_mixed, *shared_sums = feed(
        mixed_in.reshape(1, 1, tokens_all, width), grad_low.reshape(1, 1, tokens_all, width), None,
        shared_weights, 0, size if packed else 0, 1, "shared")

    backs, sums = [], []
    for h in range(groups):
        results, *grads = feed(
            arrived, grad_arrived, slot_gates, weights[h], h * size, 0, size, "experts",
            shared_sums[0] if packed and h == 0 else None, [shared_out if h == 0 else results])
        backs.append(lax.all_to_all(results, "expert", 0, 0).reshape(owners, 2, size, batch, CAP, width))
        sums.append(grads)

    layer_out, grad_tokens, first_grad = pl.pallas_call(
        functools.partial(backward_kernel, experts, groups),
        grid=(batch,),
        in_specs=[each(length, width)] * 2 + position_specs + [each(length, 2)] + weight_specs + kept_specs
        + [each(length, width)] * 2
        + [pl.BlockSpec((owners, 2, size, 1, CAP, width), lambda b: (0, 0, 0, b, 0, 0))] * groups,
        out_specs=[each(length, width)] * 2 + [whole((width, columns))],
        out_shape=[
            jax.ShapeDtypeStruct((batch, length, width), BF16),
            jax.ShapeDtypeStruct((batch, length, width), F32),
            jax.ShapeDtypeStruct((width, columns), BF16),
        ],
        scratch_shapes=[
            pltpu.VMEM((rows, width), F32),
            pltpu.VMEM((width, columns), F32),
            pltpu.VMEM((8, width), F32),
            pltpu.VMEM((length, 3 * width), BF16),
        ],
        compiler_params=params,
        cost_estimate=pl.CostEstimate(
            flops=4 * tokens_all * width * (columns + 4 * length + rows),
            bytes_accessed=4 * width * columns + tokens_all * width * 32,
            transcendentals=tokens_all * length * width // HEAD_DIM,
        ),
        name="attention_back",
    )(
        token_rows, grad_low, *position_args, route_ids, *weight_args, *kept,
        shared_out.reshape(batch, length, width), d_mixed.reshape(batch, length, width), *backs,
    )

    def over_owners(field):
        k = 1
        while k < owners:
            came = lax.ppermute(field, "expert", [(i, i ^ k) for i in range(owners)])
            field = field.astype(F32) + came.astype(F32)
            k *= 2
            field = field.astype(BF16) if k < owners else field
        return field

    units = hidden_units
    if packed:
        mine = []
        for field in sums:
            mine.append(lax.psum_scatter(tie(field[0], *mine[-1:]), "dp", scatter_dimension=0))
        first_grad = tie(first_grad, mine[-1])
        pool_mine = unpack(mine, [size] * groups, width // devices, units, "unpack_experts")
        shared_mine = unpack(
            [over_owners(mine[0][size:])], [1], width // devices, units, "unpack_shared")
        shared_mine = [field[0] for field in shared_mine]
    else:
        def scatter(both, down):
            return (lax.psum_scatter(both, "dp", scatter_dimension=2, tiled=True),
                    lax.psum_scatter(down, "dp", scatter_dimension=1, tiled=True))

        both, down = (jnp.concatenate(fields, axis=0).astype(F32) for fields in zip(*(scatter(*field) for field in sums)))
        pool_mine = [both[:, 0], both[:, 1], down]
        both, down = (over_owners(field[0]) for field in scatter(*shared_sums))
        shared_mine = [both[0], both[1], down]
    first_mine = over_owners(lax.psum_scatter(first_grad, "dp", scatter_dimension=0, tiled=True))
    return (
        layer_out.reshape(tokens.shape),
        grad_tokens.reshape(tokens.shape),
        first_mine[:, 4 * width + experts],
        first_mine[:, :width],
        first_mine[:, width : 2 * width],
        first_mine[:, 2 * width : 3 * width],
        first_mine[:, 3 * width : 4 * width],
        first_mine[:, 4 * width + experts + 1],
        first_mine[:, 4 * width : 4 * width + experts],
        *shared_mine,
        *pool_mine,
    )


def solution(mesh):
    token_spec = P(None, ("dp", "expert"), None, None)
    vector, matrix, pool = P("dp"), P("dp", None), P("expert", "dp", None)
    weights = (vector, matrix, matrix, matrix, matrix, vector, matrix, matrix, matrix, matrix, pool, pool, pool)
    return jax.shard_map(
        on_device,
        mesh=mesh,
        in_specs=(token_spec, token_spec, P(None, ("dp", "expert"), None), token_spec, token_spec) + weights,
        out_specs=(token_spec, token_spec) + weights,
        check_vma=False,
    )
```

```python
import functools

import jax
import jax.numpy as jnp
from jax import lax
from jax.experimental import pallas as pl
from jax.experimental.pallas import tpu as pltpu
from jax.sharding import PartitionSpec as P

HEAD_DIM = 64
PAIR = 2 * HEAD_DIM
CAP = 40
LANES = 128
EPSILON = 1e-06
F32 = jnp.float32
BF16 = jnp.bfloat16
NN = (((1,), (0,)), ((), ()))
NT = (((1,), (1,)), ((), ()))
TN = (((0,), (0,)), ((), ()))
VMEM_BYTES = 60 * 1024 * 1024
ANY = pl.BlockSpec(memory_space=pl.ANY)


def mm(left, right, dims):
    return lax.dot_general(left, right, dims, preferred_element_type=F32)


def iota(shape, axis):
    return lax.broadcasted_iota(jnp.int32, shape, axis)


def skipping(body, inputs, unread):
    return lambda *refs: body(*refs[:inputs], *refs[inputs + unread :])


def tie(field, *after):
    return pl.pallas_call(
        lambda *refs: None,
        out_shape=jax.ShapeDtypeStruct(field.shape, field.dtype),
        in_specs=[ANY] * (1 + len(after)),
        out_specs=ANY,
        input_output_aliases={0: 0},
        name="tie",
    )(field, *after)


def first_step(i):
    return i ^ (2 if i % 2 == 0 else 4)


def second_step(i):
    return i ^ (4 if i % 2 == 0 else 2)


def core_step(i):
    return i ^ 1


def send(field, step):
    return lax.ppermute(field, "dp", [(i, step(i)) for i in range(8)])


def scatter_rows(field):
    count = lax.axis_size("dp")
    if count != 8:
        return lax.psum_scatter(field, "dp", scatter_dimension=0, tiled=False)
    index = lax.axis_index("dp")
    core, x, y = index % 2, (index // 2) % 2, index // 4
    take = functools.partial(lax.dynamic_index_in_dim, keepdims=False)
    blocks = field.reshape((4, 2) + field.shape[1:])
    came = send(take(blocks, 1 - core, 1), core_step)
    total = (take(blocks, core, 1).astype(F32) + came.astype(F32)).astype(BF16)
    one, two = jnp.where(core == 0, x, y), jnp.where(core == 0, y, x)

    def at(first, second):
        return take(total, jnp.where(core == 0, second * 2 + first, first * 2 + second), 0)

    came = send(jnp.stack([at(1 - one, two), at(1 - one, 1 - two)]), first_step).astype(F32)
    keep = (at(one, two).astype(F32) + came[0]).astype(BF16)
    pass_on = (at(one, 1 - two).astype(F32) + came[1]).astype(BF16)
    return (keep.astype(F32) + send(pass_on, second_step).astype(F32)).astype(BF16)


def place_of(flat, rows):
    at = iota((rows, flat.shape[1]), 0)
    held = jnp.logical_or(flat[0:1, :] == at, flat[1:2, :] == at)
    return jnp.where(held, 1.0, 0.0).astype(BF16)


def put_rows(sent, out):
    for expert in range(out.shape[0]):
        out[expert, 0] = sent[expert * CAP : (expert + 1) * CAP].astype(BF16)


def dispatch_kernel(flat_ref, field_ref, out_ref):
    put_rows(mm(place_of(flat_ref[0], out_ref.shape[0] * CAP), field_ref[0], NN), out_ref)


def swap_halves(field):
    low = iota(field.shape, 1) % HEAD_DIM < HEAD_DIM // 2
    ahead = pltpu.roll(field, PAIR - HEAD_DIM // 2, 1)
    behind = pltpu.roll(field, HEAD_DIM // 2, 1)
    return jnp.where(low, ahead, behind)


def turn(field, cosine, sine):
    return field * cosine + swap_halves(field) * sine


def allowed_of(column_ref, row_ref):
    length = row_ref.shape[2]
    square = (length, length)
    return jnp.logical_and(iota(square, 0) >= iota(square, 1), column_ref[0] == row_ref[0])


def inverse_rms(field):
    return lax.rsqrt(jnp.mean(field * field, axis=-1, keepdims=True) + EPSILON)


def forward_kernel(
    experts, tokens_ref, column_ref, row_ref, flat_ref, weight_ref, gain_one_ref, gain_two_ref, cosine_ref, sine_ref,
    hidden_ref, mixed_ref, attended_ref, qkv_ref, logsum_ref, router_ref, sent_ref,
):
    width = tokens_ref.shape[2]
    x = tokens_ref[0].astype(F32)
    normed = (x * inverse_rms(x) * gain_one_ref[...]).astype(BF16)
    allowed = allowed_of(column_ref, row_ref)
    cosine, sine = cosine_ref[...], sine_ref[...]
    low = iota((x.shape[0], PAIR), 1) < HEAD_DIM
    lane = iota((x.shape[0], LANES), 1)
    logsum = jnp.zeros((x.shape[0], LANES), F32)
    for pair in range(width // PAIR):
        at = slice(pair * PAIR, (pair + 1) * PAIR)
        query = turn(mm(normed, weight_ref[:, at], NN), cosine, sine).astype(BF16) * BF16(0.125)
        key = turn(mm(normed, weight_ref[:, width + at.start : width + at.stop], NN), cosine, sine).astype(BF16)
        value = mm(normed, weight_ref[:, 2 * width + at.start : 2 * width + at.stop], NN).astype(BF16)
        qkv_ref[0, :, at] = query
        qkv_ref[0, :, width + at.start : width + at.stop] = key
        qkv_ref[0, :, 2 * width + at.start : 2 * width + at.stop] = value
        both = []
        for half in range(2):
            mine = low if half == 0 else jnp.logical_not(low)
            scores = jnp.where(allowed, mm(jnp.where(mine, query, BF16(0.0)), key, NT), -1e30)
            peak = jnp.max(scores, axis=-1, keepdims=True)
            expo = jnp.exp(scores - peak)
            total = jnp.sum(expo, axis=-1, keepdims=True)
            logsum = jnp.where(lane == 2 * pair + half, peak + jnp.log(total), logsum)
            both.append(mm((expo * (1.0 / total)).astype(BF16), value, NN))
        attended_ref[0, :, at] = jnp.where(low, both[0], both[1]).astype(BF16)
    logsum_ref[0] = logsum
    hidden = x + mm(attended_ref[0], weight_ref[:, 3 * width : 4 * width], NN)
    hidden_ref[0] = hidden
    mixed = (hidden * inverse_rms(hidden) * gain_two_ref[...]).astype(BF16)
    mixed_ref[0] = mixed
    logits = jnp.where(lane < experts, mm(mixed, weight_ref[:, 4 * width :], NN), -1e30)
    expo = jnp.exp(logits - jnp.max(logits, axis=-1, keepdims=True))
    router_ref[0] = expo / jnp.sum(expo, axis=-1, keepdims=True)
    put_rows(mm(place_of(flat_ref[0], experts * CAP), mixed, NN), sent_ref)


def get_rows(backs, which, experts, held_ref):
    owners, _, size = backs[0].shape[:3]
    for expert in range(experts):
        owner, local = expert // (len(backs) * size), expert % (len(backs) * size)
        held_ref[expert * CAP : (expert + 1) * CAP, :] = backs[local // size][owner, which, local % size, 0].astype(F32)
    return held_ref[...].astype(BF16)


def backward_kernel(
    experts, groups, tokens_ref, grad_ref, column_ref, row_ref, flat_ref, routes_ref, weight_ref, gain_one_ref, gain_two_ref,
    cosine_ref, sine_ref, hidden_ref, mixed_ref, attended_ref, qkv_ref, logsum_ref, router_ref, shared_ref, d_mixed_ref, *refs,
):
    backs = refs[:groups]
    out_ref, grad_tokens_ref, grad_weight_ref, held_ref, sum_ref, gains_ref, d_qkv_ref = refs[groups:]
    width = tokens_ref.shape[2]
    step = pl.program_id(0)

    @pl.when(step == 0)
    def _():
        sum_ref[...] = jnp.zeros_like(sum_ref)
        gains_ref[...] = jnp.zeros_like(gains_ref)

    length = tokens_ref.shape[1]
    lane = iota((length, LANES), 1)
    grad = grad_ref[0].astype(F32)
    hidden = hidden_ref[0]
    mixed = mixed_ref[0]
    router = router_ref[0]
    flat = flat_ref[0]
    rows = experts * CAP
    at_row = iota((rows, length), 0)
    came = get_rows(backs, 0, experts, held_ref)
    layer = hidden + shared_ref[0]
    d_router = jnp.zeros((length, LANES), F32)
    for choice in range(2):
        place = jnp.where(flat[choice : choice + 1, :] == at_row, 1.0, 0.0).astype(BF16)
        picked = mm(place, came, TN)
        chosen = lane == routes_ref[0, :, choice : choice + 1]
        gate = jnp.sum(jnp.where(chosen, router, 0.0), axis=-1, keepdims=True)
        layer = layer + gate * picked
        d_gate = jnp.sum(grad * picked, axis=-1, keepdims=True)
        d_router = d_router + jnp.where(chosen, d_gate, 0.0)
    out_ref[0] = layer.astype(BF16)
    d_logits = (router * (d_router - jnp.sum(router * d_router, axis=-1, keepdims=True))).astype(BF16)
    sum_ref[:, 4 * width :] += mm(mixed, d_logits, TN)
    came = get_rows(backs, 1, experts, held_ref)
    d_mixed = d_mixed_ref[0] + mm(place_of(flat, rows), came, TN) + mm(d_logits, weight_ref[:, 4 * width :], NT)

    inverse_two = inverse_rms(hidden)
    unit_two = hidden * inverse_two
    gains_ref[1:2, :] += jnp.sum(d_mixed * unit_two, axis=0, keepdims=True)
    scaled = d_mixed * gain_two_ref[...]
    d_hidden = grad + inverse_two * (scaled - unit_two * jnp.mean(scaled * unit_two, axis=-1, keepdims=True))
    d_branch = d_hidden.astype(BF16)
    sum_ref[:, 3 * width : 4 * width] += mm(attended_ref[0], d_branch, TN)
    d_attended = mm(d_branch, weight_ref[:, 3 * width : 4 * width], NT).astype(BF16)

    allowed = allowed_of(column_ref, row_ref)
    cosine, sine = cosine_ref[...], -sine_ref[...]
    low = iota((length, PAIR), 1) < HEAD_DIM
    logsum = logsum_ref[0]
    for pair in range(width // PAIR):
        at = slice(pair * PAIR, (pair + 1) * PAIR)
        query = qkv_ref[0, :, at]
        key = qkv_ref[0, :, width + at.start : width + at.stop]
        value = qkv_ref[0, :, 2 * width + at.start : 2 * width + at.stop]
        d_out = d_attended[:, at]
        parts = []
        for half in range(2):
            mine = low if half == 0 else jnp.logical_not(low)
            scores = jnp.where(allowed, mm(jnp.where(mine, query, BF16(0.0)), key, NT), -1e30)
            head = 2 * pair + half
            probs = jnp.exp(scores - logsum[:, head : head + 1])
            d_probs = mm(jnp.where(mine, d_out, BF16(0.0)), value, NT)
            d_scores = (probs * (d_probs - jnp.sum(probs * d_probs, axis=-1, keepdims=True))).astype(BF16)
            parts.append((mm(d_scores, key, NN), mm(d_scores, query, TN), mm(probs.astype(BF16), d_out, TN)))
        d_query, d_key, d_value = (jnp.where(low, a, b) for a, b in zip(*parts))
        d_qkv_ref[:, at] = turn(d_query * 0.125, cosine, sine).astype(BF16)
        d_qkv_ref[:, width + at.start : width + at.stop] = turn(d_key, cosine, sine).astype(BF16)
        d_qkv_ref[:, 2 * width + at.start : 2 * width + at.stop] = d_value.astype(BF16)

    x = tokens_ref[0].astype(F32)
    inverse_one = inverse_rms(x)
    unit_one = x * inverse_one
    normed = (unit_one * gain_one_ref[...]).astype(BF16)
    d_qkv = d_qkv_ref[...]
    sum_ref[:, : 3 * width] += mm(normed, d_qkv, TN)
    d_normed = mm(d_qkv, weight_ref[:, : 3 * width], NT)
    gains_ref[0:1, :] += jnp.sum(d_normed * unit_one, axis=0, keepdims=True)
    scaled = d_normed * gain_one_ref[...]
    grad_tokens_ref[0] = d_hidden + inverse_one * (
        scaled - unit_one * jnp.mean(scaled * unit_one, axis=-1, keepdims=True))

    @pl.when(step == pl.num_programs(0) - 1)
    def _():
        grad_weight_ref[:, : 4 * width] = sum_ref[:, : 4 * width].astype(BF16)
        gains = jnp.concatenate(
            [jnp.zeros((experts, width), F32), gains_ref[...], jnp.zeros((LANES - experts - 8, width), F32)], axis=0)
        grad_weight_ref[:, 4 * width :] = (sum_ref[:, 4 * width :] + gains.T).astype(BF16)


def pack_pieces(packed, gate, up, down):
    steps, width = packed.shape[1], packed.shape[2]
    rows = gate.shape[0]
    for f in range(steps):
        for j in range(width // rows):
            at = slice((j * steps + f) * LANES, (j * steps + f + 1) * LANES)
            yield packed.at[0, f, j * rows : (j + 1) * rows], gate.at[:, at]
            yield packed.at[1, f, j * rows : (j + 1) * rows], up.at[:, at]
        for c in range(width // LANES):
            at = slice(c * LANES, (c + 1) * LANES)
            yield packed.at[2, f, at], down.at[f * LANES : (f + 1) * LANES, at]


def pack_kernel(count, *refs):
    out = refs[-1]
    step = pl.program_id(0)
    for n in range((len(refs) - 1) // 3):
        @pl.when((step < count) if n == 0 else (step >= count))
        def _():
            for to, source in pack_pieces(out, *refs[3 * n : 3 * n + 3]):
                to[...] = source[...]


def pack(first, count, pool, shared, devices):
    rows, units = pool[0].shape[1:]
    width = rows * devices
    steps = units // (devices * LANES)
    squeezed = pl.Squeezed()
    take = lambda l: (first + jnp.minimum(l, count - 1), 0, 0)
    total = count + (1 if shared else 0)
    return pl.pallas_call(
        functools.partial(pack_kernel, count),
        grid=(total,),
        in_specs=[pl.BlockSpec((squeezed,) + field.shape[1:], take) for field in pool]
        + [pl.BlockSpec(field.shape, lambda l: (0, 0)) for field in shared],
        out_specs=pl.BlockSpec((squeezed, 3, steps, width, LANES), lambda l: (l, 0, 0, 0, 0)),
        out_shape=jax.ShapeDtypeStruct((total, 3, steps, width, LANES), BF16),
        name="pack",
    )(*pool, *shared)


def unpack_kernel(sizes, *refs):
    packs, outs = refs[: len(sizes)], refs[len(sizes) :]
    step = pl.program_id(0)
    start = 0
    for n, size in enumerate(sizes):
        @pl.when(jnp.logical_and(step >= start, step < start + size))
        def _(source=packs[n]):
            for piece, to in pack_pieces(source, *outs):
                to[...] = piece[...].astype(F32)
        start += size


def unpack(packs, sizes, rows, units, name):
    squeezed = pl.Squeezed()
    specs, start = [], 0
    for field, size in zip(packs, sizes):
        specs.append(pl.BlockSpec(
            (squeezed,) + field.shape[1:],
            lambda l, start=start, size=size: (jnp.clip(l - start, 0, size - 1), 0, 0, 0, 0)))
        start += size
    width = packs[0].shape[3]
    shapes = [(rows, units), (rows, units), (rows * units // width, width)]
    return pl.pallas_call(
        functools.partial(unpack_kernel, tuple(sizes)),
        grid=(start,),
        in_specs=specs,
        out_specs=[pl.BlockSpec((squeezed,) + shape, lambda l: (l, 0, 0)) for shape in shapes],
        out_shape=[jax.ShapeDtypeStruct((start,) + shape, F32) for shape in shapes],
        name=name,
    )(*packs)


def feed_step(x, d, gate_weight, up_weight, down_weight, out, dx):
    g = mm(x, gate_weight, NN)
    u = mm(x, up_weight, NN)
    sigma = 1.0 / (1.0 + jnp.exp(-g))
    active = g * sigma
    inner = (active * u).astype(BF16)
    out[...] += mm(inner, down_weight, NN)
    d_inner = mm(d, down_weight, NT)
    d_g = (d_inner * u * (sigma * (1.0 + g * (1.0 - sigma)))).astype(BF16)
    d_u = (d_inner * active).astype(BF16)
    dx[...] += mm(d_g, gate_weight, NT) + mm(d_u, up_weight, NT)
    return mm(x, d_g, TN).astype(BF16), mm(x, d_u, TN).astype(BF16), mm(inner, d, TN).astype(BF16)


def feed_kernel(gated, packed, rows_ref, grads_ref, *refs):
    if gated:
        gates_ref, refs = refs[0], refs[1:]
    count, part, width = rows_ref.shape
    weights = refs[: 1 if packed else 3]
    refs = refs[len(weights) :]
    if gated:
        back_ref, refs = refs[0], refs[1:]
        sums, (x_ref, d_ref, out_ref, dx_ref) = refs[:-4], refs[-4:]
    else:
        out_ref, dx_ref, sums = refs[0].at[0], refs[1].at[0], refs[2:]
    step = pl.program_id(1)

    @pl.when(step == 0)
    def _():
        out_ref[...] = jnp.zeros_like(out_ref)
        dx_ref[...] = jnp.zeros_like(dx_ref)
        if gated:
            square = (part, part)
            for k in range(count):
                at = slice(k * part, (k + 1) * part)
                x_ref[at, :] = rows_ref[k]
                line = jnp.broadcast_to(gates_ref[k], square)
                column = jnp.sum(jnp.where(iota(square, 0) == iota(square, 1), line, 0.0), axis=1, keepdims=True)
                d_ref[at, :] = (grads_ref[k].astype(F32) * column).astype(BF16)

    x, d = (x_ref[...], d_ref[...]) if gated else (rows_ref[0], grads_ref[0])
    if packed:
        field, total = weights[0], sums[0]
        devices = field.shape[0]
        rows = width // devices
        size = min(devices, 4)
        for start in range(0, devices, size):
            columns = range(start, start + size)
            side = lambda n: jnp.concatenate(
                [field[:, n, j * rows : (j + 1) * rows, :].reshape(width, LANES) for j in columns], axis=1)
            down = jnp.concatenate(
                [field[start : start + size, 2, c * LANES : (c + 1) * LANES, :].reshape(size * LANES, LANES)
                 for c in range(width // LANES)], axis=1)
            gate_sum, up_sum, down_sum = feed_step(x, d, side(0), side(1), down, out_ref, dx_ref)
            for n, value in enumerate((gate_sum, up_sum)):
                for j in columns:
                    total[:, n, j * rows : (j + 1) * rows, :] = value[
                        :, (j - start) * LANES : (j - start + 1) * LANES].reshape(devices, rows, LANES)
            for c in range(width // LANES):
                at = slice(c * LANES, (c + 1) * LANES)
                total[start : start + size, 2, at, :] = down_sum[:, at].reshape(size, LANES, LANES)
    else:
        sums[0][0], sums[0][1], sums[1][...] = feed_step(x, d, *(ref[...] for ref in weights), out_ref, dx_ref)

    if gated:
        @pl.when(step == pl.num_programs(1) - 1)
        def _():
            for k in range(count):
                at = slice(k * part, (k + 1) * part)
                back_ref[k, 0] = out_ref[at, :].astype(BF16)
                back_ref[k, 1] = dx_ref[at, :].astype(BF16)


def feed(rows, grads, gates, weights, first_row, first_weight, experts, name, carried=None, after=()):
    count, _, part, width = rows.shape
    squeezed = pl.Squeezed()
    gated, packed = gates is not None, len(weights) == 1
    total = count * part
    row = lambda l, f: (0, first_row + l, 0, 0)
    operands = [rows, grads] + ([gates] if gated else [])
    in_specs = [pl.BlockSpec((count, squeezed, part, width), row)] * 2
    in_specs += [pl.BlockSpec((count, squeezed, 1, part), row)] * gated
    if packed:
        devices, _, _, steps = weights[0].shape[:4]
        units = steps * devices * LANES
        pack_spec = pl.BlockSpec(
            (devices, squeezed, 3, squeezed, width, LANES), lambda l, f: (0, first_weight + l, 0, f, 0, 0))
        operands += weights
        in_specs += [pack_spec]
        sum_specs, sum_shapes = [pack_spec], [jax.ShapeDtypeStruct(weights[0].shape, BF16)]
    else:
        units, block = weights[1].shape[1], 512
        steps = units // block
        side = lambda n: pl.BlockSpec((squeezed, squeezed, width, block), lambda l, f: (l, n, 0, f))
        down_spec = pl.BlockSpec((squeezed, block, width), lambda l, f: (l, f, 0))
        operands += [weights[0], weights[0], weights[1]]
        in_specs += [side(0), side(1), down_spec]
        sum_specs = [pl.BlockSpec((squeezed, 2, width, block), lambda l, f: (l, 0, 0, f)), down_spec]
        sum_shapes = [jax.ShapeDtypeStruct(field.shape, BF16) for field in weights]
    if gated:
        out_specs = [pl.BlockSpec((count, 2, squeezed, part, width), lambda l, f: (0, 0, l, 0, 0))]
        out_shapes = [jax.ShapeDtypeStruct((count, 2, experts, part, width), BF16)]
        scratch = [pltpu.VMEM((total, width), BF16)] * 2 + [pltpu.VMEM((total, width), F32)] * 2
    else:
        out_specs = [pl.BlockSpec((count, squeezed, part, width), lambda l, f: (0, l, 0, 0))] * 2
        out_shapes = [jax.ShapeDtypeStruct((count, experts, part, width), F32)] * 2
        scratch = []
    inputs = len(operands)
    unread = ([carried] if carried is not None else []) + list(after)
    return pl.pallas_call(
        skipping(functools.partial(feed_kernel, gated, packed), inputs, len(unread)),
        grid=(experts, steps),
        in_specs=in_specs + [ANY] * len(unread),
        out_specs=out_specs + sum_specs,
        out_shape=out_shapes + sum_shapes,
        scratch_shapes=scratch,
        input_output_aliases={inputs: len(out_shapes)} if carried is not None else {},
        compiler_params=pltpu.CompilerParams(vmem_limit_bytes=VMEM_BYTES),
        cost_estimate=pl.CostEstimate(
            flops=18 * experts * total * width * units,
            bytes_accessed=experts * (12 * width * units + 8 * total * width),
            transcendentals=experts * total * units,
        ),
        name=name,
    )(*operands, *unread)


def on_device(
    tokens, cotangent, segments, routes, slots,
    norm1_gain, w_query, w_key, w_value, w_out, norm2_gain, w_router,
    shared_gate, shared_up, shared_down, expert_gate, expert_up, expert_down,
):
    length, width = tokens.shape[2], tokens.shape[3]
    batch = tokens.shape[0] * tokens.shape[1]
    devices = lax.axis_size("dp")
    owners = lax.axis_size("expert")
    local_experts = expert_gate.shape[0]
    experts = owners * local_experts
    hidden_units = shared_gate.shape[1]
    groups = 2
    size = local_experts // groups
    packed = (hidden_units == expert_gate.shape[2] and hidden_units % (devices * LANES) == 0
              and width % LANES == 0 and expert_gate.shape[1] % 16 == 0)
    pool = (expert_gate, expert_up, expert_down)

    pad = LANES - experts - 2
    first_part = jnp.concatenate(
        [w_query, w_key, w_value, w_out, w_router, norm1_gain[:, None], norm2_gain[:, None],
         jnp.zeros((w_query.shape[0], pad), BF16)], axis=1)
    first_all = lax.all_gather(first_part, "dp", axis=0, tiled=True)
    if packed:
        weights = [
            [lax.all_gather(
                pack(h * size, size, pool, (shared_gate, shared_up, shared_down) if h == 0 else (), devices), "dp", axis=0)]
            for h in range(groups)]
        shared_weights = weights[0]
    else:
        gather = lambda both, down: [
            lax.all_gather(both, "dp", axis=2, tiled=True), lax.all_gather(down, "dp", axis=1, tiled=True)]
        shared_weights = gather(jnp.stack([shared_gate, shared_up])[None], shared_down[None])
        weights = []
        for h in range(groups):
            part = slice(h * size, (h + 1) * size)
            weights.append(gather(jnp.stack([expert_gate[part], expert_up[part]], axis=1), expert_down[part]))
    gains = first_all[:, 4 * width + experts : 4 * width + experts + 2].astype(F32).T
    gain_one, gain_two = gains[0:1], gains[1:2]

    route_ids = routes.reshape(batch, length, 2)
    flat = (route_ids * CAP + slots.reshape(batch, length, 2)).transpose(0, 2, 1)

    def trade(field):
        return lax.all_to_all(field.reshape(owners, local_experts, batch * CAP, width), "expert", 0, 0)

    whole = lambda shape: pl.BlockSpec(shape, lambda b: (0,) * len(shape))
    each = lambda *shape: pl.BlockSpec((1,) + shape, lambda b: (b, 0, 0))
    piece_spec = pl.BlockSpec((experts, 1, CAP, width), lambda b: (0, b, 0, 0))
    piece_shape = jax.ShapeDtypeStruct((experts, batch, CAP, width), BF16)
    rows = experts * CAP
    params = pltpu.CompilerParams(vmem_limit_bytes=VMEM_BYTES)

    grad_low = cotangent.reshape(batch, length, width)
    grad_sent = pl.pallas_call(
        dispatch_kernel,
        grid=(batch,),
        in_specs=[each(2, length), each(length, width)],
        out_specs=piece_spec,
        out_shape=piece_shape,
        compiler_params=params,
        cost_estimate=pl.CostEstimate(
            flops=2 * batch * rows * length * width, bytes_accessed=4 * batch * rows * width, transcendentals=0),
        name="dispatch",
    )(flat, grad_low)
    grad_arrived = trade(grad_sent)

    token_rows = tokens.reshape(batch, length, width)
    segment_ids = segments.reshape(batch, length)
    half = HEAD_DIM // 2
    frequency = jnp.exp(-jnp.log(10000.0) * jnp.arange(half, dtype=F32) / half)
    angles = jnp.arange(length, dtype=F32)[:, None] * frequency[None, :]
    cosine = jnp.tile(jnp.cos(angles), (1, 4))
    sine = jnp.tile(jnp.concatenate([-jnp.sin(angles), jnp.sin(angles)], axis=1), (1, 2))
    columns = first_all.shape[1]
    position_args = (segment_ids[:, :, None], segment_ids[:, None, :], flat)
    position_specs = [each(length, 1), each(1, length), each(2, length)]
    weight_args = (first_all, gain_one, gain_two, cosine, sine)
    weight_specs = [
        whole((width, columns)), whole((1, width)), whole((1, width)), whole((length, LANES)), whole((length, LANES))]
    kept_shapes = [
        jax.ShapeDtypeStruct((batch, length, width), F32),
        jax.ShapeDtypeStruct((batch, length, width), BF16),
        jax.ShapeDtypeStruct((batch, length, width), BF16),
        jax.ShapeDtypeStruct((batch, length, 3 * width), BF16),
        jax.ShapeDtypeStruct((batch, length, LANES), F32),
        jax.ShapeDtypeStruct((batch, length, LANES), F32),
    ]
    kept_specs = [each(*shape.shape[1:]) for shape in kept_shapes]
    tokens_all = batch * length
    outs = pl.pallas_call(
        functools.partial(forward_kernel, experts),
        grid=(batch,),
        in_specs=[each(length, width)] + position_specs + weight_specs,
        out_specs=kept_specs + [piece_spec],
        out_shape=kept_shapes + [piece_shape],
        compiler_params=params,
        cost_estimate=pl.CostEstimate(
            flops=2 * tokens_all * width * (columns + 4 * length + rows),
            bytes_accessed=2 * width * columns + tokens_all * width * 20,
            transcendentals=tokens_all * length * width // HEAD_DIM,
        ),
        name="attention",
    )(token_rows, *position_args, *weight_args)
    kept, sent = outs[:6], outs[6]
    mixed_in, router = kept[1], kept[5]
    arrived = trade(sent)
    chosen = route_ids[..., None] == jnp.arange(experts, dtype=jnp.int32)
    gates = jnp.sum(jnp.where(chosen, router[:, :, None, :experts], 0.0), axis=-1).transpose(0, 2, 1)
    held = flat[:, :, None, :] == jnp.arange(rows, dtype=jnp.int32)[:, None]
    slot_gates = jnp.sum(jnp.where(held, gates[:, :, None, :], 0.0), axis=(1, 3))
    slot_gates = slot_gates.reshape(batch, owners, local_experts, CAP).transpose(1, 2, 0, 3)
    slot_gates = lax.all_to_all(slot_gates.reshape(owners, local_experts, 1, batch * CAP), "expert", 0, 0)

    shared_out, d_mixed, *shared_sums = feed(
        mixed_in.reshape(1, 1, tokens_all, width), grad_low.reshape(1, 1, tokens_all, width), None,
        shared_weights, 0, size if packed else 0, 1, "shared")

    backs, sums = [], []
    for h in range(groups):
        results, *grads = feed(
            arrived, grad_arrived, slot_gates, weights[h], h * size, 0, size, "experts",
            shared_sums[0] if packed and h == 0 else None, [shared_out if h == 0 else results])
        backs.append(lax.all_to_all(results, "expert", 0, 0).reshape(owners, 2, size, batch, CAP, width))
        sums.append(grads)

    layer_out, grad_tokens, first_grad = pl.pallas_call(
        functools.partial(backward_kernel, experts, groups),
        grid=(batch,),
        in_specs=[each(length, width)] * 2 + position_specs + [each(length, 2)] + weight_specs + kept_specs
        + [each(length, width)] * 2
        + [pl.BlockSpec((owners, 2, size, 1, CAP, width), lambda b: (0, 0, 0, b, 0, 0))] * groups,
        out_specs=[each(length, width)] * 2 + [whole((width, columns))],
        out_shape=[
            jax.ShapeDtypeStruct((batch, length, width), BF16),
            jax.ShapeDtypeStruct((batch, length, width), F32),
            jax.ShapeDtypeStruct((width, columns), BF16),
        ],
        scratch_shapes=[
            pltpu.VMEM((rows, width), F32),
            pltpu.VMEM((width, columns), F32),
            pltpu.VMEM((8, width), F32),
            pltpu.VMEM((length, 3 * width), BF16),
        ],
        compiler_params=params,
        cost_estimate=pl.CostEstimate(
            flops=4 * tokens_all * width * (columns + 4 * length + rows),
            bytes_accessed=4 * width * columns + tokens_all * width * 32,
            transcendentals=tokens_all * length * width // HEAD_DIM,
        ),
        name="attention_back",
    )(
        token_rows, grad_low, *position_args, route_ids, *weight_args, *kept,
        shared_out.reshape(batch, length, width), d_mixed.reshape(batch, length, width), *backs,
    )

    def over_owners(field):
        k = 1
        while k < owners:
            came = lax.ppermute(field, "expert", [(i, i ^ k) for i in range(owners)])
            field = field.astype(F32) + came.astype(F32)
            k *= 2
            field = field.astype(BF16) if k < owners else field
        return field

    units = hidden_units
    if packed:
        mine = []
        for field in sums:
            field = tie(field[0], *mine, *backs) if mine else field[0]
            mine.append(lax.psum_scatter(field, "dp", scatter_dimension=0))
        pool_mine = unpack(mine, [size] * groups, width // devices, units, "unpack_experts")
        shared_mine = unpack(
            [over_owners(mine[0][size:])], [1], width // devices, units, "unpack_shared")
        first_grad = tie(first_grad, shared_mine[0])
        shared_mine = [field[0] for field in shared_mine]
    else:
        def scatter(both, down):
            return (lax.psum_scatter(both, "dp", scatter_dimension=2, tiled=True),
                    lax.psum_scatter(down, "dp", scatter_dimension=1, tiled=True))

        both, down = (jnp.concatenate(fields, axis=0).astype(F32) for fields in zip(*(scatter(*field) for field in sums)))
        pool_mine = [both[:, 0], both[:, 1], down]
        both, down = (over_owners(field[0]) for field in scatter(*shared_sums))
        shared_mine = [both[0], both[1], down]
    first_mine = over_owners(scatter_rows(first_grad.reshape(devices, width // devices, columns)))
    return (
        layer_out.reshape(tokens.shape),
        grad_tokens.reshape(tokens.shape),
        first_mine[:, 4 * width + experts],
        first_mine[:, :width],
        first_mine[:, width : 2 * width],
        first_mine[:, 2 * width : 3 * width],
        first_mine[:, 3 * width : 4 * width],
        first_mine[:, 4 * width + experts + 1],
        first_mine[:, 4 * width : 4 * width + experts],
        *shared_mine,
        *pool_mine,
    )


def solution(mesh):
    token_spec = P(None, ("dp", "expert"), None, None)
    vector, matrix, pool = P("dp"), P("dp", None), P("expert", "dp", None)
    weights = (vector, matrix, matrix, matrix, matrix, vector, matrix, matrix, matrix, matrix, pool, pool, pool)
    return jax.shard_map(
        on_device,
        mesh=mesh,
        in_specs=(token_spec, token_spec, P(None, ("dp", "expert"), None), token_spec, token_spec) + weights,
        out_specs=(token_spec, token_spec) + weights,
        check_vma=False,
    )
```

```python
import functools

import jax
import jax.numpy as jnp
from jax import lax
from jax.experimental import pallas as pl
from jax.experimental.pallas import tpu as pltpu
from jax.sharding import PartitionSpec as P

HEAD_DIM = 64
PAIR = 2 * HEAD_DIM
CAP = 40
LANES = 128
EPSILON = 1e-06
F32 = jnp.float32
BF16 = jnp.bfloat16
NN = (((1,), (0,)), ((), ()))
NT = (((1,), (1,)), ((), ()))
TN = (((0,), (0,)), ((), ()))
VMEM_BYTES = 60 * 1024 * 1024
ANY = pl.BlockSpec(memory_space=pl.ANY)


def mm(left, right, dims):
    return lax.dot_general(left, right, dims, preferred_element_type=F32)


def iota(shape, axis):
    return lax.broadcasted_iota(jnp.int32, shape, axis)


def skipping(body, inputs, unread):
    return lambda *refs: body(*refs[:inputs], *refs[inputs + unread :])


def tie(field, *after):
    return pl.pallas_call(
        lambda *refs: None,
        out_shape=jax.ShapeDtypeStruct(field.shape, field.dtype),
        in_specs=[ANY] * (1 + len(after)),
        out_specs=ANY,
        input_output_aliases={0: 0},
        name="tie",
    )(field, *after)


def first_step(i):
    return i ^ (2 if i % 2 == 0 else 4)


def second_step(i):
    return i ^ (4 if i % 2 == 0 else 2)


def core_step(i):
    return i ^ 1


def send(field, step):
    return lax.ppermute(field, "dp", [(i, step(i)) for i in range(8)])


def scatter_rows(field):
    count = lax.axis_size("dp")
    if count != 8:
        return lax.psum_scatter(field, "dp", scatter_dimension=0, tiled=False)
    index = lax.axis_index("dp")
    core, x, y = index % 2, (index // 2) % 2, index // 4
    take = functools.partial(lax.dynamic_index_in_dim, keepdims=False)
    blocks = field.reshape((4, 2) + field.shape[1:])
    came = send(take(blocks, 1 - core, 1), core_step)
    total = (take(blocks, core, 1).astype(F32) + came.astype(F32)).astype(BF16)
    one, two = jnp.where(core == 0, x, y), jnp.where(core == 0, y, x)

    def at(first, second):
        return take(total, jnp.where(core == 0, second * 2 + first, first * 2 + second), 0)

    came = send(jnp.stack([at(1 - one, two), at(1 - one, 1 - two)]), first_step).astype(F32)
    keep = (at(one, two).astype(F32) + came[0]).astype(BF16)
    pass_on = (at(one, 1 - two).astype(F32) + came[1]).astype(BF16)
    return (keep.astype(F32) + send(pass_on, second_step).astype(F32)).astype(BF16)


def place_of(flat, rows):
    at = iota((rows, flat.shape[1]), 0)
    held = jnp.logical_or(flat[0:1, :] == at, flat[1:2, :] == at)
    return jnp.where(held, 1.0, 0.0).astype(BF16)


def put_rows(sent, outs):
    owners, size = outs[0].shape[:2]
    local = len(outs) * size
    for expert in range(owners * local):
        rows = sent[expert * CAP : (expert + 1) * CAP].astype(BF16)
        outs[expert % local // size][expert // local, expert % size, 0] = rows


def dispatch_kernel(experts, flat_ref, field_ref, *outs):
    put_rows(mm(place_of(flat_ref[0], experts * CAP), field_ref[0], NN), outs)


def swap_halves(field):
    low = iota(field.shape, 1) % HEAD_DIM < HEAD_DIM // 2
    ahead = pltpu.roll(field, PAIR - HEAD_DIM // 2, 1)
    behind = pltpu.roll(field, HEAD_DIM // 2, 1)
    return jnp.where(low, ahead, behind)


def turn(field, cosine, sine):
    return field * cosine + swap_halves(field) * sine


def allowed_of(column_ref, row_ref):
    length = row_ref.shape[2]
    square = (length, length)
    return jnp.logical_and(iota(square, 0) >= iota(square, 1), column_ref[0] == row_ref[0])


def inverse_rms(field):
    return lax.rsqrt(jnp.mean(field * field, axis=-1, keepdims=True) + EPSILON)


def forward_kernel(
    experts, tokens_ref, column_ref, row_ref, flat_ref, weight_ref, gain_one_ref, gain_two_ref, cosine_ref, sine_ref,
    hidden_ref, mixed_ref, attended_ref, qkv_ref, logsum_ref, router_ref, *outs,
):
    width = tokens_ref.shape[2]
    x = tokens_ref[0].astype(F32)
    normed = (x * inverse_rms(x) * gain_one_ref[...]).astype(BF16)
    allowed = allowed_of(column_ref, row_ref)
    cosine, sine = cosine_ref[...], sine_ref[...]
    low = iota((x.shape[0], PAIR), 1) < HEAD_DIM
    lane = iota((x.shape[0], LANES), 1)
    logsum = jnp.zeros((x.shape[0], LANES), F32)
    for pair in range(width // PAIR):
        at = slice(pair * PAIR, (pair + 1) * PAIR)
        query = turn(mm(normed, weight_ref[:, at], NN), cosine, sine).astype(BF16) * BF16(0.125)
        key = turn(mm(normed, weight_ref[:, width + at.start : width + at.stop], NN), cosine, sine).astype(BF16)
        value = mm(normed, weight_ref[:, 2 * width + at.start : 2 * width + at.stop], NN).astype(BF16)
        qkv_ref[0, :, at] = query
        qkv_ref[0, :, width + at.start : width + at.stop] = key
        qkv_ref[0, :, 2 * width + at.start : 2 * width + at.stop] = value
        both = []
        for half in range(2):
            mine = low if half == 0 else jnp.logical_not(low)
            scores = jnp.where(allowed, mm(jnp.where(mine, query, BF16(0.0)), key, NT), -1e30)
            peak = jnp.max(scores, axis=-1, keepdims=True)
            expo = jnp.exp(scores - peak)
            total = jnp.sum(expo, axis=-1, keepdims=True)
            logsum = jnp.where(lane == 2 * pair + half, peak + jnp.log(total), logsum)
            both.append(mm((expo * (1.0 / total)).astype(BF16), value, NN))
        attended_ref[0, :, at] = jnp.where(low, both[0], both[1]).astype(BF16)
    logsum_ref[0] = logsum
    hidden = x + mm(attended_ref[0], weight_ref[:, 3 * width : 4 * width], NN)
    hidden_ref[0] = hidden
    mixed = (hidden * inverse_rms(hidden) * gain_two_ref[...]).astype(BF16)
    mixed_ref[0] = mixed
    logits = jnp.where(lane < experts, mm(mixed, weight_ref[:, 4 * width :], NN), -1e30)
    expo = jnp.exp(logits - jnp.max(logits, axis=-1, keepdims=True))
    router_ref[0] = expo / jnp.sum(expo, axis=-1, keepdims=True)
    put_rows(mm(place_of(flat_ref[0], experts * CAP), mixed, NN), outs)


def get_rows(backs, which, experts, held_ref):
    owners, _, size = backs[0].shape[:3]
    for expert in range(experts):
        owner, local = expert // (len(backs) * size), expert % (len(backs) * size)
        held_ref[expert * CAP : (expert + 1) * CAP, :] = backs[local // size][owner, which, local % size, 0].astype(F32)
    return held_ref[...].astype(BF16)


def backward_kernel(
    experts, groups, tokens_ref, grad_ref, column_ref, row_ref, flat_ref, routes_ref, weight_ref, gain_one_ref, gain_two_ref,
    cosine_ref, sine_ref, hidden_ref, mixed_ref, attended_ref, qkv_ref, logsum_ref, router_ref, shared_ref, d_mixed_ref, *refs,
):
    backs = refs[:groups]
    out_ref, grad_tokens_ref, grad_weight_ref, held_ref, sum_ref, gains_ref, d_qkv_ref = refs[groups:]
    width = tokens_ref.shape[2]
    step = pl.program_id(0)

    @pl.when(step == 0)
    def _():
        sum_ref[...] = jnp.zeros_like(sum_ref)
        gains_ref[...] = jnp.zeros_like(gains_ref)

    length = tokens_ref.shape[1]
    lane = iota((length, LANES), 1)
    grad = grad_ref[0].astype(F32)
    hidden = hidden_ref[0]
    mixed = mixed_ref[0]
    router = router_ref[0]
    flat = flat_ref[0]
    rows = experts * CAP
    at_row = iota((rows, length), 0)
    came = get_rows(backs, 0, experts, held_ref)
    layer = hidden + shared_ref[0]
    d_router = jnp.zeros((length, LANES), F32)
    for choice in range(2):
        place = jnp.where(flat[choice : choice + 1, :] == at_row, 1.0, 0.0).astype(BF16)
        picked = mm(place, came, TN)
        chosen = lane == routes_ref[0, :, choice : choice + 1]
        gate = jnp.sum(jnp.where(chosen, router, 0.0), axis=-1, keepdims=True)
        layer = layer + gate * picked
        d_gate = jnp.sum(grad * picked, axis=-1, keepdims=True)
        d_router = d_router + jnp.where(chosen, d_gate, 0.0)
    out_ref[0] = layer.astype(BF16)
    d_logits = (router * (d_router - jnp.sum(router * d_router, axis=-1, keepdims=True))).astype(BF16)
    sum_ref[:, 4 * width :] += mm(mixed, d_logits, TN)
    came = get_rows(backs, 1, experts, held_ref)
    d_mixed = d_mixed_ref[0] + mm(place_of(flat, rows), came, TN) + mm(d_logits, weight_ref[:, 4 * width :], NT)

    inverse_two = inverse_rms(hidden)
    unit_two = hidden * inverse_two
    gains_ref[1:2, :] += jnp.sum(d_mixed * unit_two, axis=0, keepdims=True)
    scaled = d_mixed * gain_two_ref[...]
    d_hidden = grad + inverse_two * (scaled - unit_two * jnp.mean(scaled * unit_two, axis=-1, keepdims=True))
    d_branch = d_hidden.astype(BF16)
    sum_ref[:, 3 * width : 4 * width] += mm(attended_ref[0], d_branch, TN)
    d_attended = mm(d_branch, weight_ref[:, 3 * width : 4 * width], NT).astype(BF16)

    allowed = allowed_of(column_ref, row_ref)
    cosine, sine = cosine_ref[...], -sine_ref[...]
    low = iota((length, PAIR), 1) < HEAD_DIM
    logsum = logsum_ref[0]
    for pair in range(width // PAIR):
        at = slice(pair * PAIR, (pair + 1) * PAIR)
        query = qkv_ref[0, :, at]
        key = qkv_ref[0, :, width + at.start : width + at.stop]
        value = qkv_ref[0, :, 2 * width + at.start : 2 * width + at.stop]
        d_out = d_attended[:, at]
        parts = []
        for half in range(2):
            mine = low if half == 0 else jnp.logical_not(low)
            scores = jnp.where(allowed, mm(jnp.where(mine, query, BF16(0.0)), key, NT), -1e30)
            head = 2 * pair + half
            probs = jnp.exp(scores - logsum[:, head : head + 1])
            d_probs = mm(jnp.where(mine, d_out, BF16(0.0)), value, NT)
            d_scores = (probs * (d_probs - jnp.sum(probs * d_probs, axis=-1, keepdims=True))).astype(BF16)
            parts.append((mm(d_scores, key, NN), mm(d_scores, query, TN), mm(probs.astype(BF16), d_out, TN)))
        d_query, d_key, d_value = (jnp.where(low, a, b) for a, b in zip(*parts))
        d_qkv_ref[:, at] = turn(d_query * 0.125, cosine, sine).astype(BF16)
        d_qkv_ref[:, width + at.start : width + at.stop] = turn(d_key, cosine, sine).astype(BF16)
        d_qkv_ref[:, 2 * width + at.start : 2 * width + at.stop] = d_value.astype(BF16)

    x = tokens_ref[0].astype(F32)
    inverse_one = inverse_rms(x)
    unit_one = x * inverse_one
    normed = (unit_one * gain_one_ref[...]).astype(BF16)
    d_qkv = d_qkv_ref[...]
    sum_ref[:, : 3 * width] += mm(normed, d_qkv, TN)
    d_normed = mm(d_qkv, weight_ref[:, : 3 * width], NT)
    gains_ref[0:1, :] += jnp.sum(d_normed * unit_one, axis=0, keepdims=True)
    scaled = d_normed * gain_one_ref[...]
    grad_tokens_ref[0] = d_hidden + inverse_one * (
        scaled - unit_one * jnp.mean(scaled * unit_one, axis=-1, keepdims=True))

    @pl.when(step == pl.num_programs(0) - 1)
    def _():
        grad_weight_ref[:, : 4 * width] = sum_ref[:, : 4 * width].astype(BF16)
        gains = jnp.concatenate(
            [jnp.zeros((experts, width), F32), gains_ref[...], jnp.zeros((LANES - experts - 8, width), F32)], axis=0)
        grad_weight_ref[:, 4 * width :] = (sum_ref[:, 4 * width :] + gains.T).astype(BF16)


def pack_pieces(packed, gate, up, down):
    steps, width = packed.shape[1], packed.shape[2]
    rows = gate.shape[0]
    for f in range(steps):
        for j in range(width // rows):
            at = slice((j * steps + f) * LANES, (j * steps + f + 1) * LANES)
            yield packed.at[0, f, j * rows : (j + 1) * rows], gate.at[:, at]
            yield packed.at[1, f, j * rows : (j + 1) * rows], up.at[:, at]
        for c in range(width // LANES):
            at = slice(c * LANES, (c + 1) * LANES)
            yield packed.at[2, f, at], down.at[f * LANES : (f + 1) * LANES, at]


def pack_kernel(count, *refs):
    out = refs[-1]
    step = pl.program_id(0)
    for n in range((len(refs) - 1) // 3):
        @pl.when((step < count) if n == 0 else (step >= count))
        def _():
            for to, source in pack_pieces(out, *refs[3 * n : 3 * n + 3]):
                to[...] = source[...]


def pack(first, count, pool, shared, devices):
    rows, units = pool[0].shape[1:]
    width = rows * devices
    steps = units // (devices * LANES)
    squeezed = pl.Squeezed()
    take = lambda l: (first + jnp.minimum(l, count - 1), 0, 0)
    total = count + (1 if shared else 0)
    return pl.pallas_call(
        functools.partial(pack_kernel, count),
        grid=(total,),
        in_specs=[pl.BlockSpec((squeezed,) + field.shape[1:], take) for field in pool]
        + [pl.BlockSpec(field.shape, lambda l: (0, 0)) for field in shared],
        out_specs=pl.BlockSpec((squeezed, 3, steps, width, LANES), lambda l: (l, 0, 0, 0, 0)),
        out_shape=jax.ShapeDtypeStruct((total, 3, steps, width, LANES), BF16),
        name="pack",
    )(*pool, *shared)


def unpack_kernel(sizes, *refs):
    packs, outs = refs[: len(sizes)], refs[len(sizes) :]
    step = pl.program_id(0)
    start = 0
    for n, size in enumerate(sizes):
        @pl.when(jnp.logical_and(step >= start, step < start + size))
        def _(source=packs[n]):
            for piece, to in pack_pieces(source, *outs):
                to[...] = piece[...].astype(F32)
        start += size


def unpack(packs, sizes, rows, units, name):
    squeezed = pl.Squeezed()
    specs, start = [], 0
    for field, size in zip(packs, sizes):
        specs.append(pl.BlockSpec(
            (squeezed,) + field.shape[1:],
            lambda l, start=start, size=size: (jnp.clip(l - start, 0, size - 1), 0, 0, 0, 0)))
        start += size
    width = packs[0].shape[3]
    shapes = [(rows, units), (rows, units), (rows * units // width, width)]
    return pl.pallas_call(
        functools.partial(unpack_kernel, tuple(sizes)),
        grid=(start,),
        in_specs=specs,
        out_specs=[pl.BlockSpec((squeezed,) + shape, lambda l: (l, 0, 0)) for shape in shapes],
        out_shape=[jax.ShapeDtypeStruct((start,) + shape, F32) for shape in shapes],
        name=name,
    )(*packs)


def feed_step(x, d, gate_weight, up_weight, down_weight, out, dx):
    g = mm(x, gate_weight, NN)
    u = mm(x, up_weight, NN)
    sigma = 1.0 / (1.0 + jnp.exp(-g))
    active = g * sigma
    inner = (active * u).astype(BF16)
    out[...] += mm(inner, down_weight, NN)
    d_inner = mm(d, down_weight, NT)
    d_g = (d_inner * u * (sigma * (1.0 + g * (1.0 - sigma)))).astype(BF16)
    d_u = (d_inner * active).astype(BF16)
    dx[...] += mm(d_g, gate_weight, NT) + mm(d_u, up_weight, NT)
    return mm(x, d_g, TN).astype(BF16), mm(x, d_u, TN).astype(BF16), mm(inner, d, TN).astype(BF16)


def feed_kernel(gated, packed, rows_ref, grads_ref, *refs):
    if gated:
        gates_ref, refs = refs[0], refs[1:]
    count, part, width = rows_ref.shape
    weights = refs[: 1 if packed else 3]
    refs = refs[len(weights) :]
    if gated:
        back_ref, refs = refs[0], refs[1:]
        sums, (x_ref, d_ref, out_ref, dx_ref) = refs[:-4], refs[-4:]
    else:
        out_ref, dx_ref, sums = refs[0].at[0], refs[1].at[0], refs[2:]
    step = pl.program_id(1)

    @pl.when(step == 0)
    def _():
        out_ref[...] = jnp.zeros_like(out_ref)
        dx_ref[...] = jnp.zeros_like(dx_ref)
        if gated:
            square = (part, part)
            for k in range(count):
                at = slice(k * part, (k + 1) * part)
                x_ref[at, :] = rows_ref[k]
                line = jnp.broadcast_to(gates_ref[k], square)
                column = jnp.sum(jnp.where(iota(square, 0) == iota(square, 1), line, 0.0), axis=1, keepdims=True)
                d_ref[at, :] = (grads_ref[k].astype(F32) * column).astype(BF16)

    x, d = (x_ref[...], d_ref[...]) if gated else (rows_ref[0], grads_ref[0])
    if packed:
        field, total = weights[0], sums[0]
        devices = field.shape[0]
        rows = width // devices
        size = min(devices, 4)
        for start in range(0, devices, size):
            columns = range(start, start + size)
            side = lambda n: jnp.concatenate(
                [field[:, n, j * rows : (j + 1) * rows, :].reshape(width, LANES) for j in columns], axis=1)
            down = jnp.concatenate(
                [field[start : start + size, 2, c * LANES : (c + 1) * LANES, :].reshape(size * LANES, LANES)
                 for c in range(width // LANES)], axis=1)
            gate_sum, up_sum, down_sum = feed_step(x, d, side(0), side(1), down, out_ref, dx_ref)
            for n, value in enumerate((gate_sum, up_sum)):
                for j in columns:
                    total[:, n, j * rows : (j + 1) * rows, :] = value[
                        :, (j - start) * LANES : (j - start + 1) * LANES].reshape(devices, rows, LANES)
            for c in range(width // LANES):
                at = slice(c * LANES, (c + 1) * LANES)
                total[start : start + size, 2, at, :] = down_sum[:, at].reshape(size, LANES, LANES)
    else:
        sums[0][0], sums[0][1], sums[1][...] = feed_step(x, d, *(ref[...] for ref in weights), out_ref, dx_ref)

    if gated:
        @pl.when(step == pl.num_programs(1) - 1)
        def _():
            for k in range(count):
                at = slice(k * part, (k + 1) * part)
                back_ref[k, 0] = out_ref[at, :].astype(BF16)
                back_ref[k, 1] = dx_ref[at, :].astype(BF16)


def feed(rows, grads, gates, weights, first_grad, first_weight, experts, name, carried=None, after=()):
    count, _, part, width = rows.shape
    squeezed = pl.Squeezed()
    gated, packed = gates is not None, len(weights) == 1
    total = count * part
    row = lambda l, f: (0, l, 0, 0)
    grad = lambda l, f: (0, first_grad + l, 0, 0)
    operands = [rows, grads] + ([gates] if gated else [])
    in_specs = [pl.BlockSpec((count, squeezed, part, width), index) for index in (row, grad)]
    in_specs += [pl.BlockSpec((count, squeezed, 1, part), grad)] * gated
    if packed:
        devices, _, _, steps = weights[0].shape[:4]
        units = steps * devices * LANES
        pack_spec = pl.BlockSpec(
            (devices, squeezed, 3, squeezed, width, LANES), lambda l, f: (0, first_weight + l, 0, f, 0, 0))
        operands += weights
        in_specs += [pack_spec]
        sum_specs, sum_shapes = [pack_spec], [jax.ShapeDtypeStruct(weights[0].shape, BF16)]
    else:
        units, block = weights[1].shape[1], 512
        steps = units // block
        side = lambda n: pl.BlockSpec((squeezed, squeezed, width, block), lambda l, f: (l, n, 0, f))
        down_spec = pl.BlockSpec((squeezed, block, width), lambda l, f: (l, f, 0))
        operands += [weights[0], weights[0], weights[1]]
        in_specs += [side(0), side(1), down_spec]
        sum_specs = [pl.BlockSpec((squeezed, 2, width, block), lambda l, f: (l, 0, 0, f)), down_spec]
        sum_shapes = [jax.ShapeDtypeStruct(field.shape, BF16) for field in weights]
    if gated:
        out_specs = [pl.BlockSpec((count, 2, squeezed, part, width), lambda l, f: (0, 0, l, 0, 0))]
        out_shapes = [jax.ShapeDtypeStruct((count, 2, experts, part, width), BF16)]
        scratch = [pltpu.VMEM((total, width), BF16)] * 2 + [pltpu.VMEM((total, width), F32)] * 2
    else:
        out_specs = [pl.BlockSpec((count, squeezed, part, width), lambda l, f: (0, l, 0, 0))] * 2
        out_shapes = [jax.ShapeDtypeStruct((count, experts, part, width), F32)] * 2
        scratch = []
    inputs = len(operands)
    unread = ([carried] if carried is not None else []) + list(after)
    return pl.pallas_call(
        skipping(functools.partial(feed_kernel, gated, packed), inputs, len(unread)),
        grid=(experts, steps),
        in_specs=in_specs + [ANY] * len(unread),
        out_specs=out_specs + sum_specs,
        out_shape=out_shapes + sum_shapes,
        scratch_shapes=scratch,
        input_output_aliases={inputs: len(out_shapes)} if carried is not None else {},
        compiler_params=pltpu.CompilerParams(vmem_limit_bytes=VMEM_BYTES),
        cost_estimate=pl.CostEstimate(
            flops=360 * experts * total * width * units,
            bytes_accessed=experts * (12 * width * units + 8 * total * width),
            transcendentals=0,
        ),
        name=name,
    )(*operands, *unread)


def on_device(
    tokens, cotangent, segments, routes, slots,
    norm1_gain, w_query, w_key, w_value, w_out, norm2_gain, w_router,
    shared_gate, shared_up, shared_down, expert_gate, expert_up, expert_down,
):
    length, width = tokens.shape[2], tokens.shape[3]
    batch = tokens.shape[0] * tokens.shape[1]
    devices = lax.axis_size("dp")
    owners = lax.axis_size("expert")
    local_experts = expert_gate.shape[0]
    experts = owners * local_experts
    hidden_units = shared_gate.shape[1]
    groups = 2
    size = local_experts // groups
    packed = (hidden_units == expert_gate.shape[2] and hidden_units % (devices * LANES) == 0
              and width % LANES == 0 and expert_gate.shape[1] % 16 == 0)
    pool = (expert_gate, expert_up, expert_down)

    pad = LANES - experts - 2
    first_part = jnp.concatenate(
        [w_query, w_key, w_value, w_out, w_router, norm1_gain[:, None], norm2_gain[:, None],
         jnp.zeros((w_query.shape[0], pad), BF16)], axis=1)
    first_all = lax.all_gather(first_part, "dp", axis=0, tiled=True)
    if packed:
        weights = [
            [lax.all_gather(
                pack(h * size, size, pool, (shared_gate, shared_up, shared_down) if h == 0 else (), devices), "dp", axis=0)]
            for h in range(groups)]
        shared_weights = weights[0]
    else:
        gather = lambda both, down: [
            lax.all_gather(both, "dp", axis=2, tiled=True), lax.all_gather(down, "dp", axis=1, tiled=True)]
        shared_weights = gather(jnp.stack([shared_gate, shared_up])[None], shared_down[None])
        weights = []
        for h in range(groups):
            part = slice(h * size, (h + 1) * size)
            weights.append(gather(jnp.stack([expert_gate[part], expert_up[part]], axis=1), expert_down[part]))
    gains = first_all[:, 4 * width + experts : 4 * width + experts + 2].astype(F32).T
    gain_one, gain_two = gains[0:1], gains[1:2]

    route_ids = routes.reshape(batch, length, 2)
    flat = (route_ids * CAP + slots.reshape(batch, length, 2)).transpose(0, 2, 1)

    def trade(field):
        return lax.all_to_all(field.reshape(owners, field.shape[1], batch * CAP, width), "expert", 0, 0)

    whole = lambda shape: pl.BlockSpec(shape, lambda b: (0,) * len(shape))
    each = lambda *shape: pl.BlockSpec((1,) + shape, lambda b: (b, 0, 0))
    piece_spec = lambda count: pl.BlockSpec((owners, count, 1, CAP, width), lambda b: (0, 0, b, 0, 0))
    piece_shape = lambda count: jax.ShapeDtypeStruct((owners, count, batch, CAP, width), BF16)
    rows = experts * CAP
    params = pltpu.CompilerParams(vmem_limit_bytes=VMEM_BYTES)

    grad_low = cotangent.reshape(batch, length, width)
    grad_sent = pl.pallas_call(
        functools.partial(dispatch_kernel, experts),
        grid=(batch,),
        in_specs=[each(2, length), each(length, width)],
        out_specs=[piece_spec(local_experts)],
        out_shape=[piece_shape(local_experts)],
        compiler_params=params,
        cost_estimate=pl.CostEstimate(
            flops=2 * batch * rows * length * width, bytes_accessed=4 * batch * rows * width, transcendentals=0),
        name="dispatch",
    )(flat, grad_low)
    grad_arrived = trade(grad_sent[0])

    token_rows = tokens.reshape(batch, length, width)
    segment_ids = segments.reshape(batch, length)
    half = HEAD_DIM // 2
    frequency = jnp.exp(-jnp.log(10000.0) * jnp.arange(half, dtype=F32) / half)
    angles = jnp.arange(length, dtype=F32)[:, None] * frequency[None, :]
    cosine = jnp.tile(jnp.cos(angles), (1, 4))
    sine = jnp.tile(jnp.concatenate([-jnp.sin(angles), jnp.sin(angles)], axis=1), (1, 2))
    columns = first_all.shape[1]
    position_args = (segment_ids[:, :, None], segment_ids[:, None, :], flat)
    position_specs = [each(length, 1), each(1, length), each(2, length)]
    weight_args = (first_all, gain_one, gain_two, cosine, sine)
    weight_specs = [
        whole((width, columns)), whole((1, width)), whole((1, width)), whole((length, LANES)), whole((length, LANES))]
    kept_shapes = [
        jax.ShapeDtypeStruct((batch, length, width), F32),
        jax.ShapeDtypeStruct((batch, length, width), BF16),
        jax.ShapeDtypeStruct((batch, length, width), BF16),
        jax.ShapeDtypeStruct((batch, length, 3 * width), BF16),
        jax.ShapeDtypeStruct((batch, length, LANES), F32),
        jax.ShapeDtypeStruct((batch, length, LANES), F32),
    ]
    kept_specs = [each(*shape.shape[1:]) for shape in kept_shapes]
    tokens_all = batch * length
    outs = pl.pallas_call(
        functools.partial(forward_kernel, experts),
        grid=(batch,),
        in_specs=[each(length, width)] + position_specs + weight_specs,
        out_specs=kept_specs + [piece_spec(size)] * groups,
        out_shape=kept_shapes + [piece_shape(size)] * groups,
        compiler_params=params,
        cost_estimate=pl.CostEstimate(
            flops=2 * tokens_all * width * (columns + 4 * length + rows),
            bytes_accessed=2 * width * columns + tokens_all * width * 20,
            transcendentals=tokens_all * length * width // HEAD_DIM,
        ),
        name="attention",
    )(token_rows, *position_args, *weight_args)
    kept, sent = outs[:6], outs[6:]
    mixed_in, router = kept[1], kept[5]
    arrived = [trade(field) for field in sent]
    chosen = route_ids[..., None] == jnp.arange(experts, dtype=jnp.int32)
    gates = jnp.sum(jnp.where(chosen, router[:, :, None, :experts], 0.0), axis=-1).transpose(0, 2, 1)
    held = flat[:, :, None, :] == jnp.arange(rows, dtype=jnp.int32)[:, None]
    slot_gates = jnp.sum(jnp.where(held, gates[:, :, None, :], 0.0), axis=(1, 3))
    slot_gates = slot_gates.reshape(batch, owners, local_experts, CAP).transpose(1, 2, 0, 3)
    slot_gates = lax.all_to_all(slot_gates.reshape(owners, local_experts, 1, batch * CAP), "expert", 0, 0)

    backs, sums = [], []
    after = []
    for h in range(groups):
        results, *grads = feed(
            arrived[h], grad_arrived, slot_gates, weights[h], h * size, 0, size, "experts", None, after)
        back = lax.all_to_all(tie(results, *(backs[-1:] if h else arrived[1:])), "expert", 0, 0)
        backs.append(back.reshape(owners, 2, size, batch, CAP, width))
        sums.append(grads)
        if h == 0:
            shared_out, d_mixed, *shared_sums = feed(
                mixed_in.reshape(1, 1, tokens_all, width), grad_low.reshape(1, 1, tokens_all, width), None,
                shared_weights, 0, size if packed else 0, 1, "shared", grads[0] if packed else None, arrived[1:])
            after = [shared_out]
            if packed:
                sums[0] = shared_sums

    layer_out, grad_tokens, first_grad = pl.pallas_call(
        functools.partial(backward_kernel, experts, groups),
        grid=(batch,),
        in_specs=[each(length, width)] * 2 + position_specs + [each(length, 2)] + weight_specs + kept_specs
        + [each(length, width)] * 2
        + [pl.BlockSpec((owners, 2, size, 1, CAP, width), lambda b: (0, 0, 0, b, 0, 0))] * groups,
        out_specs=[each(length, width)] * 2 + [whole((width, columns))],
        out_shape=[
            jax.ShapeDtypeStruct((batch, length, width), BF16),
            jax.ShapeDtypeStruct((batch, length, width), F32),
            jax.ShapeDtypeStruct((width, columns), BF16),
        ],
        scratch_shapes=[
            pltpu.VMEM((rows, width), F32),
            pltpu.VMEM((width, columns), F32),
            pltpu.VMEM((8, width), F32),
            pltpu.VMEM((length, 3 * width), BF16),
        ],
        compiler_params=params,
        cost_estimate=pl.CostEstimate(
            flops=4 * tokens_all * width * (columns + 4 * length + rows),
            bytes_accessed=4 * width * columns + tokens_all * width * 32,
            transcendentals=tokens_all * length * width // HEAD_DIM,
        ),
        name="attention_back",
    )(
        token_rows, grad_low, *position_args, route_ids, *weight_args, *kept,
        shared_out.reshape(batch, length, width), d_mixed.reshape(batch, length, width), *backs,
    )

    def over_owners(field):
        k = 1
        while k < owners:
            came = lax.ppermute(field, "expert", [(i, i ^ k) for i in range(owners)])
            field = field.astype(F32) + came.astype(F32)
            k *= 2
            field = field.astype(BF16) if k < owners else field
        return field

    units = hidden_units
    if packed:
        mine = [
            lax.psum_scatter(tie(field[0], *(backs[h - 1 : h] if h else arrived[1:])), "dp", scatter_dimension=0)
            for h, field in enumerate(sums)]
        pool_mine = unpack(mine, [size] * groups, width // devices, units, "unpack_experts")
        shared_mine = unpack(
            [over_owners(mine[0][size:])], [1], width // devices, units, "unpack_shared")
        shared_mine = [field[0] for field in shared_mine]
    else:
        def scatter(both, down):
            return (lax.psum_scatter(both, "dp", scatter_dimension=2, tiled=True),
                    lax.psum_scatter(down, "dp", scatter_dimension=1, tiled=True))

        both, down = (jnp.concatenate(fields, axis=0).astype(F32) for fields in zip(*(scatter(*field) for field in sums)))
        pool_mine = [both[:, 0], both[:, 1], down]
        both, down = (over_owners(field[0]) for field in scatter(*shared_sums))
        shared_mine = [both[0], both[1], down]
    first_mine = scatter_rows(first_grad.reshape(devices, width // devices, columns))
    first_mine = over_owners(tie(first_mine, shared_mine[0]) if packed else first_mine)
    return (
        layer_out.reshape(tokens.shape),
        grad_tokens.reshape(tokens.shape),
        first_mine[:, 4 * width + experts],
        first_mine[:, :width],
        first_mine[:, width : 2 * width],
        first_mine[:, 2 * width : 3 * width],
        first_mine[:, 3 * width : 4 * width],
        first_mine[:, 4 * width + experts + 1],
        first_mine[:, 4 * width : 4 * width + experts],
        *shared_mine,
        *pool_mine,
    )


def solution(mesh):
    token_spec = P(None, ("dp", "expert"), None, None)
    vector, matrix, pool = P("dp"), P("dp", None), P("expert", "dp", None)
    weights = (vector, matrix, matrix, matrix, matrix, vector, matrix, matrix, matrix, matrix, pool, pool, pool)
    return jax.shard_map(
        on_device,
        mesh=mesh,
        in_specs=(token_spec, token_spec, P(None, ("dp", "expert"), None), token_spec, token_spec) + weights,
        out_specs=(token_spec, token_spec) + weights,
        check_vma=False,
    )
```

```python
import functools

import jax
import jax.numpy as jnp
from jax import lax
from jax.experimental import pallas as pl
from jax.experimental.pallas import tpu as pltpu
from jax.sharding import PartitionSpec as P

HEAD_DIM = 64
PAIR = 2 * HEAD_DIM
CAP = 40
LANES = 128
EPSILON = 1e-06
F32 = jnp.float32
BF16 = jnp.bfloat16
NN = (((1,), (0,)), ((), ()))
NT = (((1,), (1,)), ((), ()))
TN = (((0,), (0,)), ((), ()))
VMEM_BYTES = 60 * 1024 * 1024
ANY = pl.BlockSpec(memory_space=pl.ANY)


def mm(left, right, dims):
    return lax.dot_general(left, right, dims, preferred_element_type=F32)


def iota(shape, axis):
    return lax.broadcasted_iota(jnp.int32, shape, axis)


def skipping(body, inputs, unread):
    return lambda *refs: body(*refs[:inputs], *refs[inputs + unread :])


def tie(field, *after):
    return pl.pallas_call(
        lambda *refs: None,
        out_shape=jax.ShapeDtypeStruct(field.shape, field.dtype),
        in_specs=[ANY] * (1 + len(after)),
        out_specs=ANY,
        input_output_aliases={0: 0},
        name="tie",
    )(field, *after)


def first_step(i):
    return i ^ (2 if i % 2 == 0 else 4)


def second_step(i):
    return i ^ (4 if i % 2 == 0 else 2)


def core_step(i):
    return i ^ 1


def send(field, step):
    return lax.ppermute(field, "dp", [(i, step(i)) for i in range(8)])


def scatter_rows(field):
    count = lax.axis_size("dp")
    if count != 8:
        return lax.psum_scatter(field, "dp", scatter_dimension=0, tiled=False)
    index = lax.axis_index("dp")
    core, x, y = index % 2, (index // 2) % 2, index // 4
    take = functools.partial(lax.dynamic_index_in_dim, keepdims=False)
    blocks = field.reshape((4, 2) + field.shape[1:])
    came = send(take(blocks, 1 - core, 1), core_step)
    total = (take(blocks, core, 1).astype(F32) + came.astype(F32)).astype(BF16)
    one, two = jnp.where(core == 0, x, y), jnp.where(core == 0, y, x)

    def at(first, second):
        return take(total, jnp.where(core == 0, second * 2 + first, first * 2 + second), 0)

    came = send(jnp.stack([at(1 - one, two), at(1 - one, 1 - two)]), first_step).astype(F32)
    keep = (at(one, two).astype(F32) + came[0]).astype(BF16)
    pass_on = (at(one, 1 - two).astype(F32) + came[1]).astype(BF16)
    return (keep.astype(F32) + send(pass_on, second_step).astype(F32)).astype(BF16)


def place_of(flat, rows):
    at = iota((rows, flat.shape[1]), 0)
    held = jnp.logical_or(flat[0:1, :] == at, flat[1:2, :] == at)
    return jnp.where(held, 1.0, 0.0).astype(BF16)


def put_rows(sent, outs):
    owners, size = outs[0].shape[:2]
    local = len(outs) * size
    for expert in range(owners * local):
        rows = sent[expert * CAP : (expert + 1) * CAP].astype(BF16)
        outs[expert % local // size][expert // local, expert % size, 0] = rows


def dispatch_kernel(experts, flat_ref, field_ref, *outs):
    put_rows(mm(place_of(flat_ref[0], experts * CAP), field_ref[0], NN), outs)


def swap_halves(field):
    low = iota(field.shape, 1) % HEAD_DIM < HEAD_DIM // 2
    ahead = pltpu.roll(field, PAIR - HEAD_DIM // 2, 1)
    behind = pltpu.roll(field, HEAD_DIM // 2, 1)
    return jnp.where(low, ahead, behind)


def turn(field, cosine, sine):
    return field * cosine + swap_halves(field) * sine


def allowed_of(column_ref, row_ref):
    length = row_ref.shape[2]
    square = (length, length)
    return jnp.logical_and(iota(square, 0) >= iota(square, 1), column_ref[0] == row_ref[0])


def inverse_rms(field):
    return lax.rsqrt(jnp.mean(field * field, axis=-1, keepdims=True) + EPSILON)


def forward_kernel(
    experts, tokens_ref, column_ref, row_ref, flat_ref, weight_ref, gain_one_ref, gain_two_ref, cosine_ref, sine_ref,
    hidden_ref, mixed_ref, attended_ref, qkv_ref, logsum_ref, router_ref, *outs,
):
    width = tokens_ref.shape[2]
    x = tokens_ref[0].astype(F32)
    normed = (x * inverse_rms(x) * gain_one_ref[...]).astype(BF16)
    allowed = allowed_of(column_ref, row_ref)
    cosine, sine = cosine_ref[...], sine_ref[...]
    low = iota((x.shape[0], PAIR), 1) < HEAD_DIM
    lane = iota((x.shape[0], LANES), 1)
    logsum = jnp.zeros((x.shape[0], LANES), F32)
    for pair in range(width // PAIR):
        at = slice(pair * PAIR, (pair + 1) * PAIR)
        query = turn(mm(normed, weight_ref[:, at], NN), cosine, sine).astype(BF16) * BF16(0.125)
        key = turn(mm(normed, weight_ref[:, width + at.start : width + at.stop], NN), cosine, sine).astype(BF16)
        value = mm(normed, weight_ref[:, 2 * width + at.start : 2 * width + at.stop], NN).astype(BF16)
        qkv_ref[0, :, at] = query
        qkv_ref[0, :, width + at.start : width + at.stop] = key
        qkv_ref[0, :, 2 * width + at.start : 2 * width + at.stop] = value
        both = []
        for half in range(2):
            mine = low if half == 0 else jnp.logical_not(low)
            scores = jnp.where(allowed, mm(jnp.where(mine, query, BF16(0.0)), key, NT), -1e30)
            peak = jnp.max(scores, axis=-1, keepdims=True)
            expo = jnp.exp(scores - peak)
            total = jnp.sum(expo, axis=-1, keepdims=True)
            logsum = jnp.where(lane == 2 * pair + half, peak + jnp.log(total), logsum)
            both.append(mm((expo * (1.0 / total)).astype(BF16), value, NN))
        attended_ref[0, :, at] = jnp.where(low, both[0], both[1]).astype(BF16)
    logsum_ref[0] = logsum
    hidden = x + mm(attended_ref[0], weight_ref[:, 3 * width : 4 * width], NN)
    hidden_ref[0] = hidden
    mixed = (hidden * inverse_rms(hidden) * gain_two_ref[...]).astype(BF16)
    mixed_ref[0] = mixed
    logits = jnp.where(lane < experts, mm(mixed, weight_ref[:, 4 * width :], NN), -1e30)
    expo = jnp.exp(logits - jnp.max(logits, axis=-1, keepdims=True))
    router_ref[0] = expo / jnp.sum(expo, axis=-1, keepdims=True)
    put_rows(mm(place_of(flat_ref[0], experts * CAP), mixed, NN), outs)


def get_rows(backs, which, experts, held_ref):
    owners, _, size = backs[0].shape[:3]
    for expert in range(experts):
        owner, local = expert // (len(backs) * size), expert % (len(backs) * size)
        held_ref[expert * CAP : (expert + 1) * CAP, :] = backs[local // size][owner, which, local % size, 0].astype(F32)
    return held_ref[...].astype(BF16)


def backward_kernel(
    experts, groups, tokens_ref, grad_ref, column_ref, row_ref, flat_ref, routes_ref, weight_ref, gain_one_ref, gain_two_ref,
    cosine_ref, sine_ref, hidden_ref, mixed_ref, attended_ref, qkv_ref, logsum_ref, router_ref, shared_ref, d_mixed_ref, *refs,
):
    backs = refs[:groups]
    out_ref, grad_tokens_ref, grad_weight_ref, held_ref, sum_ref, gains_ref, d_qkv_ref = refs[groups:]
    width = tokens_ref.shape[2]
    step = pl.program_id(0)

    @pl.when(step == 0)
    def _():
        sum_ref[...] = jnp.zeros_like(sum_ref)
        gains_ref[...] = jnp.zeros_like(gains_ref)

    length = tokens_ref.shape[1]
    lane = iota((length, LANES), 1)
    grad = grad_ref[0].astype(F32)
    hidden = hidden_ref[0]
    mixed = mixed_ref[0]
    router = router_ref[0]
    flat = flat_ref[0]
    rows = experts * CAP
    at_row = iota((rows, length), 0)
    came = get_rows(backs, 0, experts, held_ref)
    layer = hidden + shared_ref[0]
    d_router = jnp.zeros((length, LANES), F32)
    for choice in range(2):
        place = jnp.where(flat[choice : choice + 1, :] == at_row, 1.0, 0.0).astype(BF16)
        picked = mm(place, came, TN)
        chosen = lane == routes_ref[0, :, choice : choice + 1]
        gate = jnp.sum(jnp.where(chosen, router, 0.0), axis=-1, keepdims=True)
        layer = layer + gate * picked
        d_gate = jnp.sum(grad * picked, axis=-1, keepdims=True)
        d_router = d_router + jnp.where(chosen, d_gate, 0.0)
    out_ref[0] = layer.astype(BF16)
    d_logits = (router * (d_router - jnp.sum(router * d_router, axis=-1, keepdims=True))).astype(BF16)
    sum_ref[:, 4 * width :] += mm(mixed, d_logits, TN)
    came = get_rows(backs, 1, experts, held_ref)
    d_mixed = d_mixed_ref[0] + mm(place_of(flat, rows), came, TN) + mm(d_logits, weight_ref[:, 4 * width :], NT)

    inverse_two = inverse_rms(hidden)
    unit_two = hidden * inverse_two
    gains_ref[1:2, :] += jnp.sum(d_mixed * unit_two, axis=0, keepdims=True)
    scaled = d_mixed * gain_two_ref[...]
    d_hidden = grad + inverse_two * (scaled - unit_two * jnp.mean(scaled * unit_two, axis=-1, keepdims=True))
    d_branch = d_hidden.astype(BF16)
    sum_ref[:, 3 * width : 4 * width] += mm(attended_ref[0], d_branch, TN)
    d_attended = mm(d_branch, weight_ref[:, 3 * width : 4 * width], NT).astype(BF16)

    allowed = allowed_of(column_ref, row_ref)
    cosine, sine = cosine_ref[...], -sine_ref[...]
    low = iota((length, PAIR), 1) < HEAD_DIM
    logsum = logsum_ref[0]
    for pair in range(width // PAIR):
        at = slice(pair * PAIR, (pair + 1) * PAIR)
        query = qkv_ref[0, :, at]
        key = qkv_ref[0, :, width + at.start : width + at.stop]
        value = qkv_ref[0, :, 2 * width + at.start : 2 * width + at.stop]
        d_out = d_attended[:, at]
        parts = []
        for half in range(2):
            mine = low if half == 0 else jnp.logical_not(low)
            scores = jnp.where(allowed, mm(jnp.where(mine, query, BF16(0.0)), key, NT), -1e30)
            head = 2 * pair + half
            probs = jnp.exp(scores - logsum[:, head : head + 1])
            d_probs = mm(jnp.where(mine, d_out, BF16(0.0)), value, NT)
            d_scores = (probs * (d_probs - jnp.sum(probs * d_probs, axis=-1, keepdims=True))).astype(BF16)
            parts.append((mm(d_scores, key, NN), mm(d_scores, query, TN), mm(probs.astype(BF16), d_out, TN)))
        d_query, d_key, d_value = (jnp.where(low, a, b) for a, b in zip(*parts))
        d_qkv_ref[:, at] = turn(d_query * 0.125, cosine, sine).astype(BF16)
        d_qkv_ref[:, width + at.start : width + at.stop] = turn(d_key, cosine, sine).astype(BF16)
        d_qkv_ref[:, 2 * width + at.start : 2 * width + at.stop] = d_value.astype(BF16)

    x = tokens_ref[0].astype(F32)
    inverse_one = inverse_rms(x)
    unit_one = x * inverse_one
    normed = (unit_one * gain_one_ref[...]).astype(BF16)
    d_qkv = d_qkv_ref[...]
    sum_ref[:, : 3 * width] += mm(normed, d_qkv, TN)
    d_normed = mm(d_qkv, weight_ref[:, : 3 * width], NT)
    gains_ref[0:1, :] += jnp.sum(d_normed * unit_one, axis=0, keepdims=True)
    scaled = d_normed * gain_one_ref[...]
    grad_tokens_ref[0] = d_hidden + inverse_one * (
        scaled - unit_one * jnp.mean(scaled * unit_one, axis=-1, keepdims=True))

    @pl.when(step == pl.num_programs(0) - 1)
    def _():
        grad_weight_ref[:, : 4 * width] = sum_ref[:, : 4 * width].astype(BF16)
        gains = jnp.concatenate(
            [jnp.zeros((experts, width), F32), gains_ref[...], jnp.zeros((LANES - experts - 8, width), F32)], axis=0)
        grad_weight_ref[:, 4 * width :] = (sum_ref[:, 4 * width :] + gains.T).astype(BF16)


def pack_pieces(packed, gate, up, down):
    steps, width = packed.shape[1], packed.shape[2]
    rows = gate.shape[0]
    for f in range(steps):
        for j in range(width // rows):
            at = slice((j * steps + f) * LANES, (j * steps + f + 1) * LANES)
            yield packed.at[0, f, j * rows : (j + 1) * rows], gate.at[:, at]
            yield packed.at[1, f, j * rows : (j + 1) * rows], up.at[:, at]
        for c in range(width // LANES):
            at = slice(c * LANES, (c + 1) * LANES)
            yield packed.at[2, f, at], down.at[f * LANES : (f + 1) * LANES, at]


def pack_kernel(count, *refs):
    out = refs[-1]
    step = pl.program_id(0)
    for n in range((len(refs) - 1) // 3):
        @pl.when((step < count) if n == 0 else (step >= count))
        def _():
            for to, source in pack_pieces(out, *refs[3 * n : 3 * n + 3]):
                to[...] = source[...]


def pack(first, count, pool, shared, devices):
    rows, units = pool[0].shape[1:]
    width = rows * devices
    steps = units // (devices * LANES)
    squeezed = pl.Squeezed()
    take = lambda l: (first + jnp.minimum(l, count - 1), 0, 0)
    total = count + (1 if shared else 0)
    return pl.pallas_call(
        functools.partial(pack_kernel, count),
        grid=(total,),
        in_specs=[pl.BlockSpec((squeezed,) + field.shape[1:], take) for field in pool]
        + [pl.BlockSpec(field.shape, lambda l: (0, 0)) for field in shared],
        out_specs=pl.BlockSpec((squeezed, 3, steps, width, LANES), lambda l: (l, 0, 0, 0, 0)),
        out_shape=jax.ShapeDtypeStruct((total, 3, steps, width, LANES), BF16),
        name="pack",
    )(*pool, *shared)


def unpack_kernel(sizes, *refs):
    packs, outs = refs[: len(sizes)], refs[len(sizes) :]
    step = pl.program_id(0)
    start = 0
    for n, size in enumerate(sizes):
        @pl.when(jnp.logical_and(step >= start, step < start + size))
        def _(source=packs[n]):
            for piece, to in pack_pieces(source, *outs):
                to[...] = piece[...].astype(F32)
        start += size


def unpack(packs, sizes, rows, units, name, after=()):
    squeezed = pl.Squeezed()
    specs, start = [], 0
    for field, size in zip(packs, sizes):
        specs.append(pl.BlockSpec(
            (squeezed,) + field.shape[1:],
            lambda l, start=start, size=size: (jnp.clip(l - start, 0, size - 1), 0, 0, 0, 0)))
        start += size
    width = packs[0].shape[3]
    shapes = [(rows, units), (rows, units), (rows * units // width, width)]
    return pl.pallas_call(
        skipping(functools.partial(unpack_kernel, tuple(sizes)), len(packs), len(after)),
        grid=(start,),
        in_specs=specs + [ANY] * len(after),
        out_specs=[pl.BlockSpec((squeezed,) + shape, lambda l: (l, 0, 0)) for shape in shapes],
        out_shape=[jax.ShapeDtypeStruct((start,) + shape, F32) for shape in shapes],
        name=name,
    )(*packs, *after)


def feed_step(x, d, gate_weight, up_weight, down_weight, out, dx):
    g = mm(x, gate_weight, NN)
    u = mm(x, up_weight, NN)
    sigma = 1.0 / (1.0 + jnp.exp(-g))
    active = g * sigma
    inner = (active * u).astype(BF16)
    out[...] += mm(inner, down_weight, NN)
    d_inner = mm(d, down_weight, NT)
    d_g = (d_inner * u * (sigma * (1.0 + g * (1.0 - sigma)))).astype(BF16)
    d_u = (d_inner * active).astype(BF16)
    dx[...] += mm(d_g, gate_weight, NT) + mm(d_u, up_weight, NT)
    return mm(x, d_g, TN).astype(BF16), mm(x, d_u, TN).astype(BF16), mm(inner, d, TN).astype(BF16)


def feed_kernel(gated, packed, rows_ref, grads_ref, *refs):
    if gated:
        gates_ref, refs = refs[0], refs[1:]
    count, part, width = rows_ref.shape
    weights = refs[: 1 if packed else 3]
    refs = refs[len(weights) :]
    if gated:
        back_ref, refs = refs[0], refs[1:]
        sums, (x_ref, d_ref, out_ref, dx_ref) = refs[:-4], refs[-4:]
    else:
        out_ref, dx_ref, sums = refs[0].at[0], refs[1].at[0], refs[2:]
    step = pl.program_id(1)

    @pl.when(step == 0)
    def _():
        out_ref[...] = jnp.zeros_like(out_ref)
        dx_ref[...] = jnp.zeros_like(dx_ref)
        if gated:
            square = (part, part)
            for k in range(count):
                at = slice(k * part, (k + 1) * part)
                x_ref[at, :] = rows_ref[k]
                line = jnp.broadcast_to(gates_ref[k], square)
                column = jnp.sum(jnp.where(iota(square, 0) == iota(square, 1), line, 0.0), axis=1, keepdims=True)
                d_ref[at, :] = (grads_ref[k].astype(F32) * column).astype(BF16)

    read = lambda: (x_ref[...], d_ref[...]) if gated else (rows_ref[0], grads_ref[0])
    if packed:
        field, total = weights[0], sums[0]
        devices = field.shape[0]
        rows = width // devices
        size = min(devices, 4)
        def half(n, carry):
            start = n * size
            chunks = [pl.ds(pl.multiple_of((start + j) * rows, rows), rows) for j in range(size)]
            side = lambda k: jnp.concatenate([field[:, k, at, :].reshape(width, LANES) for at in chunks], axis=1)
            down = jnp.concatenate(
                [field[pl.ds(start, size), 2, c * LANES : (c + 1) * LANES, :].reshape(size * LANES, LANES)
                 for c in range(width // LANES)], axis=1)
            gate_sum, up_sum, down_sum = feed_step(*read(), side(0), side(1), down, out_ref, dx_ref)
            for k, value in enumerate((gate_sum, up_sum)):
                for j, at in enumerate(chunks):
                    total[:, k, at, :] = value[:, j * LANES : (j + 1) * LANES].reshape(devices, rows, LANES)
            for c in range(width // LANES):
                at = slice(c * LANES, (c + 1) * LANES)
                total[pl.ds(start, size), 2, at, :] = down_sum[:, at].reshape(size, LANES, LANES)
            return carry

        lax.fori_loop(0, devices // size, half, 0)
    else:
        sums[0][0], sums[0][1], sums[1][...] = feed_step(*read(), *(ref[...] for ref in weights), out_ref, dx_ref)

    if gated:
        @pl.when(step == pl.num_programs(1) - 1)
        def _():
            for k in range(count):
                at = slice(k * part, (k + 1) * part)
                back_ref[k, 0] = out_ref[at, :].astype(BF16)
                back_ref[k, 1] = dx_ref[at, :].astype(BF16)


def feed(rows, grads, gates, weights, first_grad, first_weight, experts, name, carried=None, after=()):
    count, _, part, width = rows.shape
    squeezed = pl.Squeezed()
    gated, packed = gates is not None, len(weights) == 1
    total = count * part
    row = lambda l, f: (0, l, 0, 0)
    grad = lambda l, f: (0, first_grad + l, 0, 0)
    operands = [rows, grads] + ([gates] if gated else [])
    in_specs = [pl.BlockSpec((count, squeezed, part, width), index) for index in (row, grad)]
    in_specs += [pl.BlockSpec((count, squeezed, 1, part), grad)] * gated
    if packed:
        devices, _, _, steps = weights[0].shape[:4]
        units = steps * devices * LANES
        pack_spec = pl.BlockSpec(
            (devices, squeezed, 3, squeezed, width, LANES), lambda l, f: (0, first_weight + l, 0, f, 0, 0))
        operands += weights
        in_specs += [pack_spec]
        sum_specs, sum_shapes = [pack_spec], [jax.ShapeDtypeStruct(weights[0].shape, BF16)]
    else:
        units, block = weights[1].shape[1], 512
        steps = units // block
        side = lambda n: pl.BlockSpec((squeezed, squeezed, width, block), lambda l, f: (l, n, 0, f))
        down_spec = pl.BlockSpec((squeezed, block, width), lambda l, f: (l, f, 0))
        operands += [weights[0], weights[0], weights[1]]
        in_specs += [side(0), side(1), down_spec]
        sum_specs = [pl.BlockSpec((squeezed, 2, width, block), lambda l, f: (l, 0, 0, f)), down_spec]
        sum_shapes = [jax.ShapeDtypeStruct(field.shape, BF16) for field in weights]
    if gated:
        out_specs = [pl.BlockSpec((count, 2, squeezed, part, width), lambda l, f: (0, 0, l, 0, 0))]
        out_shapes = [jax.ShapeDtypeStruct((count, 2, experts, part, width), BF16)]
        scratch = [pltpu.VMEM((total, width), BF16)] * 2 + [pltpu.VMEM((total, width), F32)] * 2
    else:
        out_specs = [pl.BlockSpec((count, squeezed, part, width), lambda l, f: (0, l, 0, 0))] * 2
        out_shapes = [jax.ShapeDtypeStruct((count, experts, part, width), F32)] * 2
        scratch = []
    inputs = len(operands)
    unread = ([carried] if carried is not None else []) + list(after)
    return pl.pallas_call(
        skipping(functools.partial(feed_kernel, gated, packed), inputs, len(unread)),
        grid=(experts, steps),
        in_specs=in_specs + [ANY] * len(unread),
        out_specs=out_specs + sum_specs,
        out_shape=out_shapes + sum_shapes,
        scratch_shapes=scratch,
        input_output_aliases={inputs: len(out_shapes)} if carried is not None else {},
        compiler_params=pltpu.CompilerParams(vmem_limit_bytes=VMEM_BYTES),
        cost_estimate=pl.CostEstimate(
            flops=360 * experts * total * width * units,
            bytes_accessed=experts * (12 * width * units + 8 * total * width),
            transcendentals=0,
        ),
        name=name,
    )(*operands, *unread)


def on_device(
    tokens, cotangent, segments, routes, slots,
    norm1_gain, w_query, w_key, w_value, w_out, norm2_gain, w_router,
    shared_gate, shared_up, shared_down, expert_gate, expert_up, expert_down,
):
    length, width = tokens.shape[2], tokens.shape[3]
    batch = tokens.shape[0] * tokens.shape[1]
    devices = lax.axis_size("dp")
    owners = lax.axis_size("expert")
    local_experts = expert_gate.shape[0]
    experts = owners * local_experts
    hidden_units = shared_gate.shape[1]
    groups = 2
    size = local_experts // groups
    packed = (hidden_units == expert_gate.shape[2] and hidden_units % (devices * LANES) == 0
              and width % LANES == 0 and expert_gate.shape[1] % 16 == 0)
    pool = (expert_gate, expert_up, expert_down)

    pad = LANES - experts - 2
    first_part = jnp.concatenate(
        [w_query, w_key, w_value, w_out, w_router, norm1_gain[:, None], norm2_gain[:, None],
         jnp.zeros((w_query.shape[0], pad), BF16)], axis=1)
    first_all = lax.all_gather(first_part, "dp", axis=0, tiled=True)
    if packed:
        weights = [
            [lax.all_gather(
                pack(h * size, size, pool, (shared_gate, shared_up, shared_down) if h == 0 else (), devices), "dp", axis=0)]
            for h in range(groups)]
        shared_weights = weights[0]
    else:
        gather = lambda both, down: [
            lax.all_gather(both, "dp", axis=2, tiled=True), lax.all_gather(down, "dp", axis=1, tiled=True)]
        shared_weights = gather(jnp.stack([shared_gate, shared_up])[None], shared_down[None])
        weights = []
        for h in range(groups):
            part = slice(h * size, (h + 1) * size)
            weights.append(gather(jnp.stack([expert_gate[part], expert_up[part]], axis=1), expert_down[part]))
    gains = first_all[:, 4 * width + experts : 4 * width + experts + 2].astype(F32).T
    gain_one, gain_two = gains[0:1], gains[1:2]

    route_ids = routes.reshape(batch, length, 2)
    flat = (route_ids * CAP + slots.reshape(batch, length, 2)).transpose(0, 2, 1)

    def trade(field):
        return lax.all_to_all(field.reshape(owners, field.shape[1], batch * CAP, width), "expert", 0, 0)

    whole = lambda shape: pl.BlockSpec(shape, lambda b: (0,) * len(shape))
    each = lambda *shape: pl.BlockSpec((1,) + shape, lambda b: (b, 0, 0))
    piece_spec = lambda count: pl.BlockSpec((owners, count, 1, CAP, width), lambda b: (0, 0, b, 0, 0))
    piece_shape = lambda count: jax.ShapeDtypeStruct((owners, count, batch, CAP, width), BF16)
    rows = experts * CAP
    params = pltpu.CompilerParams(vmem_limit_bytes=VMEM_BYTES)

    grad_low = cotangent.reshape(batch, length, width)
    grad_sent = pl.pallas_call(
        functools.partial(dispatch_kernel, experts),
        grid=(batch,),
        in_specs=[each(2, length), each(length, width)],
        out_specs=[piece_spec(local_experts)],
        out_shape=[piece_shape(local_experts)],
        compiler_params=params,
        cost_estimate=pl.CostEstimate(
            flops=2 * batch * rows * length * width, bytes_accessed=4 * batch * rows * width, transcendentals=0),
        name="dispatch",
    )(flat, grad_low)
    grad_arrived = trade(grad_sent[0])

    token_rows = tokens.reshape(batch, length, width)
    segment_ids = segments.reshape(batch, length)
    half = HEAD_DIM // 2
    frequency = jnp.exp(-jnp.log(10000.0) * jnp.arange(half, dtype=F32) / half)
    angles = jnp.arange(length, dtype=F32)[:, None] * frequency[None, :]
    cosine = jnp.tile(jnp.cos(angles), (1, 4))
    sine = jnp.tile(jnp.concatenate([-jnp.sin(angles), jnp.sin(angles)], axis=1), (1, 2))
    columns = first_all.shape[1]
    position_args = (segment_ids[:, :, None], segment_ids[:, None, :], flat)
    position_specs = [each(length, 1), each(1, length), each(2, length)]
    weight_args = (first_all, gain_one, gain_two, cosine, sine)
    weight_specs = [
        whole((width, columns)), whole((1, width)), whole((1, width)), whole((length, LANES)), whole((length, LANES))]
    kept_shapes = [
        jax.ShapeDtypeStruct((batch, length, width), F32),
        jax.ShapeDtypeStruct((batch, length, width), BF16),
        jax.ShapeDtypeStruct((batch, length, width), BF16),
        jax.ShapeDtypeStruct((batch, length, 3 * width), BF16),
        jax.ShapeDtypeStruct((batch, length, LANES), F32),
        jax.ShapeDtypeStruct((batch, length, LANES), F32),
    ]
    kept_specs = [each(*shape.shape[1:]) for shape in kept_shapes]
    tokens_all = batch * length
    outs = pl.pallas_call(
        functools.partial(forward_kernel, experts),
        grid=(batch,),
        in_specs=[each(length, width)] + position_specs + weight_specs,
        out_specs=kept_specs + [piece_spec(size)] * groups,
        out_shape=kept_shapes + [piece_shape(size)] * groups,
        compiler_params=params,
        cost_estimate=pl.CostEstimate(
            flops=2 * tokens_all * width * (columns + 4 * length + rows),
            bytes_accessed=2 * width * columns + tokens_all * width * 20,
            transcendentals=tokens_all * length * width // HEAD_DIM,
        ),
        name="attention",
    )(token_rows, *position_args, *weight_args)
    kept, sent = outs[:6], outs[6:]
    mixed_in, router = kept[1], kept[5]
    arrived = [trade(field) for field in sent]
    chosen = route_ids[..., None] == jnp.arange(experts, dtype=jnp.int32)
    gates = jnp.sum(jnp.where(chosen, router[:, :, None, :experts], 0.0), axis=-1).transpose(0, 2, 1)
    held = flat[:, :, None, :] == jnp.arange(rows, dtype=jnp.int32)[:, None]
    slot_gates = jnp.sum(jnp.where(held, gates[:, :, None, :], 0.0), axis=(1, 3))
    slot_gates = slot_gates.reshape(batch, owners, local_experts, CAP).transpose(1, 2, 0, 3)
    slot_gates = lax.all_to_all(slot_gates.reshape(owners, local_experts, 1, batch * CAP), "expert", 0, 0)

    backs, sums = [], []
    after = []
    for h in range(groups):
        results, *grads = feed(
            arrived[h], grad_arrived, slot_gates, weights[h], h * size, 0, size, "experts", None, after)
        back = lax.all_to_all(tie(results, *(backs[-1:] if h else arrived[1:])), "expert", 0, 0)
        backs.append(back.reshape(owners, 2, size, batch, CAP, width))
        sums.append(grads)
        if h == 0:
            shared_out, d_mixed, *shared_sums = feed(
                mixed_in.reshape(1, 1, tokens_all, width), grad_low.reshape(1, 1, tokens_all, width), None,
                shared_weights, 0, size if packed else 0, 1, "shared", grads[0] if packed else None, arrived[1:])
            after = [shared_out]
            if packed:
                sums[0] = shared_sums

    layer_out, grad_tokens, first_grad = pl.pallas_call(
        functools.partial(backward_kernel, experts, groups),
        grid=(batch,),
        in_specs=[each(length, width)] * 2 + position_specs + [each(length, 2)] + weight_specs + kept_specs
        + [each(length, width)] * 2
        + [pl.BlockSpec((owners, 2, size, 1, CAP, width), lambda b: (0, 0, 0, b, 0, 0))] * groups,
        out_specs=[each(length, width)] * 2 + [whole((width, columns))],
        out_shape=[
            jax.ShapeDtypeStruct((batch, length, width), BF16),
            jax.ShapeDtypeStruct((batch, length, width), F32),
            jax.ShapeDtypeStruct((width, columns), BF16),
        ],
        scratch_shapes=[
            pltpu.VMEM((rows, width), F32),
            pltpu.VMEM((width, columns), F32),
            pltpu.VMEM((8, width), F32),
            pltpu.VMEM((length, 3 * width), BF16),
        ],
        compiler_params=params,
        cost_estimate=pl.CostEstimate(
            flops=4 * tokens_all * width * (columns + 4 * length + rows),
            bytes_accessed=4 * width * columns + tokens_all * width * 32,
            transcendentals=tokens_all * length * width // HEAD_DIM,
        ),
        name="attention_back",
    )(
        token_rows, grad_low, *position_args, route_ids, *weight_args, *kept,
        shared_out.reshape(batch, length, width), d_mixed.reshape(batch, length, width), *backs,
    )

    def over_owners(field):
        k, before = 1, field
        while k < owners:
            before = field.astype(BF16)
            came = lax.ppermute(before, "expert", [(i, i ^ k) for i in range(owners)])
            field = before.astype(F32) + came.astype(F32)
            k *= 2
        return field, before

    def over_owners_by_halves(field):
        place = lax.axis_index("expert")
        steps = [1 << n for n in range(owners.bit_length() - 1)]
        swap = lambda part, k: lax.ppermute(part, "expert", [(i, i ^ k) for i in range(owners)])
        for k in steps:
            second = place // k % 2
            half = field.shape[0] // 2
            keep = lax.dynamic_slice_in_dim(field, second * half, half)
            came = swap(lax.dynamic_slice_in_dim(field, (1 - second) * half, half), k)
            field = (keep.astype(F32) + came.astype(F32)).astype(BF16)
        for k in reversed(steps):
            came = swap(field, k)
            second = place // k % 2 == 1
            field = jnp.concatenate([jnp.where(second, came, field), jnp.where(second, field, came)])
        return field

    units = hidden_units
    if packed:
        mine = [
            lax.psum_scatter(tie(field[0], *(backs[h - 1 : h] if h else arrived[1:])), "dp", scatter_dimension=0)
            for h, field in enumerate(sums)]
        shared_mine = unpack(
            [over_owners_by_halves(mine[0][size].reshape(-1, LANES)).reshape(mine[0][size:].shape)], [1],
            width // devices, units, "unpack_shared")
        first_grad = tie(first_grad, mine[0])
        shared_mine = [field[0] for field in shared_mine]
    else:
        def scatter(both, down):
            return (lax.psum_scatter(both, "dp", scatter_dimension=2, tiled=True),
                    lax.psum_scatter(down, "dp", scatter_dimension=1, tiled=True))

        both, down = (jnp.concatenate(fields, axis=0).astype(F32) for fields in zip(*(scatter(*field) for field in sums)))
        pool_mine = [both[:, 0], both[:, 1], down]
        both, down = (over_owners(field[0])[0] for field in scatter(*shared_sums))
        shared_mine = [both[0], both[1], down]
    first_mine = scatter_rows(first_grad.reshape(devices, width // devices, columns))
    first_mine, before = over_owners(first_mine)
    if packed:
        pool_mine = unpack(mine, [size] * groups, width // devices, units, "unpack_experts", [before] + shared_mine)
    return (
        layer_out.reshape(tokens.shape),
        grad_tokens.reshape(tokens.shape),
        first_mine[:, 4 * width + experts],
        first_mine[:, :width],
        first_mine[:, width : 2 * width],
        first_mine[:, 2 * width : 3 * width],
        first_mine[:, 3 * width : 4 * width],
        first_mine[:, 4 * width + experts + 1],
        first_mine[:, 4 * width : 4 * width + experts],
        *shared_mine,
        *pool_mine,
    )


def solution(mesh):
    token_spec = P(None, ("dp", "expert"), None, None)
    vector, matrix, pool = P("dp"), P("dp", None), P("expert", "dp", None)
    weights = (vector, matrix, matrix, matrix, matrix, vector, matrix, matrix, matrix, matrix, pool, pool, pool)
    return jax.shard_map(
        on_device,
        mesh=mesh,
        in_specs=(token_spec, token_spec, P(None, ("dp", "expert"), None), token_spec, token_spec) + weights,
        out_specs=(token_spec, token_spec) + weights,
        check_vma=False,
    )
```

```python
import functools

import jax
import jax.numpy as jnp
from jax import lax
from jax.experimental import pallas as pl
from jax.experimental.pallas import tpu as pltpu
from jax.sharding import PartitionSpec as P

HEAD_DIM = 64
PAIR = 2 * HEAD_DIM
CAP = 40
LANES = 128
EPSILON = 1e-06
F32 = jnp.float32
BF16 = jnp.bfloat16
NN = (((1,), (0,)), ((), ()))
NT = (((1,), (1,)), ((), ()))
TN = (((0,), (0,)), ((), ()))
VMEM_BYTES = 60 * 1024 * 1024
ANY = pl.BlockSpec(memory_space=pl.ANY)


def mm(left, right, dims):
    return lax.dot_general(left, right, dims, preferred_element_type=F32)


def iota(shape, axis):
    return lax.broadcasted_iota(jnp.int32, shape, axis)


def skipping(body, inputs, unread):
    return lambda *refs: body(*refs[:inputs], *refs[inputs + unread :])


def tie(field, *after):
    return pl.pallas_call(
        lambda *refs: None,
        out_shape=jax.ShapeDtypeStruct(field.shape, field.dtype),
        in_specs=[ANY] * (1 + len(after)),
        out_specs=ANY,
        input_output_aliases={0: 0},
        name="tie",
    )(field, *after)


def first_step(i):
    return i ^ (2 if i % 2 == 0 else 4)


def second_step(i):
    return i ^ (4 if i % 2 == 0 else 2)


def core_step(i):
    return i ^ 1


def send(field, step):
    return lax.ppermute(field, "dp", [(i, step(i)) for i in range(8)])


def scatter_rows(field):
    count = lax.axis_size("dp")
    if count != 8:
        return lax.psum_scatter(field, "dp", scatter_dimension=0, tiled=False)
    index = lax.axis_index("dp")
    core, x, y = index % 2, (index // 2) % 2, index // 4
    take = functools.partial(lax.dynamic_index_in_dim, keepdims=False)
    blocks = field.reshape((4, 2) + field.shape[1:])
    came = send(take(blocks, 1 - core, 1), core_step)
    total = (take(blocks, core, 1).astype(F32) + came.astype(F32)).astype(BF16)
    one, two = jnp.where(core == 0, x, y), jnp.where(core == 0, y, x)

    def at(first, second):
        return take(total, jnp.where(core == 0, second * 2 + first, first * 2 + second), 0)

    came = send(jnp.stack([at(1 - one, two), at(1 - one, 1 - two)]), first_step).astype(F32)
    keep = (at(one, two).astype(F32) + came[0]).astype(BF16)
    pass_on = (at(one, 1 - two).astype(F32) + came[1]).astype(BF16)
    return (keep.astype(F32) + send(pass_on, second_step).astype(F32)).astype(BF16)


def place_of(flat, rows):
    at = iota((rows, flat.shape[1]), 0)
    held = jnp.logical_or(flat[0:1, :] == at, flat[1:2, :] == at)
    return jnp.where(held, 1.0, 0.0).astype(BF16)


def put_rows(sent, outs):
    owners, size = outs[0].shape[:2]
    local = len(outs) * size
    for expert in range(owners * local):
        rows = sent[expert * CAP : (expert + 1) * CAP].astype(BF16)
        outs[expert % local // size][expert // local, expert % size, 0] = rows


def dispatch_kernel(experts, flat_ref, field_ref, *outs):
    put_rows(mm(place_of(flat_ref[0], experts * CAP), field_ref[0], NN), outs)


def swap_halves(field):
    low = iota(field.shape, 1) % HEAD_DIM < HEAD_DIM // 2
    ahead = pltpu.roll(field, PAIR - HEAD_DIM // 2, 1)
    behind = pltpu.roll(field, HEAD_DIM // 2, 1)
    return jnp.where(low, ahead, behind)


def turn(field, cosine, sine):
    return field * cosine + swap_halves(field) * sine


def allowed_of(column_ref, row_ref):
    length = row_ref.shape[2]
    square = (length, length)
    return jnp.logical_and(iota(square, 0) >= iota(square, 1), column_ref[0] == row_ref[0])


def inverse_rms(field):
    return lax.rsqrt(jnp.mean(field * field, axis=-1, keepdims=True) + EPSILON)


def pair_columns(pair, width):
    return [pl.ds(pl.multiple_of(n * width + pair * PAIR, PAIR), PAIR) for n in range(3)]


def forward_kernel(
    experts, tokens_ref, column_ref, row_ref, flat_ref, weight_ref, gain_one_ref, gain_two_ref, cosine_ref, sine_ref,
    hidden_ref, mixed_ref, attended_ref, qkv_ref, logsum_ref, router_ref, *outs,
):
    width = tokens_ref.shape[2]
    x = tokens_ref[0].astype(F32)
    normed = (x * inverse_rms(x) * gain_one_ref[...]).astype(BF16)
    allowed = allowed_of(column_ref, row_ref)
    cosine, sine = cosine_ref[...], sine_ref[...]
    low = iota((x.shape[0], PAIR), 1) < HEAD_DIM
    lane = iota((x.shape[0], LANES), 1)
    logsum = jnp.zeros((x.shape[0], LANES), F32)
    def head_pair(pair, logsum):
        at, key_at, value_at = pair_columns(pair, width)
        query = turn(mm(normed, weight_ref[:, at], NN), cosine, sine).astype(BF16) * BF16(0.125)
        key = turn(mm(normed, weight_ref[:, key_at], NN), cosine, sine).astype(BF16)
        value = mm(normed, weight_ref[:, value_at], NN).astype(BF16)
        qkv_ref[0, :, at] = query
        qkv_ref[0, :, key_at] = key
        qkv_ref[0, :, value_at] = value
        both = []
        for half in range(2):
            mine = low if half == 0 else jnp.logical_not(low)
            scores = jnp.where(allowed, mm(jnp.where(mine, query, BF16(0.0)), key, NT), -1e30)
            peak = jnp.max(scores, axis=-1, keepdims=True)
            expo = jnp.exp(scores - peak)
            total = jnp.sum(expo, axis=-1, keepdims=True)
            logsum = jnp.where(lane == 2 * pair + half, peak + jnp.log(total), logsum)
            both.append(mm((expo * (1.0 / total)).astype(BF16), value, NN))
        attended_ref[0, :, at] = jnp.where(low, both[0], both[1]).astype(BF16)
        return logsum

    logsum = lax.fori_loop(0, width // PAIR, head_pair, logsum)
    logsum_ref[0] = logsum
    hidden = x + mm(attended_ref[0], weight_ref[:, 3 * width : 4 * width], NN)
    hidden_ref[0] = hidden
    mixed = (hidden * inverse_rms(hidden) * gain_two_ref[...]).astype(BF16)
    mixed_ref[0] = mixed
    logits = jnp.where(lane < experts, mm(mixed, weight_ref[:, 4 * width :], NN), -1e30)
    expo = jnp.exp(logits - jnp.max(logits, axis=-1, keepdims=True))
    router_ref[0] = expo / jnp.sum(expo, axis=-1, keepdims=True)
    put_rows(mm(place_of(flat_ref[0], experts * CAP), mixed, NN), outs)


def get_rows(backs, which, experts, held_ref):
    owners, _, size = backs[0].shape[:3]
    for expert in range(experts):
        owner, local = expert // (len(backs) * size), expert % (len(backs) * size)
        held_ref[expert * CAP : (expert + 1) * CAP, :] = backs[local // size][owner, which, local % size, 0].astype(F32)
    return held_ref[...].astype(BF16)


def backward_kernel(
    experts, groups, tokens_ref, grad_ref, column_ref, row_ref, flat_ref, routes_ref, weight_ref, gain_one_ref, gain_two_ref,
    cosine_ref, sine_ref, hidden_ref, mixed_ref, attended_ref, qkv_ref, logsum_ref, router_ref, shared_ref, d_mixed_ref, *refs,
):
    backs = refs[:groups]
    out_ref, grad_tokens_ref, grad_weight_ref, held_ref, sum_ref, gains_ref, d_qkv_ref, d_attended_ref = refs[groups:]
    width = tokens_ref.shape[2]
    step = pl.program_id(0)

    @pl.when(step == 0)
    def _():
        sum_ref[...] = jnp.zeros_like(sum_ref)
        gains_ref[...] = jnp.zeros_like(gains_ref)

    length = tokens_ref.shape[1]
    lane = iota((length, LANES), 1)
    grad = grad_ref[0].astype(F32)
    hidden = hidden_ref[0]
    mixed = mixed_ref[0]
    router = router_ref[0]
    flat = flat_ref[0]
    rows = experts * CAP
    at_row = iota((rows, length), 0)
    came = get_rows(backs, 0, experts, held_ref)
    layer = hidden + shared_ref[0]
    d_router = jnp.zeros((length, LANES), F32)
    for choice in range(2):
        place = jnp.where(flat[choice : choice + 1, :] == at_row, 1.0, 0.0).astype(BF16)
        picked = mm(place, came, TN)
        chosen = lane == routes_ref[0, :, choice : choice + 1]
        gate = jnp.sum(jnp.where(chosen, router, 0.0), axis=-1, keepdims=True)
        layer = layer + gate * picked
        d_gate = jnp.sum(grad * picked, axis=-1, keepdims=True)
        d_router = d_router + jnp.where(chosen, d_gate, 0.0)
    out_ref[0] = layer.astype(BF16)
    d_logits = (router * (d_router - jnp.sum(router * d_router, axis=-1, keepdims=True))).astype(BF16)
    sum_ref[:, 4 * width :] += mm(mixed, d_logits, TN)
    came = get_rows(backs, 1, experts, held_ref)
    d_mixed = d_mixed_ref[0] + mm(place_of(flat, rows), came, TN) + mm(d_logits, weight_ref[:, 4 * width :], NT)

    inverse_two = inverse_rms(hidden)
    unit_two = hidden * inverse_two
    gains_ref[1:2, :] += jnp.sum(d_mixed * unit_two, axis=0, keepdims=True)
    scaled = d_mixed * gain_two_ref[...]
    d_hidden = grad + inverse_two * (scaled - unit_two * jnp.mean(scaled * unit_two, axis=-1, keepdims=True))
    d_branch = d_hidden.astype(BF16)
    sum_ref[:, 3 * width : 4 * width] += mm(attended_ref[0], d_branch, TN)
    d_attended_ref[...] = mm(d_branch, weight_ref[:, 3 * width : 4 * width], NT).astype(BF16)

    allowed = allowed_of(column_ref, row_ref)
    cosine, sine = cosine_ref[...], -sine_ref[...]
    low = iota((length, PAIR), 1) < HEAD_DIM
    logsum = logsum_ref[0]
    def head_pair(pair, carry):
        at, key_at, value_at = pair_columns(pair, width)
        query, key, value = qkv_ref[0, :, at], qkv_ref[0, :, key_at], qkv_ref[0, :, value_at]
        d_out = d_attended_ref[:, at]
        parts = []
        for half in range(2):
            mine = low if half == 0 else jnp.logical_not(low)
            scores = jnp.where(allowed, mm(jnp.where(mine, query, BF16(0.0)), key, NT), -1e30)
            head = jnp.sum(jnp.where(lane == 2 * pair + half, logsum, 0.0), axis=-1, keepdims=True)
            probs = jnp.exp(scores - head)
            d_probs = mm(jnp.where(mine, d_out, BF16(0.0)), value, NT)
            d_scores = (probs * (d_probs - jnp.sum(probs * d_probs, axis=-1, keepdims=True))).astype(BF16)
            parts.append((mm(d_scores, key, NN), mm(d_scores, query, TN), mm(probs.astype(BF16), d_out, TN)))
        d_query, d_key, d_value = (jnp.where(low, a, b) for a, b in zip(*parts))
        d_qkv_ref[:, at] = turn(d_query * 0.125, cosine, sine).astype(BF16)
        d_qkv_ref[:, key_at] = turn(d_key, cosine, sine).astype(BF16)
        d_qkv_ref[:, value_at] = d_value.astype(BF16)
        return carry

    lax.fori_loop(0, width // PAIR, head_pair, 0)
    x = tokens_ref[0].astype(F32)
    inverse_one = inverse_rms(x)
    unit_one = x * inverse_one
    normed = (unit_one * gain_one_ref[...]).astype(BF16)
    d_qkv = d_qkv_ref[...]
    sum_ref[:, : 3 * width] += mm(normed, d_qkv, TN)
    d_normed = mm(d_qkv, weight_ref[:, : 3 * width], NT)
    gains_ref[0:1, :] += jnp.sum(d_normed * unit_one, axis=0, keepdims=True)
    scaled = d_normed * gain_one_ref[...]
    grad_tokens_ref[0] = d_hidden + inverse_one * (
        scaled - unit_one * jnp.mean(scaled * unit_one, axis=-1, keepdims=True))

    @pl.when(step == pl.num_programs(0) - 1)
    def _():
        grad_weight_ref[:, : 4 * width] = sum_ref[:, : 4 * width].astype(BF16)
        gains = jnp.concatenate(
            [jnp.zeros((experts, width), F32), gains_ref[...], jnp.zeros((LANES - experts - 8, width), F32)], axis=0)
        grad_weight_ref[:, 4 * width :] = (sum_ref[:, 4 * width :] + gains.T).astype(BF16)


def for_pieces(move, packed, gate, up, down):
    steps, width = packed.shape[1], packed.shape[2]
    rows = gate.shape[0]
    for f in range(steps):
        def block(j, carry):
            own = pl.ds(pl.multiple_of(j * rows, rows), rows)
            at = pl.ds(pl.multiple_of((j * steps + f) * LANES, LANES), LANES)
            move(packed.at[0, f, own], gate.at[:, at])
            move(packed.at[1, f, own], up.at[:, at])
            return carry

        def chunk(c, carry):
            at = pl.ds(pl.multiple_of(c * LANES, LANES), LANES)
            move(packed.at[2, f, at], down.at[f * LANES : (f + 1) * LANES, at])
            return carry

        lax.fori_loop(0, width // rows, block, 0)
        lax.fori_loop(0, width // LANES, chunk, 0)


def pack_kernel(count, *refs):
    out = refs[-1]
    step = pl.program_id(0)
    for n in range((len(refs) - 1) // 3):
        @pl.when((step < count) if n == 0 else (step >= count))
        def _():
            def move(piece, source):
                piece[...] = source[...]

            for_pieces(move, out, *refs[3 * n : 3 * n + 3])


def pack(first, count, pool, shared, devices):
    rows, units = pool[0].shape[1:]
    width = rows * devices
    steps = units // (devices * LANES)
    squeezed = pl.Squeezed()
    take = lambda l: (first + jnp.minimum(l, count - 1), 0, 0)
    total = count + (1 if shared else 0)
    return pl.pallas_call(
        functools.partial(pack_kernel, count),
        grid=(total,),
        in_specs=[pl.BlockSpec((squeezed,) + field.shape[1:], take) for field in pool]
        + [pl.BlockSpec(field.shape, lambda l: (0, 0)) for field in shared],
        out_specs=pl.BlockSpec((squeezed, 3, steps, width, LANES), lambda l: (l, 0, 0, 0, 0)),
        out_shape=jax.ShapeDtypeStruct((total, 3, steps, width, LANES), BF16),
        name="pack",
    )(*pool, *shared)


def unpack_kernel(packed, *outs):
    def move(piece, to):
        to[...] = piece[...].astype(F32)

    for_pieces(move, packed, *outs)


def unpack(packed, size, first, total, rows, units, name, after=(), carried=()):
    squeezed = pl.Squeezed()
    width = packed.shape[3]
    shapes = [(rows, units), (rows, units), (rows * units // width, width)]
    unread = list(after) + list(carried)
    return pl.pallas_call(
        skipping(unpack_kernel, 1, len(unread)),
        grid=(size,),
        in_specs=[pl.BlockSpec((squeezed,) + packed.shape[1:], lambda l: (l, 0, 0, 0, 0))] + [ANY] * len(unread),
        out_specs=[pl.BlockSpec((squeezed,) + shape, lambda l: (first + l, 0, 0)) for shape in shapes],
        out_shape=[jax.ShapeDtypeStruct((total,) + shape, F32) for shape in shapes],
        input_output_aliases={1 + len(after) + n: n for n in range(len(carried))},
        name=name,
    )(packed, *unread)


def feed_step(x, d, gate_weight, up_weight, down_weight, out, dx):
    g = mm(x, gate_weight, NN)
    u = mm(x, up_weight, NN)
    sigma = 1.0 / (1.0 + jnp.exp(-g))
    active = g * sigma
    inner = (active * u).astype(BF16)
    out[...] += mm(inner, down_weight, NN)
    d_inner = mm(d, down_weight, NT)
    d_g = (d_inner * u * (sigma * (1.0 + g * (1.0 - sigma)))).astype(BF16)
    d_u = (d_inner * active).astype(BF16)
    dx[...] += mm(d_g, gate_weight, NT) + mm(d_u, up_weight, NT)
    return mm(x, d_g, TN).astype(BF16), mm(x, d_u, TN).astype(BF16), mm(inner, d, TN).astype(BF16)


def feed_kernel(gated, packed, rows_ref, grads_ref, *refs):
    if gated:
        gates_ref, refs = refs[0], refs[1:]
    count, part, width = rows_ref.shape
    weights = refs[: 1 if packed else 3]
    refs = refs[len(weights) :]
    if gated:
        back_ref, refs = refs[0], refs[1:]
        sums, (x_ref, d_ref, out_ref, dx_ref) = refs[:-4], refs[-4:]
    else:
        out_ref, dx_ref, sums = refs[0].at[0], refs[1].at[0], refs[2:]
    step = pl.program_id(1)

    @pl.when(step == 0)
    def _():
        out_ref[...] = jnp.zeros_like(out_ref)
        dx_ref[...] = jnp.zeros_like(dx_ref)
        if gated:
            square = (part, part)
            for k in range(count):
                at = slice(k * part, (k + 1) * part)
                x_ref[at, :] = rows_ref[k]
                line = jnp.broadcast_to(gates_ref[k], square)
                column = jnp.sum(jnp.where(iota(square, 0) == iota(square, 1), line, 0.0), axis=1, keepdims=True)
                d_ref[at, :] = (grads_ref[k].astype(F32) * column).astype(BF16)

    read = lambda: (x_ref[...], d_ref[...]) if gated else (rows_ref[0], grads_ref[0])
    if packed:
        field, total = weights[0], sums[0]
        devices = field.shape[0]
        rows = width // devices
        size = min(devices, 2)
        def half(n, carry):
            start = n * size
            chunks = [pl.ds(pl.multiple_of((start + j) * rows, rows), rows) for j in range(size)]
            side = lambda k: jnp.concatenate([field[:, k, at, :].reshape(width, LANES) for at in chunks], axis=1)
            down = jnp.concatenate(
                [field[pl.ds(start, size), 2, c * LANES : (c + 1) * LANES, :].reshape(size * LANES, LANES)
                 for c in range(width // LANES)], axis=1)
            gate_sum, up_sum, down_sum = feed_step(*read(), side(0), side(1), down, out_ref, dx_ref)
            for k, value in enumerate((gate_sum, up_sum)):
                for j, at in enumerate(chunks):
                    total[:, k, at, :] = value[:, j * LANES : (j + 1) * LANES].reshape(devices, rows, LANES)
            for c in range(width // LANES):
                at = slice(c * LANES, (c + 1) * LANES)
                total[pl.ds(start, size), 2, at, :] = down_sum[:, at].reshape(size, LANES, LANES)
            return carry

        lax.fori_loop(0, devices // size, half, 0)
    else:
        sums[0][0], sums[0][1], sums[1][...] = feed_step(*read(), *(ref[...] for ref in weights), out_ref, dx_ref)

    if gated:
        @pl.when(step == pl.num_programs(1) - 1)
        def _():
            for k in range(count):
                at = slice(k * part, (k + 1) * part)
                back_ref[k, 0] = out_ref[at, :].astype(BF16)
                back_ref[k, 1] = dx_ref[at, :].astype(BF16)


def feed(rows, grads, gates, weights, first_grad, first_weight, experts, name, carried=None, after=()):
    count, _, part, width = rows.shape
    squeezed = pl.Squeezed()
    gated, packed = gates is not None, len(weights) == 1
    total = count * part
    row = lambda l, f: (0, l, 0, 0)
    grad = lambda l, f: (0, first_grad + l, 0, 0)
    operands = [rows, grads] + ([gates] if gated else [])
    in_specs = [pl.BlockSpec((count, squeezed, part, width), index) for index in (row, grad)]
    in_specs += [pl.BlockSpec((count, squeezed, 1, part), grad)] * gated
    if packed:
        devices, _, _, steps = weights[0].shape[:4]
        units = steps * devices * LANES
        pack_spec = pl.BlockSpec(
            (devices, squeezed, 3, squeezed, width, LANES), lambda l, f: (0, first_weight + l, 0, f, 0, 0))
        operands += weights
        in_specs += [pack_spec]
        sum_specs, sum_shapes = [pack_spec], [jax.ShapeDtypeStruct(weights[0].shape, BF16)]
    else:
        units, block = weights[1].shape[1], 512
        steps = units // block
        side = lambda n: pl.BlockSpec((squeezed, squeezed, width, block), lambda l, f: (l, n, 0, f))
        down_spec = pl.BlockSpec((squeezed, block, width), lambda l, f: (l, f, 0))
        operands += [weights[0], weights[0], weights[1]]
        in_specs += [side(0), side(1), down_spec]
        sum_specs = [pl.BlockSpec((squeezed, 2, width, block), lambda l, f: (l, 0, 0, f)), down_spec]
        sum_shapes = [jax.ShapeDtypeStruct(field.shape, BF16) for field in weights]
    if gated:
        out_specs = [pl.BlockSpec((count, 2, squeezed, part, width), lambda l, f: (0, 0, l, 0, 0))]
        out_shapes = [jax.ShapeDtypeStruct((count, 2, experts, part, width), BF16)]
        scratch = [pltpu.VMEM((total, width), BF16)] * 2 + [pltpu.VMEM((total, width), F32)] * 2
    else:
        out_specs = [pl.BlockSpec((count, squeezed, part, width), lambda l, f: (0, l, 0, 0))] * 2
        out_shapes = [jax.ShapeDtypeStruct((count, experts, part, width), F32)] * 2
        scratch = []
    inputs = len(operands)
    unread = ([carried] if carried is not None else []) + list(after)
    return pl.pallas_call(
        skipping(functools.partial(feed_kernel, gated, packed), inputs, len(unread)),
        grid=(experts, steps),
        in_specs=in_specs + [ANY] * len(unread),
        out_specs=out_specs + sum_specs,
        out_shape=out_shapes + sum_shapes,
        scratch_shapes=scratch,
        input_output_aliases={inputs: len(out_shapes)} if carried is not None else {},
        compiler_params=pltpu.CompilerParams(vmem_limit_bytes=VMEM_BYTES),
        cost_estimate=pl.CostEstimate(
            flops=360 * experts * total * width * units,
            bytes_accessed=experts * (12 * width * units + 8 * total * width),
            transcendentals=0,
        ),
        name=name,
    )(*operands, *unread)


def on_device(
    tokens, cotangent, segments, routes, slots,
    norm1_gain, w_query, w_key, w_value, w_out, norm2_gain, w_router,
    shared_gate, shared_up, shared_down, expert_gate, expert_up, expert_down,
):
    length, width = tokens.shape[2], tokens.shape[3]
    batch = tokens.shape[0] * tokens.shape[1]
    devices = lax.axis_size("dp")
    owners = lax.axis_size("expert")
    local_experts = expert_gate.shape[0]
    experts = owners * local_experts
    hidden_units = shared_gate.shape[1]
    groups = 2
    size = local_experts // groups
    packed = (hidden_units == expert_gate.shape[2] and hidden_units % (devices * LANES) == 0
              and width % LANES == 0 and expert_gate.shape[1] % 16 == 0)
    pool = (expert_gate, expert_up, expert_down)

    pad = LANES - experts - 2
    first_part = jnp.concatenate(
        [w_query, w_key, w_value, w_out, w_router, norm1_gain[:, None], norm2_gain[:, None],
         jnp.zeros((w_query.shape[0], pad), BF16)], axis=1)
    first_all = lax.all_gather(first_part, "dp", axis=0, tiled=True)
    if packed:
        weights = [
            [lax.all_gather(
                pack(h * size, size, pool, (shared_gate, shared_up, shared_down) if h == 0 else (), devices), "dp", axis=0)]
            for h in range(groups)]
        shared_weights = weights[0]
    else:
        gather = lambda both, down: [
            lax.all_gather(both, "dp", axis=2, tiled=True), lax.all_gather(down, "dp", axis=1, tiled=True)]
        shared_weights = gather(jnp.stack([shared_gate, shared_up])[None], shared_down[None])
        weights = []
        for h in range(groups):
            part = slice(h * size, (h + 1) * size)
            weights.append(gather(jnp.stack([expert_gate[part], expert_up[part]], axis=1), expert_down[part]))
    gains = first_all[:, 4 * width + experts : 4 * width + experts + 2].astype(F32).T
    gain_one, gain_two = gains[0:1], gains[1:2]

    route_ids = routes.reshape(batch, length, 2)
    flat = (route_ids * CAP + slots.reshape(batch, length, 2)).transpose(0, 2, 1)

    def trade(field):
        return lax.all_to_all(field.reshape(owners, field.shape[1], batch * CAP, width), "expert", 0, 0)

    whole = lambda shape: pl.BlockSpec(shape, lambda b: (0,) * len(shape))
    each = lambda *shape: pl.BlockSpec((1,) + shape, lambda b: (b, 0, 0))
    piece_spec = lambda count: pl.BlockSpec((owners, count, 1, CAP, width), lambda b: (0, 0, b, 0, 0))
    piece_shape = lambda count: jax.ShapeDtypeStruct((owners, count, batch, CAP, width), BF16)
    rows = experts * CAP
    params = pltpu.CompilerParams(vmem_limit_bytes=VMEM_BYTES)

    grad_low = cotangent.reshape(batch, length, width)
    grad_sent = pl.pallas_call(
        functools.partial(dispatch_kernel, experts),
        grid=(batch,),
        in_specs=[each(2, length), each(length, width)],
        out_specs=[piece_spec(local_experts)],
        out_shape=[piece_shape(local_experts)],
        compiler_params=params,
        cost_estimate=pl.CostEstimate(
            flops=2 * batch * rows * length * width, bytes_accessed=4 * batch * rows * width, transcendentals=0),
        name="dispatch",
    )(flat, grad_low)
    grad_arrived = trade(grad_sent[0])

    token_rows = tokens.reshape(batch, length, width)
    segment_ids = segments.reshape(batch, length)
    half = HEAD_DIM // 2
    frequency = jnp.exp(-jnp.log(10000.0) * jnp.arange(half, dtype=F32) / half)
    angles = jnp.arange(length, dtype=F32)[:, None] * frequency[None, :]
    cosine = jnp.tile(jnp.cos(angles), (1, 4))
    sine = jnp.tile(jnp.concatenate([-jnp.sin(angles), jnp.sin(angles)], axis=1), (1, 2))
    columns = first_all.shape[1]
    position_args = (segment_ids[:, :, None], segment_ids[:, None, :], flat)
    position_specs = [each(length, 1), each(1, length), each(2, length)]
    weight_args = (first_all, gain_one, gain_two, cosine, sine)
    weight_specs = [
        whole((width, columns)), whole((1, width)), whole((1, width)), whole((length, LANES)), whole((length, LANES))]
    kept_shapes = [
        jax.ShapeDtypeStruct((batch, length, width), F32),
        jax.ShapeDtypeStruct((batch, length, width), BF16),
        jax.ShapeDtypeStruct((batch, length, width), BF16),
        jax.ShapeDtypeStruct((batch, length, 3 * width), BF16),
        jax.ShapeDtypeStruct((batch, length, LANES), F32),
        jax.ShapeDtypeStruct((batch, length, LANES), F32),
    ]
    kept_specs = [each(*shape.shape[1:]) for shape in kept_shapes]
    tokens_all = batch * length
    outs = pl.pallas_call(
        functools.partial(forward_kernel, experts),
        grid=(batch,),
        in_specs=[each(length, width)] + position_specs + weight_specs,
        out_specs=kept_specs + [piece_spec(size)] * groups,
        out_shape=kept_shapes + [piece_shape(size)] * groups,
        compiler_params=params,
        cost_estimate=pl.CostEstimate(
            flops=2 * tokens_all * width * (columns + 4 * length + rows),
            bytes_accessed=2 * width * columns + tokens_all * width * 20,
            transcendentals=tokens_all * length * width // HEAD_DIM,
        ),
        name="attention",
    )(token_rows, *position_args, *weight_args)
    kept, sent = outs[:6], outs[6:]
    mixed_in, router = kept[1], kept[5]
    arrived = [trade(field) for field in sent]
    chosen = route_ids[..., None] == jnp.arange(experts, dtype=jnp.int32)
    gates = jnp.sum(jnp.where(chosen, router[:, :, None, :experts], 0.0), axis=-1).transpose(0, 2, 1)
    held = flat[:, :, None, :] == jnp.arange(rows, dtype=jnp.int32)[:, None]
    slot_gates = jnp.sum(jnp.where(held, gates[:, :, None, :], 0.0), axis=(1, 3))
    slot_gates = slot_gates.reshape(batch, owners, local_experts, CAP).transpose(1, 2, 0, 3)
    slot_gates = lax.all_to_all(slot_gates.reshape(owners, local_experts, 1, batch * CAP), "expert", 0, 0)

    backs, sums = [], []
    after = []
    for h in range(groups):
        results, *grads = feed(
            arrived[h], grad_arrived, slot_gates, weights[h], h * size, 0, size, "experts", None, after)
        back = lax.all_to_all(tie(results, *(backs[-1:] if h else arrived[1:])), "expert", 0, 0)
        backs.append(back.reshape(owners, 2, size, batch, CAP, width))
        sums.append(grads)
        if h == 0:
            shared_out, d_mixed, *shared_sums = feed(
                mixed_in.reshape(1, 1, tokens_all, width), grad_low.reshape(1, 1, tokens_all, width), None,
                shared_weights, 0, size if packed else 0, 1, "shared", grads[0] if packed else None, arrived[1:])
            after = [shared_out]
            if packed:
                sums[0] = shared_sums

    layer_out, grad_tokens, first_grad = pl.pallas_call(
        functools.partial(backward_kernel, experts, groups),
        grid=(batch,),
        in_specs=[each(length, width)] * 2 + position_specs + [each(length, 2)] + weight_specs + kept_specs
        + [each(length, width)] * 2
        + [pl.BlockSpec((owners, 2, size, 1, CAP, width), lambda b: (0, 0, 0, b, 0, 0))] * groups,
        out_specs=[each(length, width)] * 2 + [whole((width, columns))],
        out_shape=[
            jax.ShapeDtypeStruct((batch, length, width), BF16),
            jax.ShapeDtypeStruct((batch, length, width), F32),
            jax.ShapeDtypeStruct((width, columns), BF16),
        ],
        scratch_shapes=[
            pltpu.VMEM((rows, width), F32),
            pltpu.VMEM((width, columns), F32),
            pltpu.VMEM((8, width), F32),
            pltpu.VMEM((length, 3 * width), BF16),
            pltpu.VMEM((length, width), BF16),
        ],
        compiler_params=params,
        cost_estimate=pl.CostEstimate(
            flops=4 * tokens_all * width * (columns + 4 * length + rows),
            bytes_accessed=4 * width * columns + tokens_all * width * 32,
            transcendentals=tokens_all * length * width // HEAD_DIM,
        ),
        name="attention_back",
    )(
        token_rows, grad_low, *position_args, route_ids, *weight_args, *kept,
        shared_out.reshape(batch, length, width), d_mixed.reshape(batch, length, width), *backs,
    )

    def over_owners(field):
        k, before = 1, field
        while k < owners:
            before = field.astype(BF16)
            came = lax.ppermute(before, "expert", [(i, i ^ k) for i in range(owners)])
            field = before.astype(F32) + came.astype(F32)
            k *= 2
        return field, before

    def over_owners_by_halves(field):
        place = lax.axis_index("expert")
        steps = [1 << n for n in range(owners.bit_length() - 1)]
        swap = lambda part, k: lax.ppermute(part, "expert", [(i, i ^ k) for i in range(owners)])
        for k in steps:
            second = place // k % 2
            half = field.shape[0] // 2
            keep = lax.dynamic_slice_in_dim(field, second * half, half)
            came = swap(lax.dynamic_slice_in_dim(field, (1 - second) * half, half), k)
            field = (keep.astype(F32) + came.astype(F32)).astype(BF16)
        for k in reversed(steps):
            came = swap(field, k)
            second = place // k % 2 == 1
            field = jnp.concatenate([jnp.where(second, came, field), jnp.where(second, field, came)])
        return field

    units = hidden_units
    if packed:
        mine = [
            lax.psum_scatter(tie(field[0], *(backs[h - 1 : h] if h else arrived[1:])), "dp", scatter_dimension=0)
            for h, field in enumerate(sums)]
        shared_mine = unpack(
            over_owners_by_halves(mine[0][size].reshape(-1, LANES)).reshape(mine[0][size:].shape), 1, 0, 1,
            width // devices, units, "unpack_shared")
        first_grad = tie(first_grad, mine[0])
        shared_mine = [field[0] for field in shared_mine]
    else:
        def scatter(both, down):
            return (lax.psum_scatter(both, "dp", scatter_dimension=2, tiled=True),
                    lax.psum_scatter(down, "dp", scatter_dimension=1, tiled=True))

        both, down = (jnp.concatenate(fields, axis=0).astype(F32) for fields in zip(*(scatter(*field) for field in sums)))
        pool_mine = [both[:, 0], both[:, 1], down]
        both, down = (over_owners(field[0])[0] for field in scatter(*shared_sums))
        shared_mine = [both[0], both[1], down]
    first_mine = scatter_rows(first_grad.reshape(devices, width // devices, columns))
    first_mine, before = over_owners(first_mine)
    if packed:
        pool_mine = ()
        for h, field in enumerate(mine):
            pool_mine = unpack(
                field, size, h * size, local_experts, width // devices, units, "unpack_experts", [before] + shared_mine, pool_mine)
    return (
        layer_out.reshape(tokens.shape),
        grad_tokens.reshape(tokens.shape),
        first_mine[:, 4 * width + experts],
        first_mine[:, :width],
        first_mine[:, width : 2 * width],
        first_mine[:, 2 * width : 3 * width],
        first_mine[:, 3 * width : 4 * width],
        first_mine[:, 4 * width + experts + 1],
        first_mine[:, 4 * width : 4 * width + experts],
        *shared_mine,
        *pool_mine,
    )


def solution(mesh):
    token_spec = P(None, ("dp", "expert"), None, None)
    vector, matrix, pool = P("dp"), P("dp", None), P("expert", "dp", None)
    weights = (vector, matrix, matrix, matrix, matrix, vector, matrix, matrix, matrix, matrix, pool, pool, pool)
    return jax.shard_map(
        on_device,
        mesh=mesh,
        in_specs=(token_spec, token_spec, P(None, ("dp", "expert"), None), token_spec, token_spec) + weights,
        out_specs=(token_spec, token_spec) + weights,
        check_vma=False,
    )
```
